256 devices in a mesh: gx: 4 (over y), gy: 16 (over x, z_hi, core), gz: 4 (over z_lo).
Axes of the slice: x: 4, y: 4, z: 8 (z_hi: 2, z_lo: 4; z = z_hi * 4 + z_lo), core: 2. Of those that a mesh axis runs over, the one named last changes fastest.
Arguments:
- features: bfloat16 [8, 16, 16, 128, 128], P('gx', 'gy', 'gz'), may hold values from -6 to 6
- msg_weight: bfloat16 [128, 128], replicated, may hold values from -0.5 to 0.5
- self_weight: bfloat16 [128, 128], replicated, may hold values from -0.5 to 0.5
- charge_weight: bfloat16 [128], replicated, may hold values from -0.5 to 0.5
- spline_corner: int32 [8, 16, 16, 3, 128], P('gx', 'gy', 'gz'), may hold values from 0 to 12
- spline_fraction: float32 [8, 16, 16, 3, 128], P('gx', 'gy', 'gz'), may hold values from 0 to 1
Outputs:
- feature_grad: float32 [8, 16, 16, 128, 128], P('gx', 'gy', 'gz')
- atom_potential: float32 [8, 16, 16, 128], P('gx', 'gy', 'gz')
- energy_per_atom: float32 [], replicated
The draws below stay inside these ranges and needn't reach their ends.
All inputs are finite; a program needn't handle non-finite values.
Results may differ from the reference program's by a relative error of at most 0.0095.
Values may be sent and summed in bfloat16 or wider, within the bound.
No kernel may reach another device: no remote copies, remote signals or barrier semaphores. Data moves between devices by JAX's collectives and lax.ppermute only.
A program may use at most 64 MiB of HBM per device.

```python
import math
import jax
import jax.numpy as jnp
from jax import lax

D = 128
M = 128
PC = 16
NCX = 8
NCY = 16
NCZ = 16
NX = 128
NY = 256
NZ = 256


def set_ends(values, own_key, least, top_value):
    longest = values.shape.index(max(values.shape))
    spots = []
    for shift in (0, 1):
        where = [jax.random.randint(jax.random.fold_in(own_key, axis), (), 0, length) for axis, length in enumerate(values.shape)]
        where[longest] = (where[longest] + shift) % values.shape[longest]
        spots.append(tuple(where))
    return values.at[spots[0]].set(least).at[spots[1]].set(top_value)


def level_of(key, extent, split, low, high):
    def one(axis_at, shards_of):
        draws = jax.random.uniform(jax.random.fold_in(jax.random.fold_in(key, 6), axis_at), (shards_of,), jnp.float32, low / len(split), high / len(split))
        return jnp.repeat(jnp.exp(draws), extent[axis_at] // shards_of).reshape((-1,) + (1,) * (len(extent) - axis_at - 1))

    gain = one(*split[0])
    for cut in split[1:]:
        gain = gain * one(*cut)
    return gain


def gaussian(stream_key, shape, deviation, most, split=(), kind=jnp.bfloat16):
    values = jax.random.normal(stream_key, shape, jnp.float32) * deviation
    if len(split) > 0:
        values = level_of(stream_key, shape, split, -0.22, 0.18) * values
    return jnp.clip(values, min=-most, max=most).astype(kind)


def setup_inputs(seed: int = 0) -> dict:
    key_list = jax.random.split(jax.random.key(seed), 7)
    return {
        "features": gaussian(key_list[0], (NCX, NCY, NCZ, M, D), 1.0, 6.0, ((0, 4), (1, 16), (2, 4))),
        "msg_weight": gaussian(key_list[1], (D, D), D ** -0.5, 0.5),
        "self_weight": gaussian(key_list[2], (D, D), D ** -0.5, 0.5),
        "charge_weight": gaussian(key_list[3], (D,), D ** -0.5, 0.5),
        "spline_corner": set_ends(jax.random.randint(key_list[4], (NCX, NCY, NCZ, 3, M), 0, PC - 3), jax.random.fold_in(key_list[4], 1), 0, (PC - 3) - 1).astype(jnp.int32),
        "spline_fraction": jnp.clip(1.0 * jax.random.uniform(key_list[5], (NCX, NCY, NCZ, 3, M), jnp.float32) ** level_of(key_list[5], (NCX, NCY, NCZ, 3, M), ((0, 4), (1, 16), (2, 4)), -0.2, 0.2), 0.0, 1.0),
    }


pair_scale = 0.1
coupling = 0.125
spread_width = 0.0625
highest = lax.Precision.HIGHEST


def spline_rows(corner, fraction, mesh_points):
    offset = jnp.arange(mesh_points, dtype=jnp.int32) - corner[..., None]
    within = fraction[..., None]
    first_weight = (1.0 - within) ** 3 / 6.0
    second_weight = (3.0 * within ** 3 - 6.0 * within ** 2 + 4.0) / 6.0
    third_weight = (-3.0 * within ** 3 + 3.0 * within ** 2 + 3.0 * within + 1.0) / 6.0
    fourth_weight = within ** 3 / 6.0
    nothing = jnp.zeros_like(first_weight)
    return jnp.where(offset == 0, first_weight, jnp.where(offset == 1, second_weight, jnp.where(offset == 2, third_weight, jnp.where(offset == 3, fourth_weight, nothing))))


def pair_weights(centre, neighbour, offset):
    centre = centre.astype(jnp.float32)
    neighbour = neighbour.astype(jnp.float32)
    squared = None
    for which in range(3):
        gap = offset[which] + (neighbour[..., which, None, :] - centre[..., which, :, None])
        squared = gap * gap if squared is None else squared + gap * gap
    inside = jnp.maximum(1.0 - squared, 0.0)
    return (pair_scale * inside * inside).astype(jnp.bfloat16)


def all_offsets():
    return [(first, second, third) for first in (-1, 0, 1) for second in (-1, 0, 1) for third in (-1, 0, 1)]


def pair_sums(position, values):
    total = jnp.zeros(values.shape, jnp.float32)
    for offset in all_offsets():
        moved = (-offset[0], -offset[1], -offset[2])
        near_position = jnp.roll(position, moved, axis=(0, 1, 2))
        near_values = jnp.roll(values, moved, axis=(0, 1, 2))
        weights = pair_weights(position, near_position, offset)
        total = total + jnp.einsum('abcsn,abcnd->abcsd', weights.astype(jnp.float32), near_values.astype(jnp.float32))
    return total


def spread_cells(charge, rows):
    points = rows[0].shape[-1]
    left = charge[..., None] * rows[0]
    right = (rows[1][..., :, None] * rows[2][..., None, :]).reshape(rows[1].shape[:-1] + (points * points,))
    block = jnp.einsum('abcsi,abcsj->abcij', left, right, precision=highest)
    return block.reshape(block.shape[:-1] + (points, points))


def interpolate(cell_field, rows):
    points = rows[0].shape[-1]
    right = (rows[1][..., :, None] * rows[2][..., None, :]).reshape(rows[1].shape[:-1] + (points * points,))
    flat_field = cell_field.reshape(cell_field.shape[:3] + (points, points * points))
    partial_value = jnp.einsum('abcij,abcsj->abcsi', flat_field, right, precision=highest)
    return jnp.sum(partial_value * rows[0], axis=-1)


def cells_to_mesh(block):
    count_a, count_b, count_c, points = block.shape[0], block.shape[1], block.shape[2], block.shape[3]
    return block.transpose(0, 3, 1, 4, 2, 5).reshape(count_a * points, count_b * points, count_c * points)


def mesh_to_cells(field, count_a, count_b, count_c):
    points = field.shape[0] // count_a
    return field.reshape(count_a, points, count_b, points, count_c, points).transpose(0, 2, 4, 1, 3, 5)


def influence_of(index_x, index_y, index_z, size_x, size_y, size_z, points):
    def wave(index, size):
        signed = jnp.where(2 * index >= size, index - size, index)
        return signed.astype(jnp.float32) * (points / size)
    wave_x = wave(index_x, size_x)
    wave_y = wave(index_y, size_y)
    wave_z = wave(index_z, size_z)
    squared = wave_x * wave_x + wave_y * wave_y + wave_z * wave_z
    safe = jnp.where(squared > 0, squared, 1.0)
    return jnp.where(squared > 0, jnp.exp(-(math.pi * spread_width) ** 2 * squared) / safe, 0.0)


def reference(features, msg_weight, self_weight, charge_weight, spline_corner, spline_fraction):
    width = features.shape[-1]
    position = ((spline_corner.astype(jnp.float32) + 1.0 + spline_fraction) / PC).astype(jnp.bfloat16)
    flat = features.reshape(-1, width)
    projected = jnp.dot(flat, msg_weight, preferred_element_type=jnp.float32).astype(jnp.bfloat16).reshape(features.shape)
    message = pair_sums(position, projected)
    preact = jnp.dot(flat, self_weight, preferred_element_type=jnp.float32).reshape(features.shape) + message
    charge = jnp.sum(jax.nn.silu(preact) * charge_weight.astype(jnp.float32), axis=-1)
    rows = [spline_rows(spline_corner[..., which, :], spline_fraction[..., which, :], PC) for which in range(3)]
    mesh = cells_to_mesh(spread_cells(charge, rows))
    spectrum = jnp.fft.fftn(mesh)
    grid_x = jnp.arange(NX, dtype=jnp.int32)[:, None, None]
    grid_y = jnp.arange(NY, dtype=jnp.int32)[None, :, None]
    grid_z = jnp.arange(NZ, dtype=jnp.int32)[None, None, :]
    influence = influence_of(grid_x, grid_y, grid_z, NX, NY, NZ, PC)
    volume = (NX // PC) * (NY // PC) * (NZ // PC)
    natoms = NCX * NCY * NCZ * M
    power = jnp.real(spectrum) ** 2 + jnp.imag(spectrum) ** 2
    energy = (coupling / (2.0 * volume * natoms)) * jnp.sum(influence * power)
    mesh_potential = ((coupling / volume) * (NX * NY * NZ) * jnp.real(jnp.fft.ifftn(influence * spectrum))).astype(jnp.float32)
    atom_potential = interpolate(mesh_to_cells(mesh_potential, NCX, NCY, NCZ), rows)
    sigma = jax.nn.sigmoid(preact)
    slope = sigma * (1.0 + preact * (1.0 - sigma))
    cotangent = (atom_potential[..., None] * charge_weight.astype(jnp.float32) * slope).astype(jnp.bfloat16)
    back_message = pair_sums(position, cotangent).astype(jnp.bfloat16)
    grad = jnp.dot(back_message.reshape(-1, width), msg_weight.T, preferred_element_type=jnp.float32)
    grad = grad + jnp.dot(cotangent.reshape(-1, width), self_weight.T, preferred_element_type=jnp.float32)
    return grad.reshape(features.shape), atom_potential, energy.astype(jnp.float32)
```

```python
import functools
import math

import jax
import jax.numpy as jnp
import numpy as np
from jax import lax
from jax.experimental import pallas as pl
from jax.experimental.pallas import tpu as pltpu
from jax.sharding import PartitionSpec as P

PC = 16
pair_scale = 0.1
coupling = 0.125
spread_width = 0.0625
highest = lax.Precision.HIGHEST
f32 = jnp.float32
bf16 = jnp.bfloat16
plane = ("gx", "gz")
everyone = ("gx", "gy", "gz")


def dot(a, b):
    return jnp.dot(a, b, preferred_element_type=f32)


def dot_t(a, b, precision=None):
    return lax.dot_general(
        a, b, (((1,), (1,)), ((), ())), preferred_element_type=f32, precision=precision
    )


def whole(shape):
    zeros = (0,) * len(shape)
    return pl.BlockSpec(shape, lambda *_: zeros)


def cas(rows, columns, size):
    turns = np.outer(rows, columns) % size
    angle = 2.0 * np.pi / size * turns
    return np.cos(angle) + np.sin(angle)


def moved(value, axis, step):
    count = lax.axis_size(axis)
    return lax.ppermute(value, axis, [(i, (i + step) % count) for i in range(count)])


def with_neighbours(value, axis, dim):
    length = value.shape[dim]
    last = lax.slice_in_dim(value, length - 1, length, axis=dim)
    first = lax.slice_in_dim(value, 0, 1, axis=dim)
    return jnp.concatenate([moved(last, axis, 1), value, moved(first, axis, -1)], axis=dim)


def surrounded(value):
    value = with_neighbours(value, "gy", 0)
    value = with_neighbours(value, "gz", 2)
    return with_neighbours(value, "gx", 1)


def weights_kernel(cells_z, reach_x, reach_z, place_ref, out_ref):
    step = pl.program_id(0)
    a = step // cells_z
    c = step % cells_z

    def position(index):
        return (place_ref[index] * (1.0 / PC)).astype(bf16).astype(f32)

    centre = position((reach_x + a + 1) * reach_z + c + 1)
    columns = jnp.transpose(centre)
    centre_x = jnp.broadcast_to(columns[:, 0:1], (128, 128))
    centre_y = jnp.broadcast_to(columns[:, 1:2], (128, 128))
    centre_z = jnp.broadcast_to(columns[:, 2:3], (128, 128))
    for dy in range(3):
        for dx in range(3):
            for dz in range(3):
                near = position((dy * reach_x + a + dx) * reach_z + c + dz)
                gap_x = (near[0:1] + (dx - 1.0)) - centre_x
                gap_y = (near[1:2] + (dy - 1.0)) - centre_y
                gap_z = (near[2:3] + (dz - 1.0)) - centre_z
                squared = gap_x * gap_x + gap_y * gap_y + gap_z * gap_z
                inside = jnp.maximum(1.0 - squared, 0.0)
                out_ref[0, dy * 3 + dx, :, dz * 128 : (dz + 1) * 128] = (
                    pair_scale * inside * inside
                ).astype(bf16)


def pair_weights(place, cells, reach):
    cells_x, cells_z = cells
    count = cells_x * cells_z
    return pl.pallas_call(
        functools.partial(weights_kernel, cells_z, reach[1], reach[2]),
        grid=(count,),
        in_specs=[whole(place.shape)],
        out_specs=pl.BlockSpec((1, 9, 128, 384), lambda i: (i, 0, 0, 0)),
        out_shape=jax.ShapeDtypeStruct((count, 9, 128, 384), bf16),
        cost_estimate=pl.CostEstimate(
            flops=count * 27 * 16384 * 14, bytes_accessed=count * 27 * 32768, transcendentals=0
        ),
        name="pair_weights",
    )(place)


def spline_row(place):
    point = lax.broadcasted_iota(jnp.int32, (PC, 128), 0).astype(f32)
    away = jnp.abs(point - place)
    near = (4.0 - 6.0 * away * away + 3.0 * away * away * away) * (1.0 / 6.0)
    rest = 2.0 - away
    far = rest * rest * rest * (1.0 / 6.0)
    return jnp.where(away < 1.0, near, jnp.where(away < 2.0, far, 0.0))


def message_kernel(
    cells_z,
    reach_x,
    reach_z,
    weight_ref,
    near_ref,
    own_ref,
    self_ref,
    read_ref,
    place_ref,
    slope_ref,
    mesh_ref,
    sum_ref,
):
    step = pl.program_id(0)
    a = step // cells_z
    c = step % cells_z
    preact = dot(own_ref[0], self_ref[...])
    for dy in range(3):
        for dx in range(3):
            near = near_ref[pl.ds((dy * reach_x + a + dx) * reach_z + c, 3)]
            preact = preact + dot(weight_ref[0, dy * 3 + dx], near.reshape(384, 128))
    sigma = 1.0 / (1.0 + jnp.exp(-preact))
    read = read_ref[...]
    slope_ref[0] = (read[0:1] * (sigma * (1.0 + preact * (1.0 - sigma)))).astype(bf16)
    charge = dot_t(read, preact * sigma, highest)[0:1]
    place = place_ref[0]
    row_x = spline_row(place[0:1])
    row_y = spline_row(place[1:2]) * charge
    row_z = spline_row(place[2:3])
    left = (row_y[:, None, :] * row_x[None, :, :]).reshape(PC * PC, 128).astype(bf16)
    block = lax.broadcasted_iota(jnp.int32, (128, 128), 0) // PC
    right = jnp.where(block == step, jnp.tile(row_z, (8, 1)), 0.0).astype(bf16)

    @pl.when(step == 0)
    def _():
        sum_ref[...] = jnp.zeros_like(sum_ref)

    sum_ref[...] += dot_t(left, right)

    @pl.when(step == pl.num_programs(0) - 1)
    def _():
        mesh_ref[...] = sum_ref[...].reshape(PC, PC, 128).astype(bf16)


def message_layer(weights, near, own, self_weight, read, place, cells, reach):
    count = cells[0] * cells[1]
    return pl.pallas_call(
        functools.partial(message_kernel, cells[1], reach[1], reach[2]),
        grid=(count,),
        in_specs=[
            pl.BlockSpec((1, 9, 128, 384), lambda i: (i, 0, 0, 0)),
            whole(near.shape),
            pl.BlockSpec((1, 128, 128), lambda i: (i, 0, 0)),
            whole((128, 128)),
            whole((8, 128)),
            pl.BlockSpec((1, 8, 128), lambda i: (i, 0, 0)),
        ],
        out_specs=[
            pl.BlockSpec((1, 128, 128), lambda i: (i, 0, 0)),
            whole((PC, PC, 128)),
        ],
        out_shape=[
            jax.ShapeDtypeStruct((count, 128, 128), bf16),
            jax.ShapeDtypeStruct((PC, PC, 128), bf16),
        ],
        scratch_shapes=[pltpu.VMEM((PC * PC, 128), f32)],
        cost_estimate=pl.CostEstimate(
            flops=count * 28 * 2 * 128**3,
            bytes_accessed=count * 27 * 32768 + 3000000,
            transcendentals=count * 16384,
        ),
        name="message",
    )(weights, near, own, self_weight, read, place)


def forward_kernel(mesh_ref, along_z_ref, along_x_ref, out_ref):
    total = jnp.zeros((64, 512), f32)
    for g in range(4):
        total = total + dot(mesh_ref[:, g].reshape(64, 128), along_z_ref[g])
    lines = jnp.concatenate([total[:, :256], total[:, 256:]], axis=0).astype(bf16)
    waves = dot(along_x_ref[...], lines)
    out_ref[0:128, :] = waves[:, :128]
    out_ref[128:256, :] = waves[:, 128:]


def forward_xz(mesh, along_z, along_x):
    return pl.pallas_call(
        forward_kernel,
        out_shape=jax.ShapeDtypeStruct((256, 128), f32),
        cost_estimate=pl.CostEstimate(
            flops=2 * 64 * 512 * 512, bytes_accessed=800000, transcendentals=0
        ),
        name="forward_xz",
    )(mesh, along_z, along_x)


def filter_kernel(lines_ref, into_ref, back_ref, influence_ref, out_ref):
    waves = dot(into_ref[...], lines_ref[...].astype(bf16))
    scaled = influence_ref[...] * waves
    power = jnp.sum(jnp.sum(scaled * waves, axis=0, keepdims=True), axis=1, keepdims=True)
    out_ref[:, :128] = dot(back_ref[...], scaled.astype(bf16))
    out_ref[:, 128:] = jnp.broadcast_to(power, (256, 128))


def filter_y(lines, into, back, influence):
    return pl.pallas_call(
        filter_kernel,
        out_shape=jax.ShapeDtypeStruct((256, 256), f32),
        cost_estimate=pl.CostEstimate(
            flops=4 * 256 * 256 * 128, bytes_accessed=700000, transcendentals=0
        ),
        name="filter_y",
    )(lines, into, back, influence)


def inverse_kernel(energy_scale, lines_ref, along_x_ref, along_z_ref, out_ref, energy_ref):
    lines = lines_ref[...]
    waves = jnp.concatenate([lines[:128, :128], lines[128:, :128]], axis=1).astype(bf16)
    half = dot(along_x_ref[...], waves).astype(bf16)
    field = dot(half, along_z_ref[...]).astype(bf16)
    for gx in range(4):
        for gz in range(4):
            out_ref[gx, gz] = field[gx * 64 : (gx + 1) * 64, gz * 128 : (gz + 1) * 128]
    power = jnp.sum(lines[:, 128:], axis=0, keepdims=True)
    energy_ref[...] = jnp.broadcast_to(power * energy_scale, (8, 128))


def inverse_xz(lines, along_x, along_z, energy_scale):
    return pl.pallas_call(
        functools.partial(inverse_kernel, energy_scale),
        out_shape=[
            jax.ShapeDtypeStruct((4, 4, 64, 128), bf16),
            jax.ShapeDtypeStruct((8, 128), f32),
        ],
        cost_estimate=pl.CostEstimate(
            flops=2 * 256 * 256 * 640, bytes_accessed=900000, transcendentals=0
        ),
        name="inverse_xz",
    )(lines, along_x, along_z)


def interpolate_kernel(field_scale, field_ref, place_ref, out_ref):
    block = lax.broadcasted_iota(jnp.int32, (128, 128), 0) // PC
    for ax in range(4):
        field = field_ref[:, ax * PC : (ax + 1) * PC, :].reshape(PC * PC, 128)
        for cz in range(6):
            place = place_ref[ax * 6 + cz]
            row_x = spline_row(place[0:1])
            row_y = spline_row(place[1:2])
            row_z = spline_row(place[2:3])
            right = jnp.where(block == cz + 1, jnp.tile(row_z, (8, 1)), 0.0).astype(bf16)
            partial = dot(field, right)
            left = (row_y[:, None, :] * row_x[None, :, :]).reshape(PC * PC, 128)
            out_ref[ax * 6 + cz : ax * 6 + cz + 1, :] = (
                jnp.sum(partial * left, axis=0, keepdims=True) * field_scale
            )


def interpolate(field, place, field_scale):
    return pl.pallas_call(
        functools.partial(interpolate_kernel, field_scale),
        out_shape=jax.ShapeDtypeStruct((24, 128), f32),
        cost_estimate=pl.CostEstimate(
            flops=24 * 2 * 256 * 128 * 128, bytes_accessed=400000, transcendentals=0
        ),
        name="interpolate",
    )(field, place)


def backward_kernel(
    cells_z, reach_x, reach_z, weight_ref, slope_ref, potential_ref, msg_ref, self_ref, out_ref, near_ref
):
    step = pl.program_id(0)
    a = step // cells_z
    c = step % cells_z
    cells = slope_ref.shape[0]

    @pl.when(step == 0)
    def _():
        columns = jnp.transpose(potential_ref[...])
        for cell in range(cells):
            near_ref[cell] = (
                columns[:, cell : cell + 1] * slope_ref[cell].astype(f32)
            ).astype(bf16)

    total = jnp.zeros((128, 128), f32)
    for dy in range(3):
        for dx in range(3):
            near = near_ref[pl.ds((dy * reach_x + a + dx) * reach_z + c, 3)]
            total = total + dot(weight_ref[0, dy * 3 + dx], near.reshape(384, 128))
    own = near_ref[(reach_x + a + 1) * reach_z + c + 1]
    out_ref[0] = dot_t(total.astype(bf16), msg_ref[...]) + dot_t(own, self_ref[...])


def backward(weights, slope, potential, msg_weight, self_weight, cells, reach):
    count = cells[0] * cells[1]
    return pl.pallas_call(
        functools.partial(backward_kernel, cells[1], reach[1], reach[2]),
        grid=(count,),
        in_specs=[
            pl.BlockSpec((1, 9, 128, 384), lambda i: (i, 0, 0, 0)),
            whole(slope.shape),
            whole(potential.shape),
            whole((128, 128)),
            whole((128, 128)),
        ],
        out_specs=pl.BlockSpec((1, 128, 128), lambda i: (i, 0, 0)),
        out_shape=jax.ShapeDtypeStruct((count, 128, 128), f32),
        scratch_shapes=[pltpu.VMEM(slope.shape, bf16)],
        cost_estimate=pl.CostEstimate(
            flops=count * 29 * 2 * 128**3,
            bytes_accessed=count * 27 * 32768 + 3000000,
            transcendentals=0,
        ),
        name="backward",
    )(weights, slope, potential, msg_weight, self_weight)


def wave_tables(size_x, size_y, size_z):
    i16 = np.arange(16)
    along_z = np.zeros((4, 2, 64, 2, size_z))
    for g in range(4):
        table = cas(g * 64 + np.arange(64), np.arange(size_z), size_z)
        for a in range(2):
            along_z[g, a, :, a, :] = table
    points_x = np.array([g * 32 + a * 16 + i for a in range(2) for g in range(4) for i in i16])
    along_x = cas(np.arange(size_x), points_x, size_x)
    points_y = np.array(
        [gy * 16 + gx * 4 + gz for gx in range(4) for gy in range(16) for gz in range(4)]
    )
    into_y = cas(np.arange(size_y), points_y, size_y)
    back_x = np.array(
        [((2 * g - 1 + a) % 8) * 16 + i for g in range(4) for a in range(4) for i in i16]
    )
    back_z = np.array(
        [((4 * g - 2 + c) % 16) * 16 + k for g in range(4) for c in range(8) for k in i16]
    )
    tables = (
        along_z.reshape(4, 128, 2 * size_z),
        along_x,
        into_y,
        into_y.T,
        cas(back_x, np.arange(size_x), size_x),
        cas(np.arange(size_z), back_z, size_z),
    )
    return [jnp.asarray(np.ascontiguousarray(t), dtype=bf16) for t in tables]


def influence_of(size_x, size_y, size_z):
    device = lax.axis_index(everyone)

    def wave(index, size):
        signed = jnp.where(2 * index >= size, index - size, index)
        return signed.astype(f32) * (PC / size)

    wave_x = wave(device % size_x, size_x)
    wave_y = wave(jnp.arange(size_y, dtype=jnp.int32), size_y)[:, None]
    wave_z = wave(
        device // size_x * 128 + jnp.arange(size_z // 2, dtype=jnp.int32), size_z
    )[None, :]
    squared = wave_x * wave_x + wave_y * wave_y + wave_z * wave_z
    safe = jnp.where(squared > 0, squared, 1.0)
    return jnp.where(squared > 0, jnp.exp(-((math.pi * spread_width) ** 2) * squared) / safe, 0.0)


def swapped(value, axis):
    return lax.all_to_all(value, axis, split_axis=0, concat_axis=0, tiled=True)


def body(features, msg_weight, self_weight, charge_weight, spline_corner, spline_fraction):
    cells_x, cells_y, cells_z, slots, width = features.shape
    size_x = cells_x * PC * lax.axis_size("gx")
    size_y = cells_y * PC * lax.axis_size("gy")
    size_z = cells_z * PC * lax.axis_size("gz")
    cells = (cells_x, cells_z)
    reach = (3, cells_x + 2, cells_z + 2)
    volume = size_x // PC * (size_y // PC) * (size_z // PC)
    natoms = volume * slots

    own = features.reshape(cells_x * cells_z, slots, width)
    projected = dot(own.reshape(-1, width), msg_weight).astype(bf16)
    place = (spline_corner.astype(f32) + 1.0 + spline_fraction).reshape(1, cells_x, cells_z, 3, slots)
    near_place = surrounded(place).reshape(-1, 3, slots)
    near_place = jnp.pad(near_place, ((0, 0), (0, 5), (0, 0)))
    own_place = jnp.pad(place.reshape(-1, 3, slots), ((0, 0), (0, 5), (0, 0)))
    near = surrounded(projected.reshape(1, cells_x, cells_z, slots, width)).reshape(-1, slots, width)
    weights = pair_weights(near_place, cells, reach)
    read = jnp.broadcast_to(charge_weight.astype(f32)[None, :], (8, width))
    influence = influence_of(size_x, size_y, size_z)
    along_z, along_x, into_y, from_y, back_x, back_z = wave_tables(size_x, size_y, size_z)

    slope, mesh = message_layer(weights, near, own, self_weight, read, own_place, cells, reach)
    near_slope = surrounded(slope.reshape(1, cells_x, cells_z, slots, width)).reshape(
        -1, slots, width
    )

    mesh = swapped(mesh, plane).reshape(4, 4, PC, 128)
    lines = swapped(forward_xz(mesh, along_z, along_x), everyone)
    lines = swapped(filter_y(lines, into_y, from_y, influence), everyone)
    field, energy = inverse_xz(lines, back_x, back_z, coupling / (2.0 * volume * natoms))
    field = swapped(field.reshape(16, 64, 128), plane)
    row_place = near_place.reshape(3, 24, 8, slots)[1]
    potential = interpolate(field, row_place, coupling / volume)
    near_potential = with_neighbours(potential[None], "gy", 0).reshape(-1, slots)
    grad = backward(weights, near_slope, near_potential, msg_weight, self_weight, cells, reach)
    atom_potential = potential.reshape(reach[1], reach[2], slots)[1:-1, 1:-1]
    return (
        grad.reshape(features.shape),
        atom_potential.reshape(cells_x, cells_y, cells_z, slots),
        energy[0, 0],
    )


def solution(mesh):
    in_specs = (
        P("gx", "gy", "gz", None, None),
        P(),
        P(),
        P(),
        P("gx", "gy", "gz", None, None),
        P("gx", "gy", "gz", None, None),
    )
    out_specs = (P("gx", "gy", "gz", None, None), P("gx", "gy", "gz", None), P())
    return jax.shard_map(body, mesh=mesh, in_specs=in_specs, out_specs=out_specs, check_vma=False)
```

```python
import functools
import math

import jax
import jax.numpy as jnp
import numpy as np
from jax import lax
from jax.experimental import pallas as pl
from jax.experimental.pallas import tpu as pltpu
from jax.sharding import PartitionSpec as P

PC = 16
pair_scale = 0.1
coupling = 0.125
spread_width = 0.0625
f32 = jnp.float32
bf16 = jnp.bfloat16
plane = ("gx", "gz")
everyone = ("gx", "gy", "gz")


def dot(a, b):
    return jnp.dot(a, b, preferred_element_type=f32)


def dot_t(a, b, precision=None):
    return lax.dot_general(
        a, b, (((1,), (1,)), ((), ())), preferred_element_type=f32, precision=precision
    )


VM = pl.BlockSpec(memory_space=pltpu.VMEM)
ANY = pl.BlockSpec(memory_space=pl.ANY)
SMALL = pltpu.CompilerParams(vmem_limit_bytes=20 << 20)


def cas(rows, columns, size):
    turns = np.outer(rows, columns) % size
    angle = 2.0 * np.pi / size * turns
    return np.cos(angle) + np.sin(angle)


def moved(value, axis, step):
    count = lax.axis_size(axis)
    return lax.ppermute(value, axis, [(i, (i + step) % count) for i in range(count)])


def with_neighbours(value, axis, dim):
    length = value.shape[dim]
    last = lax.slice_in_dim(value, length - 1, length, axis=dim)
    first = lax.slice_in_dim(value, 0, 1, axis=dim)
    return jnp.concatenate([moved(last, axis, 1), value, moved(first, axis, -1)], axis=dim)


def halo_pieces(own):
    cells_x, cells_z = own.shape[:2]
    ends_z = ((cells_z - 1, 1), (0, -1))
    ends_x = ((cells_x - 1, 1), (0, -1))
    sides = [moved(own, "gy", 1), moved(own, "gy", -1)]
    own_z = [moved(own[:, at : at + 1], "gz", step) for at, step in ends_z]
    own_x = [moved(own[at : at + 1], "gx", step) for at, step in ends_x]
    side_z = [
        moved(jnp.stack([side[:, at : at + 1] for side in sides]), "gz", step)
        for at, step in ends_z
    ]
    side_x = [
        moved(jnp.stack([side[at : at + 1] for side in sides]), "gx", step) for at, step in ends_x
    ]
    corner = []
    for at, step in ends_x:
        rows = [
            jnp.concatenate([end[at : at + 1] for end in ends], axis=1)
            for ends in (
                [side_z[0][0], side_z[1][0]],
                own_z,
                [side_z[0][1], side_z[1][1]],
            )
        ]
        corner.append(moved(jnp.stack(rows), "gx", step))
    return [own] + sides + own_z + own_x + side_z + side_x + corner


PIECES = 13


def gather_pieces(pieces, near, sems, cells):
    cells_x, cells_z = cells
    inner_x, inner_z = pl.ds(1, cells_x), pl.ds(1, cells_z)
    edge_x = (pl.ds(0, 1), pl.ds(cells_x + 1, 1))
    edge_z = (pl.ds(0, 1), pl.ds(cells_z + 1, 1))
    own, below, above, zb, za, xb, xa, szb, sza, sxb, sxa, cb, ca = pieces
    pairs = [
        (own, near.at[1, inner_x, inner_z]),
        (below, near.at[0, inner_x, inner_z]),
        (above, near.at[2, inner_x, inner_z]),
        (zb, near.at[1, inner_x, edge_z[0]]),
        (za, near.at[1, inner_x, edge_z[1]]),
        (xb, near.at[1, edge_x[0], inner_z]),
        (xa, near.at[1, edge_x[1], inner_z]),
    ]
    for side, dy in ((0, 0), (1, 2)):
        pairs += [
            (szb.at[side], near.at[dy, inner_x, edge_z[0]]),
            (sza.at[side], near.at[dy, inner_x, edge_z[1]]),
            (sxb.at[side], near.at[dy, edge_x[0], inner_z]),
            (sxa.at[side], near.at[dy, edge_x[1], inner_z]),
        ]
    for end in (0, 1):
        pairs += [
            (cb.at[:, :, pl.ds(end, 1)], near.at[:, edge_x[0], edge_z[end]]),
            (ca.at[:, :, pl.ds(end, 1)], near.at[:, edge_x[1], edge_z[end]]),
        ]
    copies = [
        pltpu.make_async_copy(source, target, sems.at[i])
        for i, (source, target) in enumerate(pairs)
    ]
    for copy in copies:
        copy.start()
    for copy in copies:
        copy.wait()


COPIES = 19


BLOCKS = ((0, 0), (0, 1), (1, 0), (1, 1), (1, 2), (1, 3), (2, 2), (2, 3))
COLUMNS = ((0, 0, 1, 0, 1), (3, 1, 2, 1, 1), (1, 2, 4, 0, 2), (2, 4, 6, 0, 2))
SPANS = ((0, 2, 0, 2), (2, 6, 0, 4), (6, 8, 2, 2))


def weights_kernel(place_ref, out_ref):
    def position(index):
        place = place_ref[index]
        return (place * (1.0 / PC)).astype(bf16).astype(f32)

    def combination(t, carry):
        a = t % 2
        column = jnp.where(t < 2, 3 * t, t // 2)
        shift = (column - a - 1).astype(f32)
        for c in range(4):
            centre = position((4 + a + 1) * 6 + c + 1)
            centre = jnp.concatenate([centre, jnp.zeros((5, 128), f32)], axis=0)
            columns = jnp.transpose(centre)
            centre_x = jnp.broadcast_to(columns[:, 0:1], (128, 128))
            centre_y = jnp.broadcast_to(columns[:, 1:2], (128, 128))
            centre_z = jnp.broadcast_to(columns[:, 2:3], (128, 128))
            for block, (pair, owner) in enumerate(BLOCKS):
                if owner != c:
                    continue
                for dy in range(3):
                    for half in range(2):
                        where = (dy * 2 + half) * 128
                        dz = 2 * pair + half - c - 1
                        if abs(dz) > 1:
                            tile = jnp.zeros((128, 128), bf16)
                        else:
                            near = position((dy * 4 + column) * 6 + 2 * pair + half)
                            gap_x = (near[0:1] + shift) - centre_x
                            gap_y = (near[1:2] + (dy - 1.0)) - centre_y
                            gap_z = (near[2:3] + float(dz)) - centre_z
                            squared = gap_x * gap_x + gap_y * gap_y + gap_z * gap_z
                            inside = jnp.maximum(1.0 - squared, 0.0)
                            tile = (pair_scale * inside * inside).astype(bf16)
                        out_ref[t, block, :, where : where + 128] = tile
        return carry

    lax.fori_loop(0, 6, combination, 0)


def pair_weights(place):
    return pl.pallas_call(
        weights_kernel,
        in_specs=[VM],
        out_specs=VM,
        out_shape=jax.ShapeDtypeStruct((6, 8, 128, 768), bf16),
        cost_estimate=pl.CostEstimate(
            flops=216 * 16384 * 14, bytes_accessed=288 * 32768, transcendentals=0
        ),
        compiler_params=SMALL,
        name="pair_weights",
    )(place)


def add_pairs(weight_ref, near_ref, total_ref):
    for column, low, high, first, count in COLUMNS:
        for pair, (start, stop, cell, width) in enumerate(SPANS):
            left = weight_ref[low:high, start:stop].reshape(count * width * 128, 768)
            right = jnp.concatenate(
                [
                    near_ref[dy, column, 2 * pair : 2 * pair + 2].reshape(256, 128)
                    for dy in range(3)
                ],
                axis=0,
            )
            total_ref[first : first + count, cell : cell + width] += dot(left, right).reshape(
                count, width, 128, 128
            )


def spline_row(place):
    point = lax.broadcasted_iota(jnp.int32, (PC, 128), 0).astype(f32)
    away = jnp.abs(point - place)
    near = (4.0 - 6.0 * away * away + 3.0 * away * away * away) * (1.0 / 6.0)
    rest = 2.0 - away
    far = rest * rest * rest * (1.0 / 6.0)
    return jnp.where(away < 1.0, near, jnp.where(away < 2.0, far, 0.0))


def message_kernel(*refs):
    weight_ref = refs[0]
    pieces = refs[1 : 1 + PIECES]
    own_ref, self_ref, read_ref, place_ref = refs[1 + PIECES : 5 + PIECES]
    slope_ref, mesh_ref = refs[5 + PIECES : 7 + PIECES]
    near_ref, total_ref, high_ref, low_ref, left_ref, right_ref, sems = refs[7 + PIECES :]
    gather_pieces(pieces, near_ref, sems, (2, 4))
    total_ref[...] = dot(own_ref[...].reshape(1024, 128), self_ref[...]).reshape(2, 4, 128, 128)
    add_pairs(weight_ref, near_ref, total_ref)
    read = read_ref[...].astype(f32)

    def finish(cell, carry):
        a, c = cell // 4, cell % 4
        preact = total_ref[a, c]
        sigma = 0.5 + 0.5 * jnp.tanh(0.5 * preact)
        slope_ref[a, c] = (read * (sigma * (1.0 + preact * (1.0 - sigma)))).astype(bf16)
        silu = preact * sigma
        high = silu.astype(bf16)
        high_ref[cell] = high
        low_ref[cell] = (silu - high.astype(f32)).astype(bf16)
        return carry

    lax.fori_loop(0, 8, finish, 0)
    wide = jnp.broadcast_to(read_ref[...], (16, 128))
    charge = dot_t(wide, high_ref[...].reshape(1024, 128)) + dot_t(
        wide, low_ref[...].reshape(1024, 128)
    )
    block = lax.broadcasted_iota(jnp.int32, (128, 128), 0) // PC
    for cell in range(8):
        lanes = slice(cell * 128, (cell + 1) * 128)
        place = place_ref[cell]
        row_x = spline_row(place[0:1])
        row_y = spline_row(place[1:2]) * charge[0:1, lanes]
        row_z = spline_row(place[2:3])
        left_ref[:, lanes] = (
            (row_y[:, None, :] * row_x[None, :, :]).reshape(PC * PC, 128).astype(bf16)
        )
        right_ref[:, lanes] = jnp.where(block == cell, jnp.tile(row_z, (8, 1)), 0.0).astype(bf16)
    mesh_ref[...] = dot_t(left_ref[...], right_ref[...]).reshape(PC, PC, 128).astype(bf16)


def message_layer(weights, pieces, own, self_weight, read, place):
    return pl.pallas_call(
        message_kernel,
        in_specs=[VM] + [ANY] * PIECES + [VM] * 4,
        out_specs=[VM, VM],
        out_shape=[
            jax.ShapeDtypeStruct((2, 4, 128, 128), bf16),
            jax.ShapeDtypeStruct((PC, PC, 128), bf16),
        ],
        scratch_shapes=[
            pltpu.VMEM((3, 4, 6, 128, 128), bf16),
            pltpu.VMEM((2, 4, 128, 128), f32),
            pltpu.VMEM((8, 128, 128), bf16),
            pltpu.VMEM((8, 128, 128), bf16),
            pltpu.VMEM((PC * PC, 1024), bf16),
            pltpu.VMEM((128, 1024), bf16),
            pltpu.SemaphoreType.DMA((COPIES,)),
        ],
        cost_estimate=pl.CostEstimate(
            flops=8 * 28 * 2 * 128**3, bytes_accessed=12000000, transcendentals=8 * 16384
        ),
        compiler_params=SMALL,
        name="message",
    )(weights, *pieces, own, self_weight, read, place)


def forward_kernel(mesh_ref, along_z_ref, along_x_ref, out_ref):
    total = jnp.zeros((64, 512), f32)
    for g in range(4):
        total = total + dot(mesh_ref[:, g].reshape(64, 128), along_z_ref[g])
    lines = jnp.concatenate([total[:, :256], total[:, 256:]], axis=0).astype(bf16)
    waves = dot(along_x_ref[...], lines)
    out_ref[0:128, :] = waves[:, :128]
    out_ref[128:256, :] = waves[:, 128:]


def forward_xz(mesh, along_z, along_x):
    return pl.pallas_call(
        forward_kernel,
        in_specs=[VM] * 3,
        out_specs=VM,
        compiler_params=SMALL,
        out_shape=jax.ShapeDtypeStruct((256, 128), f32),
        cost_estimate=pl.CostEstimate(
            flops=2 * 64 * 512 * 512, bytes_accessed=800000, transcendentals=0
        ),
        name="forward_xz",
    )(mesh, along_z, along_x)


def filter_kernel(lines_ref, into_ref, back_ref, influence_ref, out_ref):
    waves = dot(into_ref[...], lines_ref[...].astype(bf16))
    scaled = influence_ref[...] * waves
    power = jnp.sum(jnp.sum(scaled * waves, axis=0, keepdims=True), axis=1, keepdims=True)
    out_ref[:, :128] = dot(back_ref[...], scaled.astype(bf16))
    out_ref[:, 128:] = jnp.broadcast_to(power, (256, 128))


def filter_y(lines, into, back, influence):
    return pl.pallas_call(
        filter_kernel,
        in_specs=[VM] * 4,
        out_specs=VM,
        compiler_params=SMALL,
        out_shape=jax.ShapeDtypeStruct((256, 256), f32),
        cost_estimate=pl.CostEstimate(
            flops=4 * 256 * 256 * 128, bytes_accessed=700000, transcendentals=0
        ),
        name="filter_y",
    )(lines, into, back, influence)


def inverse_kernel(energy_scale, lines_ref, along_x_ref, along_z_ref, out_ref, energy_ref):
    lines = lines_ref[...]
    waves = jnp.concatenate([lines[:128, :128], lines[128:, :128]], axis=1).astype(bf16)
    half = dot(along_x_ref[...], waves).astype(bf16)
    field = dot(half, along_z_ref[...]).astype(bf16)
    for gx in range(4):
        for gz in range(4):
            out_ref[gx, gz] = field[gx * 64 : (gx + 1) * 64, gz * 128 : (gz + 1) * 128]
    power = jnp.sum(lines[:, 128:], axis=0, keepdims=True)
    energy_ref[...] = jnp.broadcast_to(power * energy_scale, (8, 128))


def inverse_xz(lines, along_x, along_z, energy_scale):
    return pl.pallas_call(
        functools.partial(inverse_kernel, energy_scale),
        in_specs=[VM] * 3,
        out_specs=[VM, VM],
        compiler_params=SMALL,
        out_shape=[
            jax.ShapeDtypeStruct((4, 4, 64, 128), bf16),
            jax.ShapeDtypeStruct((8, 128), f32),
        ],
        cost_estimate=pl.CostEstimate(
            flops=2 * 256 * 256 * 640, bytes_accessed=900000, transcendentals=0
        ),
        name="inverse_xz",
    )(lines, along_x, along_z)


def interpolate_kernel(field_scale, field_ref, place_ref, out_ref, own_ref):
    block = lax.broadcasted_iota(jnp.int32, (128, 128), 0) // PC
    for ax in range(4):
        field = field_ref[:, ax * PC : (ax + 1) * PC, :].reshape(PC * PC, 128)
        for cz in range(6):
            place = place_ref[ax * 6 + cz]
            row_x = spline_row(place[0:1])
            row_y = spline_row(place[1:2])
            row_z = spline_row(place[2:3])
            right = jnp.where(block == cz + 1, jnp.tile(row_z, (8, 1)), 0.0).astype(bf16)
            partial = dot(field, right)
            left = (row_y[:, None, :] * row_x[None, :, :]).reshape(PC * PC, 128)
            potential = jnp.sum(partial * left, axis=0, keepdims=True) * field_scale
            out_ref[ax * 6 + cz : ax * 6 + cz + 1, :] = potential
            if 1 <= ax <= 2 and 1 <= cz <= 4:
                at = (ax - 1) * 4 + cz - 1
                own_ref[at : at + 1, :] = potential


def interpolate(field, place, field_scale):
    return pl.pallas_call(
        functools.partial(interpolate_kernel, field_scale),
        in_specs=[VM] * 2,
        out_specs=[VM, VM],
        compiler_params=SMALL,
        out_shape=[
            jax.ShapeDtypeStruct((24, 128), f32),
            jax.ShapeDtypeStruct((8, 128), f32),
        ],
        cost_estimate=pl.CostEstimate(
            flops=24 * 2 * 256 * 128 * 128, bytes_accessed=400000, transcendentals=0
        ),
        name="interpolate",
    )(field, place)


def backward_kernel(*refs):
    weight_ref = refs[0]
    pieces = refs[1 : 1 + PIECES]
    potential_refs = refs[1 + PIECES : 4 + PIECES]
    msg_ref, self_ref = refs[4 + PIECES : 6 + PIECES]
    out_ref = refs[6 + PIECES]
    slope_ref, near_ref, total_ref, sems = refs[7 + PIECES :]
    gather_pieces(pieces, slope_ref, sems, (2, 4))
    for dy in range(3):
        columns = jnp.transpose(potential_refs[dy][...])
        for x in range(4):
            for z in range(6):
                cell = x * 6 + z
                near_ref[dy, x, z] = (
                    columns[:, cell : cell + 1] * slope_ref[dy, x, z].astype(f32)
                ).astype(bf16)
    total_ref[...] = jnp.zeros_like(total_ref)
    add_pairs(weight_ref, near_ref, total_ref)
    back = total_ref[...].reshape(1024, 128).astype(bf16)
    own = near_ref[1, 1:3, 1:5].reshape(1024, 128)
    out_ref[...] = (dot_t(back, msg_ref[...]) + dot_t(own, self_ref[...])).reshape(8, 128, 128)


def backward(weights, pieces, potentials, msg_weight, self_weight):
    return pl.pallas_call(
        backward_kernel,
        in_specs=[VM] + [ANY] * PIECES + [VM] * 5,
        out_specs=VM,
        out_shape=jax.ShapeDtypeStruct((8, 128, 128), f32),
        scratch_shapes=[
            pltpu.VMEM((3, 4, 6, 128, 128), bf16),
            pltpu.VMEM((3, 4, 6, 128, 128), bf16),
            pltpu.VMEM((2, 4, 128, 128), f32),
            pltpu.SemaphoreType.DMA((COPIES,)),
        ],
        cost_estimate=pl.CostEstimate(
            flops=8 * 29 * 2 * 128**3, bytes_accessed=12000000, transcendentals=0
        ),
        compiler_params=SMALL,
        name="backward",
    )(weights, *pieces, *potentials, msg_weight, self_weight)


def wave_tables(size_x, size_y, size_z):
    i16 = np.arange(16)
    along_z = np.zeros((4, 2, 64, 2, size_z))
    for g in range(4):
        table = cas(g * 64 + np.arange(64), np.arange(size_z), size_z)
        for a in range(2):
            along_z[g, a, :, a, :] = table
    points_x = np.array([g * 32 + a * 16 + i for a in range(2) for g in range(4) for i in i16])
    along_x = cas(np.arange(size_x), points_x, size_x)
    points_y = np.array(
        [gy * 16 + gx * 4 + gz for gx in range(4) for gy in range(16) for gz in range(4)]
    )
    into_y = cas(np.arange(size_y), points_y, size_y)
    back_x = np.array(
        [((2 * g - 1 + a) % 8) * 16 + i for g in range(4) for a in range(4) for i in i16]
    )
    back_z = np.array(
        [((4 * g - 2 + c) % 16) * 16 + k for g in range(4) for c in range(8) for k in i16]
    )
    tables = (
        along_z.reshape(4, 128, 2 * size_z),
        along_x,
        into_y,
        into_y.T,
        cas(back_x, np.arange(size_x), size_x),
        cas(np.arange(size_z), back_z, size_z),
    )
    return [jnp.asarray(np.ascontiguousarray(t), dtype=bf16) for t in tables]


def influence_of(size_x, size_y, size_z):
    device = lax.axis_index(everyone)

    def wave(index, size):
        signed = jnp.where(2 * index >= size, index - size, index)
        return signed.astype(f32) * (PC / size)

    wave_x = wave(device % size_x, size_x)
    wave_y = wave(jnp.arange(size_y, dtype=jnp.int32), size_y)[:, None]
    wave_z = wave(
        device // size_x * 128 + jnp.arange(size_z // 2, dtype=jnp.int32), size_z
    )[None, :]
    squared = wave_x * wave_x + wave_y * wave_y + wave_z * wave_z
    safe = jnp.where(squared > 0, squared, 1.0)
    return jnp.where(squared > 0, jnp.exp(-((math.pi * spread_width) ** 2) * squared) / safe, 0.0)


def swapped(value, axis):
    return lax.all_to_all(value, axis, split_axis=0, concat_axis=0, tiled=True)


def body(features, msg_weight, self_weight, charge_weight, spline_corner, spline_fraction):
    cells_x, cells_y, cells_z, slots, width = features.shape
    size_x = cells_x * PC * lax.axis_size("gx")
    size_y = cells_y * PC * lax.axis_size("gy")
    size_z = cells_z * PC * lax.axis_size("gz")
    volume = size_x // PC * (size_y // PC) * (size_z // PC)
    natoms = volume * slots
    columns = (cells_x, cells_z, slots, width)

    own = features.reshape(cells_x * cells_z, slots, width)
    projected = dot(own.reshape(-1, width), msg_weight).astype(bf16)
    place = spline_corner.astype(f32) + 1.0 + spline_fraction
    place = place.reshape(cells_x, cells_z, 3, slots)
    row_place = with_neighbours(with_neighbours(place, "gz", 1), "gx", 0)
    near_place = with_neighbours(row_place[None], "gy", 0).reshape(-1, 3, slots)
    row_place = row_place.reshape(-1, 3, slots)
    weights = pair_weights(near_place)
    pieces = halo_pieces(projected.reshape(columns))
    influence = influence_of(size_x, size_y, size_z)
    along_z, along_x, into_y, from_y, back_x, back_z = wave_tables(size_x, size_y, size_z)

    slope, mesh = message_layer(
        weights, pieces, own, self_weight, charge_weight[None, :], place.reshape(-1, 3, slots)
    )
    slope_pieces = halo_pieces(slope)

    mesh = swapped(mesh, plane).reshape(4, 4, PC, 128)
    lines = swapped(forward_xz(mesh, along_z, along_x), everyone)
    lines = swapped(filter_y(lines, into_y, from_y, influence), everyone)
    field, energy = inverse_xz(lines, back_x, back_z, coupling / (2.0 * volume * natoms))
    field = swapped(field.reshape(16, 64, 128), plane)
    potential, atom_potential = interpolate(field, row_place, coupling / volume)
    potentials = [moved(potential, "gy", 1), potential, moved(potential, "gy", -1)]
    grad = backward(weights, slope_pieces, potentials, msg_weight, self_weight)
    return (
        grad.reshape(features.shape),
        atom_potential.reshape(cells_x, cells_y, cells_z, slots),
        energy[0, 0],
    )


def solution(mesh):
    in_specs = (
        P("gx", "gy", "gz", None, None),
        P(),
        P(),
        P(),
        P("gx", "gy", "gz", None, None),
        P("gx", "gy", "gz", None, None),
    )
    out_specs = (P("gx", "gy", "gz", None, None), P("gx", "gy", "gz", None), P())
    return jax.shard_map(body, mesh=mesh, in_specs=in_specs, out_specs=out_specs, check_vma=False)
```

```python
import functools
import math

import jax
import jax.numpy as jnp
import numpy as np
from jax import lax
from jax.experimental import pallas as pl
from jax.experimental.pallas import tpu as pltpu
from jax.sharding import PartitionSpec as P

PC = 16
pair_scale = 0.1
coupling = 0.125
spread_width = 0.0625
f32 = jnp.float32
bf16 = jnp.bfloat16
plane = ("gx", "gz")
everyone = ("gx", "gy", "gz")


def dot(a, b):
    return jnp.dot(a, b, preferred_element_type=f32)


def dot_t(a, b, precision=None):
    return lax.dot_general(
        a, b, (((1,), (1,)), ((), ())), preferred_element_type=f32, precision=precision
    )


def whole(shape):
    zeros = (0,) * len(shape)
    return pl.BlockSpec(shape, lambda *_: zeros)


VM = pl.BlockSpec(memory_space=pltpu.VMEM)
ANY = pl.BlockSpec(memory_space=pl.ANY)
SMALL = pltpu.CompilerParams(vmem_limit_bytes=20 << 20)
LARGE = pltpu.CompilerParams(vmem_limit_bytes=50 << 20)
MIDDLE = pltpu.CompilerParams(vmem_limit_bytes=36 << 20)


def cas(rows, columns, size):
    turns = np.outer(rows, columns) % size
    angle = 2.0 * np.pi / size * turns
    return np.cos(angle) + np.sin(angle)


def moved(value, axis, step):
    count = lax.axis_size(axis)
    pairs = [(i, (i + step) % count) for i in range(count)]
    return lax.ppermute(value.reshape(-1, 128), axis, pairs).reshape(value.shape)


def halo_yz(own):
    last = own.shape[1] - 1
    sides = [moved(own, "gy", 1), moved(own, "gy", -1)]
    rows = [sides[0], own, sides[1]]
    ends = [
        moved(jnp.stack([row[:, last:] for row in rows]), "gz", 1),
        moved(jnp.stack([row[:, :1] for row in rows]), "gz", -1),
    ]
    return sides + ends


def halo_x(own, near):
    below, above, left, right = near
    last = own.shape[0] - 1
    rows = (below, own, above)

    def slab(at):
        return jnp.stack(
            [
                jnp.concatenate(
                    [left[i, at : at + 1], row[at : at + 1], right[i, at : at + 1]], axis=1
                )
                for i, row in enumerate(rows)
            ]
        )

    return [moved(slab(last), "gx", 1), moved(slab(0), "gx", -1)]


def project_kernel(features_ref, weight_ref, corner_ref, fraction_ref, out_ref):
    value = dot(features_ref[...].reshape(1024, 128), weight_ref[...]).astype(bf16)
    out_ref[:, :128, :] = value.reshape(8, 128, 128)
    place = corner_ref[...].astype(f32) + 1.0 + fraction_ref[...]
    high = place.astype(bf16).astype(f32)
    rest = place - high
    middle = rest.astype(bf16).astype(f32)
    low = rest - middle
    two = jnp.zeros((8, 2, 128), f32)
    five = jnp.zeros((8, 5, 128), f32)
    out_ref[:, 128:, :] = jnp.concatenate([high, low, two, middle, five], axis=1).astype(bf16)


def project(features, weight, corner, fraction):
    return pl.pallas_call(
        project_kernel,
        grid=(1,),
        in_specs=[whole((8, 128, 128)), whole((128, 128)), whole((8, 3, 128)), whole((8, 3, 128))],
        out_specs=whole((8, 144, 128)),
        out_shape=jax.ShapeDtypeStruct((8, 144, 128), bf16),
        compiler_params=SMALL,
        name="project",
    )(features, weight, corner, fraction)


def place_of(rows):
    rows = rows.astype(f32)
    return rows[0:8] + rows[8:16] + pltpu.roll(rows[0:8], 5, 0)


BLOCKS = ((0, 0), (0, 1), (1, 0), (1, 1), (1, 2), (1, 3), (2, 2), (2, 3))
SPANS = ((0, 2, 0, 2), (2, 6, 0, 4), (6, 8, 2, 2))
ORDER_Y = (0, 2, 1)


def weigh(centres, a, shift, near, store):
    for c in range(4):
        columns = jnp.transpose(centres[a, c])
        centre_x = jnp.broadcast_to(columns[:, 0:1], (128, 128))
        centre_y = jnp.broadcast_to(columns[:, 1:2], (128, 128))
        centre_z = jnp.broadcast_to(columns[:, 2:3], (128, 128))
        for block, (pair, owner) in enumerate(BLOCKS):
            if owner != c:
                continue
            for at, dy in enumerate(ORDER_Y):
                for half in range(2):
                    dz = 2 * pair + half - c - 1
                    if abs(dz) > 1:
                        tile = jnp.zeros((128, 128), bf16)
                    else:
                        row = near(dy, 2 * pair + half)
                        gap_x = (row[0:1] + shift) - centre_x
                        gap_y = (row[1:2] + (dy - 1.0)) - centre_y
                        gap_z = (row[2:3] + float(dz)) - centre_z
                        squared = gap_x * gap_x + gap_y * gap_y + gap_z * gap_z
                        inside = jnp.maximum(1.0 - squared, 0.0)
                        tile = (pair_scale * inside * inside).astype(bf16)
                    store(block, (at * 2 + half) * 128, tile)


def inner_kernel(
    own_ref, below_ref, above_ref, left_ref, right_ref, features_ref, self_ref,
    weight_out, total_ref, place_ref, weight_ref, position_ref, sems
):
    refs = (below_ref, own_ref, above_ref)

    def cell(dy, x, z):
        if z == 0:
            return left_ref.at[dy, x, 0]
        if z == 5:
            return right_ref.at[dy, x, 0]
        return refs[dy].at[x, z - 1]

    def places(x, carry):
        for dy in range(3):
            for z in range(6):
                place = place_of(cell(dy, x, z)[128:144, :])
                place_ref[dy, x, z] = place
                position_ref[dy, x, z] = (place * (1.0 / PC)).astype(bf16).astype(f32)
        return carry

    lax.fori_loop(0, 2, places, 0)

    def copy_out(t):
        return pltpu.make_async_copy(weight_ref.at[t], weight_out.at[t], sems.at[t])

    total_ref[...] = dot(features_ref[...].reshape(1024, 128), self_ref[...]).reshape(
        2, 4, 128, 128
    )

    def combination(t, carry):
        x, a = t // 2, t % 2

        def store(block, lane, tile):
            weight_ref[t, block, :, lane : lane + 128] = tile

        weigh(
            position_ref.at[1, :, 1:5],
            a,
            (x - a).astype(f32),
            lambda dy, z: position_ref[dy, x, z],
            store,
        )
        copy_out(t).start()
        for pair, (start, stop, first, width) in enumerate(SPANS):
            near = jnp.concatenate(
                [
                    cell(dy, x, 2 * pair + half)[0:128, :]
                    for dy in ORDER_Y
                    for half in range(2)
                ],
                axis=0,
            )
            part = dot(weight_ref[t, start:stop].reshape(width * 128, 768), near)
            total_ref[a, first : first + width] += part.reshape(width, 128, 128)
        return carry

    lax.fori_loop(0, 4, combination, 0)
    for t in range(4):
        copy_out(t).wait()


def inner_pairs(own, near, features, self_weight):
    return pl.pallas_call(
        inner_kernel,
        in_specs=[VM] * 7,
        out_specs=[ANY, VM, VM],
        out_shape=[
            jax.ShapeDtypeStruct((6, 8, 128, 768), bf16),
            jax.ShapeDtypeStruct((2, 4, 128, 128), f32),
            jax.ShapeDtypeStruct((3, 2, 6, 8, 128), f32),
        ],
        scratch_shapes=[
            pltpu.VMEM((4, 8, 128, 768), bf16),
            pltpu.VMEM((3, 2, 6, 8, 128), f32),
            pltpu.SemaphoreType.DMA((4,)),
        ],
        cost_estimate=pl.CostEstimate(
            flops=9000000000, bytes_accessed=9000000, transcendentals=0
        ),
        compiler_params=LARGE,
        name="inner_pairs",
    )(own, *near, features, self_weight)


def spline_row(place):
    point = lax.broadcasted_iota(jnp.int32, (PC, 128), 0).astype(f32)
    away = jnp.abs(point - place)
    near = (4.0 - 6.0 * away * away + 3.0 * away * away * away) * (1.0 / 6.0)
    rest = 2.0 - away
    far = rest * rest * rest * (1.0 / 6.0)
    return jnp.where(away < 1.0, near, jnp.where(away < 2.0, far, 0.0))


def message_kernel(
    before_ref, after_ref, part_ref, place_ref, read_ref, _,
    weight_out, slope_ref, mesh_ref, row_place_ref,
    weight_ref, position_ref, centre_ref, total_ref, high_ref, low_ref, charge_ref, left_ref,
    right_ref, sems
):
    refs = (before_ref, after_ref)

    def position(place):
        return (place * (1.0 / PC)).astype(bf16).astype(f32)

    def places(dy, carry):
        for side in range(2):
            for z in range(6):
                place = place_of(refs[side][dy, 0, z, 128:144, :])
                position_ref[side, dy, z] = position(place)

                @pl.when(dy == 1)
                def _():
                    row_place_ref[3 * side, z] = place

        return carry

    lax.fori_loop(0, 3, places, 0)
    for x in range(2):
        for z in range(6):
            place = place_ref[1, x, z]
            row_place_ref[1 + x, z] = place
            if 1 <= z <= 4:
                centre_ref[x, z - 1] = position(place)

    def copy_out(t):
        return pltpu.make_async_copy(weight_ref.at[t], weight_out.at[4 + t], sems.at[t])

    def combination(t, carry):
        def store(block, lane, tile):
            weight_ref[t, block, :, lane : lane + 128] = tile

        weigh(
            centre_ref,
            t,
            (2 * t - 1).astype(f32),
            lambda dy, z: position_ref[t, dy, z],
            store,
        )
        copy_out(t).start()
        return carry

    lax.fori_loop(0, 2, combination, 0)
    total_ref[...] = part_ref[...]
    for t in range(2):
        for pair, (start, stop, first, width) in enumerate(SPANS):
            near = jnp.concatenate(
                [
                    refs[t][dy, 0, 2 * pair + half, 0:128, :]
                    for dy in ORDER_Y
                    for half in range(2)
                ],
                axis=0,
            )
            part = dot(weight_ref[t, start:stop].reshape(width * 128, 768), near)
            total_ref[t, first : first + width] += part.reshape(width, 128, 128)
    read = read_ref[...].astype(f32)

    def finish(cell, carry):
        a, c = cell // 4, cell % 4
        preact = total_ref[a, c]
        sigma = 0.5 + 0.5 * jnp.tanh(0.5 * preact)
        slope_ref[a, c] = (read * (sigma * (1.0 + preact * (1.0 - sigma)))).astype(bf16)
        silu = preact * sigma
        high = silu.astype(bf16)
        high_ref[cell] = high
        low_ref[cell] = (silu - high.astype(f32)).astype(bf16)
        return carry

    lax.fori_loop(0, 8, finish, 0)
    wide = jnp.broadcast_to(read_ref[...], (16, 128))
    charge_ref[...] = dot_t(wide, high_ref[...].reshape(1024, 128)) + dot_t(
        wide, low_ref[...].reshape(1024, 128)
    )
    block = lax.broadcasted_iota(jnp.int32, (128, 128), 0) // PC

    def spread(cell, carry):
        lanes = pl.ds(pl.multiple_of(cell * 128, 128), 128)
        place = place_ref[1, cell // 4, cell % 4 + 1]
        row_x = spline_row(place[0:1])
        row_y = spline_row(place[1:2]) * charge_ref[0:1, lanes]
        row_z = spline_row(place[2:3])
        left_ref[:, lanes] = (
            (row_y[:, None, :] * row_x[None, :, :]).reshape(PC * PC, 128).astype(bf16)
        )
        right_ref[:, lanes] = jnp.where(block == cell, jnp.tile(row_z, (8, 1)), 0.0).astype(bf16)
        return carry

    lax.fori_loop(0, 8, spread, 0)
    mesh_ref[...] = dot_t(left_ref[...], right_ref[...]).reshape(PC, PC, 128).astype(bf16)
    for t in range(2):
        copy_out(t).wait()


def message_layer(ends, part, place, read, weights):
    return pl.pallas_call(
        message_kernel,
        in_specs=[VM] * 5 + [ANY],
        out_specs=[ANY, VM, VM, VM],
        input_output_aliases={5: 0},
        out_shape=[
            jax.ShapeDtypeStruct((6, 8, 128, 768), bf16),
            jax.ShapeDtypeStruct((2, 4, 128, 128), bf16),
            jax.ShapeDtypeStruct((PC, PC, 128), bf16),
            jax.ShapeDtypeStruct((4, 6, 8, 128), f32),
        ],
        scratch_shapes=[
            pltpu.VMEM((2, 8, 128, 768), bf16),
            pltpu.VMEM((2, 3, 6, 8, 128), f32),
            pltpu.VMEM((2, 4, 8, 128), f32),
            pltpu.VMEM((2, 4, 128, 128), f32),
            pltpu.VMEM((8, 128, 128), bf16),
            pltpu.VMEM((8, 128, 128), bf16),
            pltpu.VMEM((16, 1024), f32),
            pltpu.VMEM((PC * PC, 1024), bf16),
            pltpu.VMEM((128, 1024), bf16),
            pltpu.SemaphoreType.DMA((2,)),
        ],
        cost_estimate=pl.CostEstimate(
            flops=5000000000, bytes_accessed=6000000, transcendentals=8 * 16384
        ),
        compiler_params=LARGE,
        name="message",
    )(*ends, part, place, read, weights)


def forward_kernel(mesh_ref, along_z_ref, along_x_ref, out_ref):
    total = jnp.zeros((64, 512), f32)
    for g in range(4):
        total = total + dot(mesh_ref[:, g].reshape(64, 128), along_z_ref[g])
    lines = jnp.concatenate([total[:, :256], total[:, 256:]], axis=0).astype(bf16)
    waves = dot(along_x_ref[...], lines)
    out_ref[0:128, :] = waves[:, :128]
    out_ref[128:256, :] = waves[:, 128:]


def forward_xz(mesh, along_z, along_x):
    return pl.pallas_call(
        forward_kernel,
        in_specs=[VM] * 3,
        out_specs=VM,
        compiler_params=SMALL,
        out_shape=jax.ShapeDtypeStruct((256, 128), f32),
        cost_estimate=pl.CostEstimate(
            flops=2 * 64 * 512 * 512, bytes_accessed=800000, transcendentals=0
        ),
        name="forward_xz",
    )(mesh, along_z, along_x)


def filter_kernel(lines_ref, into_ref, back_ref, influence_ref, out_ref):
    waves = dot(into_ref[...], lines_ref[...].astype(bf16))
    scaled = influence_ref[...] * waves
    power = jnp.sum(jnp.sum(scaled * waves, axis=0, keepdims=True), axis=1, keepdims=True)
    out_ref[pl.ds(0, 256, stride=2), :] = dot(back_ref[...], scaled.astype(bf16))
    out_ref[pl.ds(1, 256, stride=2), :] = jnp.broadcast_to(power, (256, 128))


def filter_y(lines, into, back, influence):
    return pl.pallas_call(
        filter_kernel,
        in_specs=[VM] * 4,
        out_specs=VM,
        compiler_params=SMALL,
        out_shape=jax.ShapeDtypeStruct((512, 128), f32),
        cost_estimate=pl.CostEstimate(
            flops=4 * 256 * 256 * 128, bytes_accessed=700000, transcendentals=0
        ),
        name="filter_y",
    )(lines, into, back, influence)


def inverse_kernel(energy_scale, lines_ref, along_x_ref, along_z_ref, out_ref, energy_ref):
    waves = jnp.concatenate(
        [lines_ref[pl.ds(0, 128, stride=2), :], lines_ref[pl.ds(256, 128, stride=2), :]], axis=1
    ).astype(bf16)
    half = dot(along_x_ref[...], waves).astype(bf16)
    field = dot(half, along_z_ref[...]).astype(bf16)
    for gx in range(4):
        for gz in range(4):
            out_ref[gx, gz] = field[gx * 64 : (gx + 1) * 64, gz * 128 : (gz + 1) * 128]
    power = jnp.sum(lines_ref[pl.ds(1, 256, stride=2), :], axis=0, keepdims=True)
    energy_ref[...] = jnp.broadcast_to(power * energy_scale, (8, 128))


def inverse_xz(lines, along_x, along_z, energy_scale):
    return pl.pallas_call(
        functools.partial(inverse_kernel, energy_scale),
        in_specs=[VM] * 3,
        out_specs=[VM, VM],
        compiler_params=SMALL,
        out_shape=[
            jax.ShapeDtypeStruct((4, 4, 64, 128), bf16),
            jax.ShapeDtypeStruct((8, 128), f32),
        ],
        cost_estimate=pl.CostEstimate(
            flops=2 * 256 * 256 * 640, bytes_accessed=900000, transcendentals=0
        ),
        name="inverse_xz",
    )(lines, along_x, along_z)


def interpolate_kernel(field_scale, field_ref, place_ref, out_ref, own_ref):
    block = lax.broadcasted_iota(jnp.int32, (128, 128), 0) // PC

    def gather(cell, carry):
        ax, cz = cell // 6, cell % 6
        field = field_ref[:, pl.ds(pl.multiple_of(ax * PC, PC), PC), :].reshape(PC * PC, 128)
        place = place_ref[cell]
        row_x = spline_row(place[0:1])
        row_y = spline_row(place[1:2])
        row_z = spline_row(place[2:3])
        right = jnp.where(block == cz + 1, jnp.tile(row_z, (8, 1)), 0.0).astype(bf16)
        partial = dot(field, right)
        left = (row_y[:, None, :] * row_x[None, :, :]).reshape(PC * PC, 128)
        out_ref[pl.ds(cell, 1), :] = jnp.sum(partial * left, axis=0, keepdims=True) * field_scale
        return carry

    lax.fori_loop(0, 24, gather, 0)
    own_ref[0:4, :] = out_ref[7:11, :]
    own_ref[4:8, :] = out_ref[13:17, :]


def interpolate(field, place, field_scale):
    return pl.pallas_call(
        functools.partial(interpolate_kernel, field_scale),
        in_specs=[VM] * 2,
        out_specs=[VM, VM],
        compiler_params=SMALL,
        out_shape=[
            jax.ShapeDtypeStruct((24, 128), f32),
            jax.ShapeDtypeStruct((8, 128), f32),
        ],
        cost_estimate=pl.CostEstimate(
            flops=24 * 2 * 256 * 128 * 128, bytes_accessed=400000, transcendentals=0
        ),
        name="interpolate",
    )(field, place)


def combination_of(t):
    return jnp.where(t < 4, 1 + t // 2, 3 * (t - 4)), t % 2


def scaled(columns, cell, slope):
    return (columns[:, cell : cell + 1] * slope.astype(f32)).astype(bf16)


def beside_kernel(
    stored_ref, own_ref, below_ref, above_ref, left_ref, right_ref, before_ref, after_ref,
    potential_ref, weight_ref, slope_ref, total_ref, own_out, near_ref, sems
):
    inner_x, inner_z = pl.ds(1, 2), pl.ds(1, 4)
    pairs = [
        (own_ref, slope_ref.at[1, inner_x, inner_z]),
        (left_ref, slope_ref.at[:, inner_x, pl.ds(0, 1)]),
        (right_ref, slope_ref.at[:, inner_x, pl.ds(5, 1)]),
        (before_ref, slope_ref.at[:, pl.ds(0, 1)]),
        (after_ref, slope_ref.at[:, pl.ds(3, 1)]),
        (below_ref, slope_ref.at[0, inner_x, inner_z]),
        (above_ref, slope_ref.at[2, inner_x, inner_z]),
        (stored_ref.at[pl.ds(0, 3)], weight_ref.at[pl.ds(0, 3)]),
        (stored_ref.at[pl.ds(3, 3)], weight_ref.at[pl.ds(3, 3)]),
    ]
    copies = [
        pltpu.make_async_copy(source, target, sems.at[i])
        for i, (source, target) in enumerate(pairs)
    ]
    for copy in copies:
        copy.start()
    for copy in copies[:7]:
        copy.wait()
    columns = jnp.transpose(potential_ref[...])
    for x in range(4):
        for z in range(6):
            near_ref[x, z] = scaled(columns, x * 6 + z, slope_ref[1, x, z])
    own_out[...] = near_ref[1:3, 1:5]
    total_ref[...] = jnp.zeros_like(total_ref)
    for copy in copies[7:]:
        copy.wait()

    def combination(t, carry):
        x, a = combination_of(t)
        for pair, (start, stop, first, width) in enumerate(SPANS):
            part = dot(
                weight_ref[t, start:stop, :, 512:768].reshape(width * 128, 256),
                near_ref[x, 2 * pair : 2 * pair + 2].reshape(256, 128),
            )
            total_ref[a, first : first + width] += part.reshape(width, 128, 128)
        return carry

    lax.fori_loop(0, 6, combination, 0)


def beside(weights, own, near, ends, potential):
    return pl.pallas_call(
        beside_kernel,
        in_specs=[ANY] * 8 + [VM],
        out_specs=[VM] * 4,
        out_shape=[
            jax.ShapeDtypeStruct((6, 8, 128, 768), bf16),
            jax.ShapeDtypeStruct((3, 4, 6, 128, 128), bf16),
            jax.ShapeDtypeStruct((2, 4, 128, 128), f32),
            jax.ShapeDtypeStruct((2, 4, 128, 128), bf16),
        ],
        scratch_shapes=[
            pltpu.VMEM((4, 6, 128, 128), bf16),
            pltpu.SemaphoreType.DMA((9,)),
        ],
        cost_estimate=pl.CostEstimate(
            flops=3000000000, bytes_accessed=12000000, transcendentals=0
        ),
        compiler_params=MIDDLE,
        name="beside",
    )(weights, own, *near, *ends, potential)


def backward_kernel(
    weight_ref, slope_ref, part_ref, own_ref, below_ref, above_ref, msg_ref, self_ref, out_ref,
    near_ref, total_ref, potential_ref
):
    potential_ref[0] = below_ref[...]
    potential_ref[1] = above_ref[...]

    def scale(side, carry):
        columns = jnp.transpose(potential_ref[side])
        for x in range(4):
            for z in range(6):
                near_ref[side, x, z] = scaled(columns, x * 6 + z, slope_ref[2 * side, x, z])
        return carry

    lax.fori_loop(0, 2, scale, 0)
    total_ref[...] = part_ref[...]

    def combination(t, carry):
        x, a = combination_of(t)
        for pair, (start, stop, first, width) in enumerate(SPANS):
            near = jnp.concatenate(
                [
                    near_ref[side, x, 2 * pair : 2 * pair + 2].reshape(256, 128)
                    for side in range(2)
                ],
                axis=0,
            )
            part = dot(weight_ref[t, start:stop, :, 0:512].reshape(width * 128, 512), near)
            total_ref[a, first : first + width] += part.reshape(width, 128, 128)
        return carry

    lax.fori_loop(0, 6, combination, 0)

    def finish(a, carry):
        back = total_ref[a].reshape(512, 128).astype(bf16)
        own = own_ref[a].reshape(512, 128)
        out_ref[a] = (dot_t(back, msg_ref[...]) + dot_t(own, self_ref[...])).reshape(4, 128, 128)
        return carry

    lax.fori_loop(0, 2, finish, 0)


def backward(weights, slope, part, own, below, above, msg_weight, self_weight):
    return pl.pallas_call(
        backward_kernel,
        in_specs=[VM] * 8,
        out_specs=VM,
        out_shape=jax.ShapeDtypeStruct((2, 4, 128, 128), f32),
        scratch_shapes=[
            pltpu.VMEM((2, 4, 6, 128, 128), bf16),
            pltpu.VMEM((2, 4, 128, 128), f32),
            pltpu.VMEM((2, 24, 128), f32),
        ],
        cost_estimate=pl.CostEstimate(
            flops=4000000000, bytes_accessed=12000000, transcendentals=0
        ),
        compiler_params=SMALL,
        name="backward",
    )(weights, slope, part, own, below, above, msg_weight, self_weight)


def wave_tables(size_x, size_y, size_z):
    i16 = np.arange(16)
    along_z = np.zeros((4, 2, 64, 2, size_z))
    for g in range(4):
        table = cas(g * 64 + np.arange(64), np.arange(size_z), size_z)
        for a in range(2):
            along_z[g, a, :, a, :] = table
    points_x = np.array([g * 32 + a * 16 + i for a in range(2) for g in range(4) for i in i16])
    along_x = cas(np.arange(size_x), points_x, size_x)
    points_y = np.array(
        [gy * 16 + gx * 4 + gz for gx in range(4) for gy in range(16) for gz in range(4)]
    )
    into_y = cas(np.arange(size_y), points_y, size_y)
    back_x = np.array(
        [((2 * g - 1 + a) % 8) * 16 + i for g in range(4) for a in range(4) for i in i16]
    )
    back_z = np.array(
        [((4 * g - 2 + c) % 16) * 16 + k for g in range(4) for c in range(8) for k in i16]
    )
    tables = (
        along_z.reshape(4, 128, 2 * size_z),
        along_x,
        into_y,
        into_y.T,
        cas(back_x, np.arange(size_x), size_x),
        cas(np.arange(size_z), back_z, size_z),
    )
    return [jnp.asarray(np.ascontiguousarray(t), dtype=bf16) for t in tables]


def influence_of(size_x, size_y, size_z):
    device = lax.axis_index(everyone)

    def wave(index, size):
        signed = jnp.where(2 * index >= size, index - size, index)
        return signed.astype(f32) * (PC / size)

    wave_x = wave(device % size_x, size_x)
    wave_y = wave(jnp.arange(size_y, dtype=jnp.int32), size_y)[:, None]
    wave_z = wave(
        device // size_x * 128 + jnp.arange(size_z // 2, dtype=jnp.int32), size_z
    )[None, :]
    squared = wave_x * wave_x + wave_y * wave_y + wave_z * wave_z
    safe = jnp.where(squared > 0, squared, 1.0)
    return jnp.where(squared > 0, jnp.exp(-((math.pi * spread_width) ** 2) * squared) / safe, 0.0)


def swapped(value, axis):
    return lax.all_to_all(value, axis, split_axis=0, concat_axis=0, tiled=True)


def body(features, msg_weight, self_weight, charge_weight, spline_corner, spline_fraction):
    cells_x, cells_y, cells_z, slots, width = features.shape
    size_x = cells_x * PC * lax.axis_size("gx")
    size_y = cells_y * PC * lax.axis_size("gy")
    size_z = cells_z * PC * lax.axis_size("gz")
    volume = size_x // PC * (size_y // PC) * (size_z // PC)
    natoms = volume * slots
    cells = cells_x * cells_z

    features_own = features.reshape(cells, slots, width)
    own = project(
        features_own,
        msg_weight,
        spline_corner.reshape(cells, 3, slots),
        spline_fraction.reshape(cells, 3, slots),
    ).reshape(cells_x, cells_z, slots + 16, width)
    near = halo_yz(own)
    ends = halo_x(own, near)
    weights, part, place = inner_pairs(own, near, features_own, self_weight)
    influence = influence_of(size_x, size_y, size_z)
    along_z, along_x, into_y, from_y, back_x, back_z = wave_tables(size_x, size_y, size_z)

    weights, slope, mesh, row_place = message_layer(
        ends, part, place, charge_weight[None, :], weights
    )
    slope_near = halo_yz(slope)
    slope_ends = halo_x(slope, slope_near)

    mesh = swapped(mesh, plane).reshape(4, 4, PC, 128)
    lines = swapped(forward_xz(mesh, along_z, along_x), everyone)
    lines = swapped(filter_y(lines, into_y, from_y, influence), everyone)
    field, energy = inverse_xz(lines, back_x, back_z, coupling / (2.0 * volume * natoms))
    field = swapped(field.reshape(16, 64, 128), plane)
    potential, atom_potential = interpolate(field, row_place.reshape(24, 8, slots), coupling / volume)
    below, above = moved(potential, "gy", 1), moved(potential, "gy", -1)
    weights, slopes, total, cotangent = beside(
        weights, slope, slope_near, slope_ends, potential
    )
    grad = backward(weights, slopes, total, cotangent, below, above, msg_weight, self_weight)
    return (
        grad.reshape(features.shape),
        atom_potential.reshape(cells_x, cells_y, cells_z, slots),
        energy[0, 0],
    )


def solution(mesh):
    in_specs = (
        P("gx", "gy", "gz", None, None),
        P(),
        P(),
        P(),
        P("gx", "gy", "gz", None, None),
        P("gx", "gy", "gz", None, None),
    )
    out_specs = (P("gx", "gy", "gz", None, None), P("gx", "gy", "gz", None), P())
    return jax.shard_map(body, mesh=mesh, in_specs=in_specs, out_specs=out_specs, check_vma=False)
```

```python
import functools
import math

import jax
import jax.numpy as jnp
import numpy as np
from jax import lax
from jax.experimental import pallas as pl
from jax.experimental.pallas import tpu as pltpu
from jax.sharding import PartitionSpec as P

PC = 16
pair_scale = 0.1
coupling = 0.125
spread_width = 0.0625
f32 = jnp.float32
bf16 = jnp.bfloat16
plane = ("gx", "gz")
everyone = ("gx", "gy", "gz")


def dot(a, b):
    return jnp.dot(a, b, preferred_element_type=f32)


def dot_t(a, b, precision=None):
    return lax.dot_general(
        a, b, (((1,), (1,)), ((), ())), preferred_element_type=f32, precision=precision
    )


def whole(shape):
    zeros = (0,) * len(shape)
    return pl.BlockSpec(shape, lambda *_: zeros)


VM = pl.BlockSpec(memory_space=pltpu.VMEM)
ANY = pl.BlockSpec(memory_space=pl.ANY)
SMALL = pltpu.CompilerParams(vmem_limit_bytes=20 << 20)
LARGE = pltpu.CompilerParams(vmem_limit_bytes=50 << 20)
MIDDLE = pltpu.CompilerParams(vmem_limit_bytes=36 << 20)


def cas(rows, columns, size):
    turns = np.outer(rows, columns) % size
    angle = 2.0 * np.pi / size * turns
    return np.cos(angle) + np.sin(angle)


def moved(value, axis, step):
    count = lax.axis_size(axis)
    pairs = [(i, (i + step) % count) for i in range(count)]
    return lax.ppermute(value.reshape(-1, 128), axis, pairs).reshape(value.shape)


def late_halo(own):
    last_x, last_z = own.shape[0] - 1, own.shape[1] - 1
    left, right = moved(own[:, last_z:], "gz", 1), moved(own[:, :1], "gz", -1)
    row = jnp.concatenate([left, own, right], axis=1)
    rows = jnp.stack([moved(row, "gy", 1), row, moved(row, "gy", -1)])
    return [rows, moved(rows[:, last_x:], "gx", 1), moved(rows[:, :1], "gx", -1)]


def early_halo(own):
    last_x, last_z = own.shape[0] - 1, own.shape[1] - 1
    below, above = moved(own, "gy", 1), moved(own, "gy", -1)
    beside = [moved(own[last_x:], "gx", 1), moved(own[:1], "gx", -1)]
    sides = jnp.stack([below, above])
    rows = [below, own, above]
    left = moved(jnp.stack([row[:, last_z:] for row in rows]), "gz", 1)
    right = moved(jnp.stack([row[:, :1] for row in rows]), "gz", -1)
    aside = [moved(sides[:, last_x:], "gx", 1), moved(sides[:, :1], "gx", -1)]
    corners = [
        moved(jnp.concatenate([left[:, at : at + 1], right[:, at : at + 1]], axis=2), "gx", step)
        for at, step in ((last_x, 1), (0, -1))
    ]
    return [below, above, left, right], beside + aside + corners


def project_kernel(features_ref, weight_ref, corner_ref, fraction_ref, out_ref):
    value = dot(features_ref[...].reshape(1024, 128), weight_ref[...]).astype(bf16)
    out_ref[:, :128, :] = value.reshape(8, 128, 128)
    place = corner_ref[:, 0].astype(f32) + 1.0 + fraction_ref[:, 0]
    place = place.reshape(8, 3, 128)
    high = place.astype(bf16).astype(f32)
    rest = place - high
    middle = rest.astype(bf16).astype(f32)
    low = rest - middle
    two = jnp.zeros((8, 2, 128), f32)
    five = jnp.zeros((8, 5, 128), f32)
    out_ref[:, 128:, :] = jnp.concatenate([high, low, two, middle, five], axis=1).astype(bf16)


def project(features, weight, corner, fraction):
    return pl.pallas_call(
        project_kernel,
        grid=(1,),
        in_specs=[whole((8, 128, 128)), whole((128, 128))]
        + [whole((2, 1, 4, 3, 128))] * 2,
        out_specs=whole((8, 144, 128)),
        out_shape=jax.ShapeDtypeStruct((8, 144, 128), bf16),
        compiler_params=SMALL,
        name="project",
    )(features, weight, corner, fraction)


def place_of(rows):
    rows = rows.astype(f32)
    return rows[0:8] + rows[8:16] + pltpu.roll(rows[0:8], 5, 0)


BLOCKS = ((0, 0), (0, 1), (1, 0), (1, 1), (1, 2), (1, 3), (2, 2), (2, 3))
SPANS = ((0, 2, 0, 2), (2, 6, 0, 4), (6, 8, 2, 2))
ORDER_Y = (0, 2, 1)


def weigh(centres, a, shift, near, store):
    for c in range(4):
        columns = jnp.transpose(centres[a, c])
        centre_x = jnp.broadcast_to(columns[:, 0:1], (128, 128))
        centre_y = jnp.broadcast_to(columns[:, 1:2], (128, 128))
        centre_z = jnp.broadcast_to(columns[:, 2:3], (128, 128))
        for block, (pair, owner) in enumerate(BLOCKS):
            if owner != c:
                continue
            for at, dy in enumerate(ORDER_Y):
                for half in range(2):
                    dz = 2 * pair + half - c - 1
                    if abs(dz) > 1:
                        tile = jnp.zeros((128, 128), bf16)
                    else:
                        row = near(dy, 2 * pair + half)
                        gap_x = (row[0:1] + shift) - centre_x
                        gap_y = (row[1:2] + (dy - 1.0)) - centre_y
                        gap_z = (row[2:3] + float(dz)) - centre_z
                        squared = gap_x * gap_x + gap_y * gap_y + gap_z * gap_z
                        inside = jnp.maximum(1.0 - squared, 0.0)
                        tile = (pair_scale * inside * inside).astype(bf16)
                    store(block, (at * 2 + half) * 128, tile)


def inner_kernel(
    own_ref, below_ref, above_ref, left_ref, right_ref, features_ref, self_ref,
    weight_out, total_ref, place_ref, weight_ref, position_ref, sems
):
    refs = (below_ref, own_ref, above_ref)

    def cell(dy, x, z):
        if z == 0:
            return left_ref.at[dy, x, 0]
        if z == 5:
            return right_ref.at[dy, x, 0]
        return refs[dy].at[x, z - 1]

    def places(x, carry):
        for dy in range(3):
            for z in range(6):
                place = place_of(cell(dy, x, z)[128:144, :])
                place_ref[dy, x, z] = place
                position_ref[dy, x, z] = (place * (1.0 / PC)).astype(bf16).astype(f32)
        return carry

    lax.fori_loop(0, 2, places, 0)

    def copy_out(t):
        return pltpu.make_async_copy(weight_ref.at[t], weight_out.at[t], sems.at[t])

    total_ref[...] = dot(features_ref[...].reshape(1024, 128), self_ref[...]).reshape(
        2, 4, 128, 128
    )

    def combination(t, carry):
        x, a = t // 2, t % 2

        def store(block, lane, tile):
            weight_ref[t, block, :, lane : lane + 128] = tile

        weigh(
            position_ref.at[1, :, 1:5],
            a,
            (x - a).astype(f32),
            lambda dy, z: position_ref[dy, x, z],
            store,
        )
        copy_out(t).start()
        for pair, (start, stop, first, width) in enumerate(SPANS):
            near = jnp.concatenate(
                [
                    cell(dy, x, 2 * pair + half)[0:128, :]
                    for dy in ORDER_Y
                    for half in range(2)
                ],
                axis=0,
            )
            part = dot(weight_ref[t, start:stop].reshape(width * 128, 768), near)
            total_ref[a, first : first + width] += part.reshape(width, 128, 128)
        return carry

    lax.fori_loop(0, 4, combination, 0)
    for t in range(4):
        copy_out(t).wait()


def inner_pairs(own, near, features, self_weight):
    return pl.pallas_call(
        inner_kernel,
        in_specs=[VM] * 7,
        out_specs=[ANY, VM, VM],
        out_shape=[
            jax.ShapeDtypeStruct((6, 8, 128, 768), bf16),
            jax.ShapeDtypeStruct((2, 4, 128, 128), f32),
            jax.ShapeDtypeStruct((3, 2, 6, 8, 128), f32),
        ],
        scratch_shapes=[
            pltpu.VMEM((4, 8, 128, 768), bf16),
            pltpu.VMEM((3, 2, 6, 8, 128), f32),
            pltpu.SemaphoreType.DMA((4,)),
        ],
        cost_estimate=pl.CostEstimate(
            flops=9000000000, bytes_accessed=9000000, transcendentals=0
        ),
        compiler_params=LARGE,
        name="inner_pairs",
    )(own, *near, features, self_weight)


def spline_row(place):
    point = lax.broadcasted_iota(jnp.int32, (PC, 128), 0).astype(f32)
    away = jnp.abs(point - place)
    near = (4.0 - 6.0 * away * away + 3.0 * away * away * away) * (1.0 / 6.0)
    rest = 2.0 - away
    far = rest * rest * rest * (1.0 / 6.0)
    return jnp.where(away < 1.0, near, jnp.where(away < 2.0, far, 0.0))


def message_kernel(
    before_own, after_own, before_side, after_side, before_end, after_end,
    part_ref, place_ref, read_ref, _,
    weight_out, total_ref, mesh_ref, row_place_ref,
    weight_ref, position_ref, centre_ref, high_ref, low_ref, charge_ref, left_ref,
    right_ref, sems
):
    refs = ((before_own, before_side, before_end), (after_own, after_side, after_end))

    def cell(side, dy, z):
        own, beside, end = refs[side]
        if z in (0, 5):
            return end.at[dy, 0, z // 5]
        return own.at[0, z - 1] if dy == 1 else beside.at[dy // 2, 0, z - 1]

    def position(place):
        return (place * (1.0 / PC)).astype(bf16).astype(f32)

    for side in range(2):
        for dy in range(3):
            for z in range(6):
                place = place_of(cell(side, dy, z)[128:144, :])
                position_ref[side, dy, z] = position(place)
                if dy == 1:
                    row_place_ref[3 * side, z] = place
    for x in range(2):
        for z in range(6):
            place = place_ref[1, x, z]
            row_place_ref[1 + x, z] = place
            if 1 <= z <= 4:
                centre_ref[x, z - 1] = position(place)

    def copy_out(t):
        return pltpu.make_async_copy(weight_ref.at[t], weight_out.at[4 + t], sems.at[t])

    def combination(t, carry):
        def store(block, lane, tile):
            weight_ref[t, block, :, lane : lane + 128] = tile

        weigh(
            centre_ref,
            t,
            (2 * t - 1).astype(f32),
            lambda dy, z: position_ref[t, dy, z],
            store,
        )
        copy_out(t).start()
        return carry

    lax.fori_loop(0, 2, combination, 0)
    total_ref[...] = part_ref[...]
    for t in range(2):
        for pair, (start, stop, first, width) in enumerate(SPANS):
            near = jnp.concatenate(
                [
                    cell(t, dy, 2 * pair + half)[0:128, :]
                    for dy in ORDER_Y
                    for half in range(2)
                ],
                axis=0,
            )
            part = dot(weight_ref[t, start:stop].reshape(width * 128, 768), near)
            total_ref[t, first : first + width] += part.reshape(width, 128, 128)

    def finish(index, carry):
        preact = total_ref[index // 4, index % 4]
        silu = preact * (0.5 + 0.5 * jnp.tanh(0.5 * preact))
        high = silu.astype(bf16)
        high_ref[index] = high
        low_ref[index] = (silu - high.astype(f32)).astype(bf16)
        return carry

    lax.fori_loop(0, 8, finish, 0, unroll=2)
    wide = jnp.broadcast_to(read_ref[...], (16, 128))
    charge_ref[...] = dot_t(wide, high_ref[...].reshape(1024, 128)) + dot_t(
        wide, low_ref[...].reshape(1024, 128)
    )
    block = lax.broadcasted_iota(jnp.int32, (128, 128), 0) // PC

    def spread(cell, carry):
        lanes = pl.ds(pl.multiple_of(cell * 128, 128), 128)
        place = place_ref[1, cell // 4, cell % 4 + 1]
        row_x = spline_row(place[0:1])
        row_y = spline_row(place[1:2]) * charge_ref[0:1, lanes]
        row_z = spline_row(place[2:3])
        left_ref[:, lanes] = (
            (row_y[:, None, :] * row_x[None, :, :]).reshape(PC * PC, 128).astype(bf16)
        )
        right_ref[:, lanes] = jnp.where(block == cell, jnp.tile(row_z, (8, 1)), 0.0).astype(bf16)
        return carry

    lax.fori_loop(0, 8, spread, 0)
    mesh_ref[...] = dot_t(left_ref[...], right_ref[...]).reshape(PC, PC, 128).astype(bf16)
    for t in range(2):
        copy_out(t).wait()


def message_layer(ends, part, place, read, weights):
    return pl.pallas_call(
        message_kernel,
        in_specs=[VM] * 9 + [ANY],
        out_specs=[ANY, VM, VM, VM],
        input_output_aliases={9: 0},
        out_shape=[
            jax.ShapeDtypeStruct((6, 8, 128, 768), bf16),
            jax.ShapeDtypeStruct((2, 4, 128, 128), f32),
            jax.ShapeDtypeStruct((PC, PC, 128), bf16),
            jax.ShapeDtypeStruct((4, 6, 8, 128), f32),
        ],
        scratch_shapes=[
            pltpu.VMEM((2, 8, 128, 768), bf16),
            pltpu.VMEM((2, 3, 6, 8, 128), f32),
            pltpu.VMEM((2, 4, 8, 128), f32),
            pltpu.VMEM((8, 128, 128), bf16),
            pltpu.VMEM((8, 128, 128), bf16),
            pltpu.VMEM((16, 1024), f32),
            pltpu.VMEM((PC * PC, 1024), bf16),
            pltpu.VMEM((128, 1024), bf16),
            pltpu.SemaphoreType.DMA((2,)),
        ],
        cost_estimate=pl.CostEstimate(
            flops=5000000000, bytes_accessed=6000000, transcendentals=8 * 16384
        ),
        compiler_params=LARGE,
        name="message",
    )(*ends, part, place, read, weights)


def slope_kernel(total_ref, read_ref, out_ref):
    read = read_ref[...].astype(f32)

    def one(index, carry):
        a, c = index // 4, index % 4
        preact = total_ref[a, c]
        sigma = 0.5 + 0.5 * jnp.tanh(0.5 * preact)
        out_ref[a, c] = (read * (sigma * (1.0 + preact * (1.0 - sigma)))).astype(bf16)
        return carry

    lax.fori_loop(0, 8, one, 0, unroll=2)


def slope_of(total, read):
    return pl.pallas_call(
        slope_kernel,
        in_specs=[VM] * 2,
        out_specs=VM,
        out_shape=jax.ShapeDtypeStruct(total.shape, bf16),
        cost_estimate=pl.CostEstimate(
            flops=8 * 16384 * 8, bytes_accessed=900000, transcendentals=8 * 16384
        ),
        compiler_params=SMALL,
        name="slope",
    )(total, read)


def forward_kernel(mesh_ref, along_z_ref, along_x_ref, out_ref):
    total = jnp.zeros((64, 512), f32)
    for g in range(4):
        total = total + dot(mesh_ref[:, g].reshape(64, 128), along_z_ref[g])
    lines = jnp.concatenate([total[:, :256], total[:, 256:]], axis=0).astype(bf16)
    waves = dot(along_x_ref[...], lines)
    out_ref[0:128, :] = waves[:, :128]
    out_ref[128:256, :] = waves[:, 128:]


def forward_xz(mesh, along_z, along_x):
    return pl.pallas_call(
        forward_kernel,
        in_specs=[VM] * 3,
        out_specs=VM,
        compiler_params=SMALL,
        out_shape=jax.ShapeDtypeStruct((256, 128), f32),
        cost_estimate=pl.CostEstimate(
            flops=2 * 64 * 512 * 512, bytes_accessed=800000, transcendentals=0
        ),
        name="forward_xz",
    )(mesh, along_z, along_x)


def filter_kernel(lines_ref, into_ref, back_ref, influence_ref, out_ref):
    waves = dot(into_ref[...], lines_ref[...].astype(bf16))
    scaled = influence_ref[...] * waves
    power = jnp.sum(jnp.sum(scaled * waves, axis=0, keepdims=True), axis=1, keepdims=True)
    out_ref[pl.ds(0, 256, stride=2), :] = dot(back_ref[...], scaled.astype(bf16))
    out_ref[pl.ds(1, 256, stride=2), :] = jnp.broadcast_to(power, (256, 128))


def filter_y(lines, into, back, influence):
    return pl.pallas_call(
        filter_kernel,
        in_specs=[VM] * 4,
        out_specs=VM,
        compiler_params=SMALL,
        out_shape=jax.ShapeDtypeStruct((512, 128), f32),
        cost_estimate=pl.CostEstimate(
            flops=4 * 256 * 256 * 128, bytes_accessed=700000, transcendentals=0
        ),
        name="filter_y",
    )(lines, into, back, influence)


def inverse_kernel(energy_scale, lines_ref, along_x_ref, along_z_ref, out_ref, energy_ref):
    waves = jnp.concatenate(
        [lines_ref[pl.ds(0, 128, stride=2), :], lines_ref[pl.ds(256, 128, stride=2), :]], axis=1
    ).astype(bf16)
    half = dot(along_x_ref[...], waves).astype(bf16)
    field = dot(half, along_z_ref[...]).astype(bf16)
    for gx in range(4):
        for gz in range(4):
            out_ref[gx, gz] = field[gx * 64 : (gx + 1) * 64, gz * 128 : (gz + 1) * 128]
    power = jnp.sum(lines_ref[pl.ds(1, 256, stride=2), :], axis=0, keepdims=True)
    energy_ref[...] = jnp.broadcast_to(power * energy_scale, (8, 128))


def inverse_xz(lines, along_x, along_z, energy_scale):
    return pl.pallas_call(
        functools.partial(inverse_kernel, energy_scale),
        in_specs=[VM] * 3,
        out_specs=[VM, VM],
        compiler_params=SMALL,
        out_shape=[
            jax.ShapeDtypeStruct((4, 4, 64, 128), bf16),
            jax.ShapeDtypeStruct((8, 128), f32),
        ],
        cost_estimate=pl.CostEstimate(
            flops=2 * 256 * 256 * 640, bytes_accessed=900000, transcendentals=0
        ),
        name="inverse_xz",
    )(lines, along_x, along_z)


def interpolate_kernel(field_scale, field_ref, place_ref, out_ref, own_ref):
    block = lax.broadcasted_iota(jnp.int32, (128, 128), 0) // PC

    def gather(step, carry):
        ax, half = step // 2, 3 * (step % 2)
        field = field_ref[:, pl.ds(pl.multiple_of(ax * PC, PC), PC), :].reshape(PC * PC, 128)
        for third in range(3):
            cz = half + third
            place = place_ref[ax * 6 + cz]
            row_x = spline_row(place[0:1])
            row_y = spline_row(place[1:2])
            row_z = spline_row(place[2:3])
            right = jnp.where(block == cz + 1, jnp.tile(row_z, (8, 1)), 0.0).astype(bf16)
            partial = dot(field, right)
            left = (row_y[:, None, :] * row_x[None, :, :]).reshape(PC * PC, 128)
            out_ref[pl.ds(ax * 6 + cz, 1), :] = (
                jnp.sum(partial * left, axis=0, keepdims=True) * field_scale
            )
        return carry

    lax.fori_loop(0, 8, gather, 0)
    own_ref[0:4, :] = out_ref[7:11, :]
    own_ref[4:8, :] = out_ref[13:17, :]


def interpolate(field, place, field_scale):
    return pl.pallas_call(
        functools.partial(interpolate_kernel, field_scale),
        in_specs=[VM] * 2,
        out_specs=[VM, VM],
        compiler_params=SMALL,
        out_shape=[
            jax.ShapeDtypeStruct((24, 128), f32),
            jax.ShapeDtypeStruct((8, 128), f32),
        ],
        cost_estimate=pl.CostEstimate(
            flops=24 * 2 * 256 * 128 * 128, bytes_accessed=400000, transcendentals=0
        ),
        name="interpolate",
    )(field, place)


def combination_of(t):
    return jnp.where(t < 4, 1 + t // 2, 3 * (t - 4)), t % 2


def scaled(columns, cell, slope):
    return (columns[:, cell : cell + 1] * slope.astype(f32)).astype(bf16)


def beside_kernel(
    stored_ref, rows_ref, before_ref, after_ref, potential_ref,
    weight_ref, slope_ref, total_ref, own_out, near_ref, sems
):
    pairs = [
        (rows_ref, slope_ref.at[:, pl.ds(1, 2)]),
        (before_ref, slope_ref.at[:, pl.ds(0, 1)]),
        (after_ref, slope_ref.at[:, pl.ds(3, 1)]),
        (stored_ref.at[pl.ds(0, 3)], weight_ref.at[pl.ds(0, 3)]),
        (stored_ref.at[pl.ds(3, 3)], weight_ref.at[pl.ds(3, 3)]),
    ]
    copies = [
        pltpu.make_async_copy(source, target, sems.at[i])
        for i, (source, target) in enumerate(pairs)
    ]
    for copy in copies:
        copy.start()
    for copy in copies[:3]:
        copy.wait()
    columns = jnp.transpose(potential_ref[...])
    for x in range(4):
        for z in range(6):
            near_ref[x, z] = scaled(columns, x * 6 + z, slope_ref[1, x, z])
    own_out[...] = near_ref[1:3, 1:5]
    total_ref[...] = jnp.zeros_like(total_ref)
    for copy in copies[3:]:
        copy.wait()

    def combination(t, carry):
        x, a = combination_of(t)
        for pair, (start, stop, first, width) in enumerate(SPANS):
            part = dot(
                weight_ref[t, start:stop, :, 512:768].reshape(width * 128, 256),
                near_ref[x, 2 * pair : 2 * pair + 2].reshape(256, 128),
            )
            total_ref[a, first : first + width] += part.reshape(width, 128, 128)
        return carry

    lax.fori_loop(0, 6, combination, 0)


def beside(weights, slopes, potential):
    return pl.pallas_call(
        beside_kernel,
        in_specs=[ANY] * 4 + [VM],
        out_specs=[VM] * 4,
        out_shape=[
            jax.ShapeDtypeStruct((6, 8, 128, 768), bf16),
            jax.ShapeDtypeStruct((3, 4, 6, 128, 128), bf16),
            jax.ShapeDtypeStruct((2, 4, 128, 128), f32),
            jax.ShapeDtypeStruct((2, 4, 128, 128), bf16),
        ],
        scratch_shapes=[
            pltpu.VMEM((4, 6, 128, 128), bf16),
            pltpu.SemaphoreType.DMA((5,)),
        ],
        cost_estimate=pl.CostEstimate(
            flops=3000000000, bytes_accessed=12000000, transcendentals=0
        ),
        compiler_params=MIDDLE,
        name="beside",
    )(weights, *slopes, potential)


def backward_kernel(
    weight_ref, slope_ref, part_ref, own_ref, below_ref, above_ref, msg_ref, self_ref, out_ref,
    near_ref, total_ref, potential_ref
):
    potential_ref[0] = below_ref[...]
    potential_ref[1] = above_ref[...]

    def scale(side, carry):
        columns = jnp.transpose(potential_ref[side])
        for x in range(4):
            for z in range(6):
                near_ref[side, x, z] = scaled(columns, x * 6 + z, slope_ref[2 * side, x, z])
        return carry

    lax.fori_loop(0, 2, scale, 0)
    total_ref[...] = part_ref[...]

    def combination(t, carry):
        x, a = combination_of(t)
        for pair, (start, stop, first, width) in enumerate(SPANS):
            near = jnp.concatenate(
                [
                    near_ref[side, x, 2 * pair : 2 * pair + 2].reshape(256, 128)
                    for side in range(2)
                ],
                axis=0,
            )
            part = dot(weight_ref[t, start:stop, :, 0:512].reshape(width * 128, 512), near)
            total_ref[a, first : first + width] += part.reshape(width, 128, 128)
        return carry

    lax.fori_loop(0, 6, combination, 0)

    def finish(a, carry):
        back = total_ref[a].reshape(512, 128).astype(bf16)
        own = own_ref[a].reshape(512, 128)
        out_ref[a] = (dot_t(back, msg_ref[...]) + dot_t(own, self_ref[...])).reshape(4, 128, 128)
        return carry

    lax.fori_loop(0, 2, finish, 0)


def backward(weights, slope, part, own, below, above, msg_weight, self_weight):
    return pl.pallas_call(
        backward_kernel,
        in_specs=[VM] * 8,
        out_specs=VM,
        out_shape=jax.ShapeDtypeStruct((2, 4, 128, 128), f32),
        scratch_shapes=[
            pltpu.VMEM((2, 4, 6, 128, 128), bf16),
            pltpu.VMEM((2, 4, 128, 128), f32),
            pltpu.VMEM((2, 24, 128), f32),
        ],
        cost_estimate=pl.CostEstimate(
            flops=4000000000, bytes_accessed=12000000, transcendentals=0
        ),
        compiler_params=SMALL,
        name="backward",
    )(weights, slope, part, own, below, above, msg_weight, self_weight)


def wave_tables(size_x, size_y, size_z):
    i16 = np.arange(16)
    along_z = np.zeros((4, 2, 64, 2, size_z))
    for g in range(4):
        table = cas(g * 64 + np.arange(64), np.arange(size_z), size_z)
        for a in range(2):
            along_z[g, a, :, a, :] = table
    points_x = np.array([g * 32 + a * 16 + i for a in range(2) for g in range(4) for i in i16])
    along_x = cas(np.arange(size_x), points_x, size_x)
    points_y = np.array(
        [gy * 16 + gx * 4 + gz for gx in range(4) for gy in range(16) for gz in range(4)]
    )
    into_y = cas(np.arange(size_y), points_y, size_y)
    back_x = np.array(
        [((2 * g - 1 + a) % 8) * 16 + i for g in range(4) for a in range(4) for i in i16]
    )
    back_z = np.array(
        [((4 * g - 2 + c) % 16) * 16 + k for g in range(4) for c in range(8) for k in i16]
    )
    tables = (
        along_z.reshape(4, 128, 2 * size_z),
        along_x,
        into_y,
        into_y.T,
        cas(back_x, np.arange(size_x), size_x),
        cas(np.arange(size_z), back_z, size_z),
    )
    return [jnp.asarray(np.ascontiguousarray(t), dtype=bf16) for t in tables]


def influence_of(size_x, size_y, size_z):
    device = lax.axis_index(everyone)

    def wave(index, size):
        signed = jnp.where(2 * index >= size, index - size, index)
        return signed.astype(f32) * (PC / size)

    wave_x = wave(device % size_x, size_x)
    wave_y = wave(jnp.arange(size_y, dtype=jnp.int32), size_y)[:, None]
    wave_z = wave(
        device // size_x * 128 + jnp.arange(size_z // 2, dtype=jnp.int32), size_z
    )[None, :]
    squared = wave_x * wave_x + wave_y * wave_y + wave_z * wave_z
    safe = jnp.where(squared > 0, squared, 1.0)
    return jnp.where(squared > 0, jnp.exp(-((math.pi * spread_width) ** 2) * squared) / safe, 0.0)


def swapped(value, axis):
    return lax.all_to_all(value, axis, split_axis=0, concat_axis=0, tiled=True)


def body(features, msg_weight, self_weight, charge_weight, spline_corner, spline_fraction):
    cells_x, cells_y, cells_z, slots, width = features.shape
    size_x = cells_x * PC * lax.axis_size("gx")
    size_y = cells_y * PC * lax.axis_size("gy")
    size_z = cells_z * PC * lax.axis_size("gz")
    volume = size_x // PC * (size_y // PC) * (size_z // PC)
    natoms = volume * slots
    cells = cells_x * cells_z

    features_own = features.reshape(cells, slots, width)
    own = project(features_own, msg_weight, spline_corner, spline_fraction)
    own = own.reshape(cells_x, cells_z, slots + 16, width)
    near, ends = early_halo(own)
    weights, part, place = inner_pairs(own, near, features_own, self_weight)
    influence = influence_of(size_x, size_y, size_z)
    along_z, along_x, into_y, from_y, back_x, back_z = wave_tables(size_x, size_y, size_z)

    read = charge_weight[None, :]
    weights, preact, mesh, row_place = message_layer(ends, part, place, read, weights)
    slope = slope_of(preact, read)
    slope_near = late_halo(slope)

    mesh = swapped(mesh, plane).reshape(4, 4, PC, 128)
    lines = swapped(forward_xz(mesh, along_z, along_x), everyone)
    lines = swapped(filter_y(lines, into_y, from_y, influence), everyone)
    field, energy = inverse_xz(lines, back_x, back_z, coupling / (2.0 * volume * natoms))
    field = swapped(field.reshape(16, 64, 128), plane)
    potential, atom_potential = interpolate(field, row_place.reshape(24, 8, slots), coupling / volume)
    below, above = moved(potential, "gy", 1), moved(potential, "gy", -1)
    weights, slopes, total, cotangent = beside(
        weights, slope_near, potential
    )
    grad = backward(weights, slopes, total, cotangent, below, above, msg_weight, self_weight)
    return (
        grad.reshape(features.shape),
        atom_potential.reshape(cells_x, cells_y, cells_z, slots),
        energy[0, 0],
    )


def solution(mesh):
    in_specs = (
        P("gx", "gy", "gz", None, None),
        P(),
        P(),
        P(),
        P("gx", "gy", "gz", None, None),
        P("gx", "gy", "gz", None, None),
    )
    out_specs = (P("gx", "gy", "gz", None, None), P("gx", "gy", "gz", None), P())
    return jax.shard_map(body, mesh=mesh, in_specs=in_specs, out_specs=out_specs, check_vma=False)
```

```python
import functools
import math

import jax
import jax.numpy as jnp
import numpy as np
from jax import lax
from jax.experimental import pallas as pl
from jax.experimental.pallas import tpu as pltpu
from jax.sharding import PartitionSpec as P

PC = 16
pair_scale = 0.1
coupling = 0.125
spread_width = 0.0625
f32 = jnp.float32
bf16 = jnp.bfloat16
plane = ("gx", "gz")
everyone = ("gx", "gy", "gz")


def dot(a, b):
    return jnp.dot(a, b, preferred_element_type=f32)


def dot_t(a, b, precision=None):
    return lax.dot_general(
        a, b, (((1,), (1,)), ((), ())), preferred_element_type=f32, precision=precision
    )


def whole(shape):
    zeros = (0,) * len(shape)
    return pl.BlockSpec(shape, lambda *_: zeros)


VM = pl.BlockSpec(memory_space=pltpu.VMEM)
ANY = pl.BlockSpec(memory_space=pl.ANY)
SMALL = pltpu.CompilerParams(vmem_limit_bytes=20 << 20)
FIRST = pltpu.CompilerParams(vmem_limit_bytes=60 << 20)
LARGE = pltpu.CompilerParams(vmem_limit_bytes=50 << 20)
MIDDLE = pltpu.CompilerParams(vmem_limit_bytes=36 << 20)


def cas(rows, columns, size):
    turns = np.outer(rows, columns) % size
    angle = 2.0 * np.pi / size * turns
    return np.cos(angle) + np.sin(angle)


def moved(value, axis, step):
    count = lax.axis_size(axis)
    pairs = [(i, (i + step) % count) for i in range(count)]
    return lax.ppermute(value.reshape(-1, 128), axis, pairs).reshape(value.shape)


def late_halo(own):
    last_x, last_z = own.shape[0] - 1, own.shape[1] - 1
    left, right = moved(own[:, last_z:], "gz", 1), moved(own[:, :1], "gz", -1)
    row = jnp.concatenate([left, own, right], axis=1)
    rows = jnp.stack([moved(row, "gy", 1), row, moved(row, "gy", -1)])
    return [rows, moved(rows[:, last_x:], "gx", 1), moved(rows[:, :1], "gx", -1)]


def early_halo(own):
    last_x, last_z = own.shape[0] - 1, own.shape[1] - 1
    below, above = moved(own, "gy", 1), moved(own, "gy", -1)
    beside = [moved(own[last_x:], "gx", 1), moved(own[:1], "gx", -1)]
    sides = jnp.stack([below, above])
    rows = [below, own, above]
    left = moved(jnp.stack([row[:, last_z:] for row in rows]), "gz", 1)
    right = moved(jnp.stack([row[:, :1] for row in rows]), "gz", -1)
    aside = [moved(sides[:, last_x:], "gx", 1), moved(sides[:, :1], "gx", -1)]
    corners = [
        moved(jnp.concatenate([left[:, at : at + 1], right[:, at : at + 1]], axis=2), "gx", step)
        for at, step in ((last_x, 1), (0, -1))
    ]
    return [below, above], [left, right], beside + aside, corners


def project_kernel(features_ref, weight_ref, corner_ref, fraction_ref, out_ref):
    value = dot(features_ref[...].reshape(1024, 128), weight_ref[...]).astype(bf16)
    out_ref[:, :128, :] = value.reshape(8, 128, 128)
    none = jnp.zeros((5, 128), f32)
    for x in range(2):
        place = corner_ref[x, 0].astype(f32) + 1.0 + fraction_ref[x, 0]
        high = place.astype(bf16).astype(f32)
        rest = place - high
        middle = rest.astype(bf16).astype(f32)
        low = rest - middle
        for z in range(4):
            rows = [part[d, z : z + 1] for part in (high, low) for d in range(3)]
            rows += [none[:2]] + [middle[d, z : z + 1] for d in range(3)] + [none]
            out_ref[x * 4 + z, 128:, :] = jnp.concatenate(rows, axis=0).astype(bf16)


def project(features, weight, corner, fraction):
    return pl.pallas_call(
        project_kernel,
        grid=(1,),
        in_specs=[whole((8, 128, 128)), whole((128, 128))]
        + [whole((2, 1, 3, 4, 128))] * 2,
        out_specs=whole((8, 144, 128)),
        out_shape=jax.ShapeDtypeStruct((8, 144, 128), bf16),
        compiler_params=FIRST,
        name="project",
    )(features, weight, corner, fraction)


def place_of(rows):
    rows = rows.astype(f32)
    return rows[0:8] + rows[8:16] + pltpu.roll(rows[0:8], 5, 0)


BLOCKS = ((0, 0), (0, 1), (1, 0), (1, 1), (1, 2), (1, 3), (2, 2), (2, 3))
SPANS = ((0, 2, 0, 2), (2, 6, 0, 4), (6, 8, 2, 2))
ORDER_Y = (0, 2, 1)


def position_of(rows):
    return (place_of(rows) * (1.0 / PC)).astype(bf16).astype(f32)


def weigh(centres, a, shift, near, store, pairs):
    for c in range(4):
        columns = jnp.transpose(centres[a, c])
        centre_x = jnp.broadcast_to(columns[:, 0:1], (128, 128))
        centre_y = jnp.broadcast_to(columns[:, 1:2], (128, 128))
        centre_z = jnp.broadcast_to(columns[:, 2:3], (128, 128))
        for block, (pair, owner) in enumerate(BLOCKS):
            if owner != c or pair not in pairs:
                continue
            for at, dy in enumerate(ORDER_Y):
                for half in range(2):
                    dz = 2 * pair + half - c - 1
                    if abs(dz) > 1:
                        tile = jnp.zeros((128, 128), bf16)
                    else:
                        row = near(dy, 2 * pair + half)
                        gap_x = (row[0:1] + shift) - centre_x
                        gap_y = (row[1:2] + (dy - 1.0)) - centre_y
                        gap_z = (row[2:3] + float(dz)) - centre_z
                        squared = gap_x * gap_x + gap_y * gap_y + gap_z * gap_z
                        inside = jnp.maximum(1.0 - squared, 0.0)
                        tile = (pair_scale * inside * inside).astype(bf16)
                    store(block, (at * 2 + half) * 128, tile)


def add_near(weight_ref, t, a, cell, total_ref, pairs):
    for pair in pairs:
        start, stop, first, width = SPANS[pair]
        near = jnp.concatenate(
            [cell(dy, 2 * pair + half)[0:128, :] for dy in ORDER_Y for half in range(2)], axis=0
        )
        part = dot(weight_ref[t, start:stop].reshape(width * 128, 768), near)
        total_ref[a, first : first + width] += part.reshape(width, 128, 128)


def columns_kernel(first, count, weight_ref, weight_out, sems, slot, spans):
    return [
        pltpu.make_async_copy(
            weight_ref.at[pl.ds(first, count), pl.ds(start, size)],
            weight_out.at[pl.ds(first, count), pl.ds(start, size)],
            sems.at[slot + i],
        )
        for i, (start, size) in enumerate(spans)
    ]


INSIDE = (1,)
ENDS = (0, 2)
INSIDE_BLOCKS = ((2, 4),)
END_BLOCKS = ((0, 2), (6, 2))


def centres_of(own_ref, centre_ref):
    def one(cell, carry):
        x, z = cell // 4, cell % 4
        centre_ref[x, z] = position_of(own_ref[x, z, 128:144, :])
        return carry

    lax.fori_loop(0, 8, one, 0)


def inside_kernel(
    own_ref, below_ref, above_ref, features_ref, self_ref,
    weight_out, total_ref, weight_ref, position_ref, sems
):
    refs = (below_ref, own_ref, above_ref)

    def positions(x, carry):
        for dy in range(3):
            for z in range(4):
                position_ref[dy, x, z] = position_of(refs[dy][x, z, 128:144, :])
        return carry

    lax.fori_loop(0, 2, positions, 0)
    total_ref[...] = dot(features_ref[...].reshape(1024, 128), self_ref[...]).reshape(
        2, 4, 128, 128
    )

    def column(t, carry):
        x, a = t // 2, t % 2

        def store(block, lane, tile):
            weight_ref[t, block, :, lane : lane + 128] = tile

        def near(dy, z):
            return position_ref[dy, x, z - 1]

        weigh(position_ref.at[1], a, (x - a).astype(f32), near, store, INSIDE)
        add_near(weight_ref, t, a, lambda dy, z: refs[dy].at[x, z - 1], total_ref, INSIDE)
        return carry

    lax.fori_loop(0, 4, column, 0)
    copies = columns_kernel(0, 4, weight_ref, weight_out, sems, 0, INSIDE_BLOCKS)
    for copy in copies:
        copy.start()
    for copy in copies:
        copy.wait()


def inside_pairs(own, sides, features, self_weight):
    return pl.pallas_call(
        inside_kernel,
        in_specs=[VM] * 5,
        out_specs=[ANY, VM],
        out_shape=[
            jax.ShapeDtypeStruct((6, 8, 128, 768), bf16),
            jax.ShapeDtypeStruct((2, 4, 128, 128), f32),
        ],
        scratch_shapes=[
            pltpu.VMEM((4, 8, 128, 768), bf16),
            pltpu.VMEM((3, 2, 4, 8, 128), f32),
            pltpu.SemaphoreType.DMA((1,)),
        ],
        cost_estimate=pl.CostEstimate(
            flops=5000000000, bytes_accessed=9000000, transcendentals=0
        ),
        compiler_params=LARGE,
        name="inside_pairs",
    )(own, *sides, features, self_weight)


def ends_kernel(
    own_ref, below_ref, above_ref, left_ref, right_ref,
    before_own, after_own, before_side, after_side, part_ref, _,
    weight_out, total_ref, weight_ref, centre_ref, position_ref, outer_ref, sems
):
    refs = (below_ref, own_ref, above_ref)
    outer = ((before_own, before_side), (after_own, after_side))

    def cell(dy, x, z):
        if z == 0:
            return left_ref.at[dy, x, 0]
        if z == 5:
            return right_ref.at[dy, x, 0]
        return refs[dy].at[x, z - 1]

    def outer_cell(side, dy, z):
        own, beside = outer[side]
        return own.at[0, z - 1] if dy == 1 else beside.at[dy // 2, 0, z - 1]

    centres_of(own_ref, centre_ref)

    def positions(x, carry):
        for dy in range(3):
            for z in (0, 1, 4, 5):
                position_ref[dy, x, z] = position_of(cell(dy, x, z)[128:144, :])
        return carry

    lax.fori_loop(0, 2, positions, 0)
    for side in range(2):
        for dy in range(3):
            for z in (2, 3):
                outer_ref[side, dy, z] = position_of(outer_cell(side, dy, z)[128:144, :])
    total_ref[...] = part_ref[...]

    def column(t, carry):
        x, a = t // 2, t % 2

        def store(block, lane, tile):
            weight_ref[t, block, :, lane : lane + 128] = tile

        def near(dy, z):
            return position_ref[dy, x, z]

        weigh(centre_ref, a, (x - a).astype(f32), near, store, ENDS)
        add_near(weight_ref, t, a, lambda dy, z: cell(dy, x, z), total_ref, ENDS)
        return carry

    lax.fori_loop(0, 4, column, 0)
    copies = columns_kernel(0, 4, weight_ref, weight_out, sems, 0, END_BLOCKS)
    for copy in copies:
        copy.start()

    def outer_column(side, carry):
        def store(block, lane, tile):
            weight_ref[4 + side, block, :, lane : lane + 128] = tile

        def near(dy, z):
            return outer_ref[side, dy, z]

        weigh(centre_ref, side, (2 * side - 1).astype(f32), near, store, INSIDE)
        return carry

    lax.fori_loop(0, 2, outer_column, 0)
    last = columns_kernel(4, 2, weight_ref, weight_out, sems, 2, INSIDE_BLOCKS)
    for copy in last:
        copy.start()
    for side in range(2):
        add_near(
            weight_ref, 4 + side, side, lambda dy, z: outer_cell(side, dy, z), total_ref, INSIDE
        )
    for copy in copies + last:
        copy.wait()


def ends_pairs(own, sides, ends, outer, part, weights):
    return pl.pallas_call(
        ends_kernel,
        in_specs=[VM] * 10 + [ANY],
        out_specs=[ANY, VM],
        input_output_aliases={10: 0},
        out_shape=[
            jax.ShapeDtypeStruct((6, 8, 128, 768), bf16),
            jax.ShapeDtypeStruct((2, 4, 128, 128), f32),
        ],
        scratch_shapes=[
            pltpu.VMEM((6, 8, 128, 768), bf16),
            pltpu.VMEM((2, 4, 8, 128), f32),
            pltpu.VMEM((3, 2, 6, 8, 128), f32),
            pltpu.VMEM((2, 3, 6, 8, 128), f32),
            pltpu.SemaphoreType.DMA((3,)),
        ],
        cost_estimate=pl.CostEstimate(
            flops=9000000000, bytes_accessed=9000000, transcendentals=0
        ),
        compiler_params=LARGE,
        name="ends_pairs",
    )(own, *sides, *ends, *outer, part, weights)


def spline_row(place):
    point = lax.broadcasted_iota(jnp.int32, (PC, 128), 0).astype(f32)
    away = jnp.abs(point - place)
    near = (4.0 - 6.0 * away * away + 3.0 * away * away * away) * (1.0 / 6.0)
    rest = 2.0 - away
    far = rest * rest * rest * (1.0 / 6.0)
    return jnp.where(away < 1.0, near, jnp.where(away < 2.0, far, 0.0))


def message_kernel(
    own_ref, left_ref, right_ref, before_own, after_own, before_side, after_side, before_end,
    after_end, part_ref, read_ref, _,
    weight_out, total_ref, mesh_ref, row_place_ref,
    weight_ref, position_ref, centre_ref, high_ref, low_ref, charge_ref, left_rows, right_rows, sems
):
    refs = ((before_own, before_side, before_end), (after_own, after_side, after_end))

    def cell(side, dy, z):
        own, beside, end = refs[side]
        if z in (0, 5):
            return end.at[dy, 0, z // 5]
        return own.at[0, z - 1] if dy == 1 else beside.at[dy // 2, 0, z - 1]

    centres_of(own_ref, centre_ref)
    for side in range(2):
        for dy in range(3):
            for z in (0, 1, 4, 5):
                position_ref[side, dy, z] = position_of(cell(side, dy, z)[128:144, :])
        for z in range(6):
            row_place_ref[3 * side, z] = place_of(cell(side, 1, z)[128:144, :])

    def row_places(x, carry):
        row_place_ref[1 + x, 0] = place_of(left_ref[1, x, 0, 128:144, :])
        for z in range(4):
            row_place_ref[1 + x, 1 + z] = place_of(own_ref[x, z, 128:144, :])
        row_place_ref[1 + x, 5] = place_of(right_ref[1, x, 0, 128:144, :])
        return carry

    lax.fori_loop(0, 2, row_places, 0)

    def column(side, carry):
        def store(block, lane, tile):
            weight_ref[side, block, :, lane : lane + 128] = tile

        def near(dy, z):
            return position_ref[side, dy, z]

        weigh(centre_ref, side, (2 * side - 1).astype(f32), near, store, ENDS)
        return carry

    lax.fori_loop(0, 2, column, 0)
    copies = [
        pltpu.make_async_copy(
            weight_ref.at[:, pl.ds(start, size)],
            weight_out.at[pl.ds(4, 2), pl.ds(start, size)],
            sems.at[i],
        )
        for i, (start, size) in enumerate(END_BLOCKS)
    ]
    for copy in copies:
        copy.start()
    total_ref[...] = part_ref[...]
    for side in range(2):
        add_near(weight_ref, side, side, lambda dy, z: cell(side, dy, z), total_ref, ENDS)

    def finish(index, carry):
        preact = total_ref[index // 4, index % 4]
        silu = preact * (0.5 + 0.5 * jnp.tanh(0.5 * preact))
        high = silu.astype(bf16)
        high_ref[index] = high
        low_ref[index] = (silu - high.astype(f32)).astype(bf16)
        return carry

    lax.fori_loop(0, 8, finish, 0, unroll=2)
    wide = jnp.broadcast_to(read_ref[...], (16, 128))
    charge_ref[...] = dot_t(wide, high_ref[...].reshape(1024, 128)) + dot_t(
        wide, low_ref[...].reshape(1024, 128)
    )
    block = lax.broadcasted_iota(jnp.int32, (128, 128), 0) // PC

    def spread(cell, carry):
        lanes = pl.ds(pl.multiple_of(cell * 128, 128), 128)
        place = row_place_ref[1 + cell // 4, 1 + cell % 4]
        row_x = spline_row(place[0:1])
        row_y = spline_row(place[1:2]) * charge_ref[0:1, lanes]
        row_z = spline_row(place[2:3])
        left_rows[:, lanes] = (
            (row_y[:, None, :] * row_x[None, :, :]).reshape(PC * PC, 128).astype(bf16)
        )
        right_rows[:, lanes] = jnp.where(block == cell, jnp.tile(row_z, (8, 1)), 0.0).astype(bf16)
        return carry

    lax.fori_loop(0, 8, spread, 0)
    mesh_ref[...] = dot_t(left_rows[...], right_rows[...]).reshape(PC, PC, 128).astype(bf16)
    for copy in copies:
        copy.wait()


def message_layer(own, ends, outer, corners, part, read, weights):
    return pl.pallas_call(
        message_kernel,
        in_specs=[VM] * 11 + [ANY],
        out_specs=[ANY, VM, VM, VM],
        input_output_aliases={11: 0},
        out_shape=[
            jax.ShapeDtypeStruct((6, 8, 128, 768), bf16),
            jax.ShapeDtypeStruct((2, 4, 128, 128), f32),
            jax.ShapeDtypeStruct((PC, PC, 128), bf16),
            jax.ShapeDtypeStruct((4, 6, 8, 128), f32),
        ],
        scratch_shapes=[
            pltpu.VMEM((2, 8, 128, 768), bf16),
            pltpu.VMEM((2, 3, 6, 8, 128), f32),
            pltpu.VMEM((2, 4, 8, 128), f32),
            pltpu.VMEM((8, 128, 128), bf16),
            pltpu.VMEM((8, 128, 128), bf16),
            pltpu.VMEM((16, 1024), f32),
            pltpu.VMEM((PC * PC, 1024), bf16),
            pltpu.VMEM((128, 1024), bf16),
            pltpu.SemaphoreType.DMA((2,)),
        ],
        cost_estimate=pl.CostEstimate(
            flops=5000000000, bytes_accessed=6000000, transcendentals=8 * 16384
        ),
        compiler_params=LARGE,
        name="message",
    )(own, *ends, *outer, *corners, part, read, weights)


def slope_kernel(total_ref, read_ref, out_ref):
    read = read_ref[...].astype(f32)

    def one(index, carry):
        a, c = index // 4, index % 4
        preact = total_ref[a, c]
        sigma = 0.5 + 0.5 * jnp.tanh(0.5 * preact)
        out_ref[a, c] = (read * (sigma * (1.0 + preact * (1.0 - sigma)))).astype(bf16)
        return carry

    lax.fori_loop(0, 8, one, 0, unroll=2)


def slope_of(total, read):
    return pl.pallas_call(
        slope_kernel,
        in_specs=[VM] * 2,
        out_specs=VM,
        out_shape=jax.ShapeDtypeStruct(total.shape, bf16),
        cost_estimate=pl.CostEstimate(
            flops=8 * 16384 * 8, bytes_accessed=900000, transcendentals=8 * 16384
        ),
        compiler_params=SMALL,
        name="slope",
    )(total, read)


def forward_kernel(mesh_ref, along_z_ref, along_x_ref, out_ref):
    lane = lax.broadcasted_iota(jnp.int32, (64, 128), 1)
    total = jnp.zeros((128, 256), f32)
    for g in range(4):
        mesh = mesh_ref[:, g].reshape(64, 128)
        none = jnp.zeros_like(mesh)
        halves = jnp.concatenate(
            [jnp.where(lane < 64, mesh, none), jnp.where(lane < 64, none, mesh)], axis=0
        )
        table = along_z_ref[g * 64 : (g + 1) * 64, :]
        total = total + dot(halves, jnp.concatenate([table, table], axis=0))
    lines = total.astype(bf16)
    waves = dot(along_x_ref[...], lines)
    out_ref[0:128, :] = waves[:, :128]
    out_ref[128:256, :] = waves[:, 128:]


def forward_xz(mesh, along_z, along_x):
    return pl.pallas_call(
        forward_kernel,
        in_specs=[VM] * 3,
        out_specs=VM,
        compiler_params=SMALL,
        out_shape=jax.ShapeDtypeStruct((256, 128), f32),
        cost_estimate=pl.CostEstimate(
            flops=2 * 64 * 512 * 512, bytes_accessed=800000, transcendentals=0
        ),
        name="forward_xz",
    )(mesh, along_z, along_x)


def filter_kernel(lines_ref, into_ref, influence_ref, out_ref):
    waves = dot(into_ref[...], lines_ref[...].astype(bf16))
    scaled = influence_ref[...] * waves
    power = jnp.sum(jnp.sum(scaled * waves, axis=0, keepdims=True), axis=1, keepdims=True)
    out_ref[pl.ds(0, 256, stride=2), :] = lax.dot_general(
        into_ref[...],
        scaled.astype(bf16),
        (((0,), (0,)), ((), ())),
        preferred_element_type=f32,
    )
    out_ref[pl.ds(1, 256, stride=2), :] = jnp.broadcast_to(power, (256, 128))


def filter_y(lines, into, influence):
    return pl.pallas_call(
        filter_kernel,
        in_specs=[VM] * 3,
        out_specs=VM,
        compiler_params=SMALL,
        out_shape=jax.ShapeDtypeStruct((512, 128), f32),
        cost_estimate=pl.CostEstimate(
            flops=4 * 256 * 256 * 128, bytes_accessed=700000, transcendentals=0
        ),
        name="filter_y",
    )(lines, into, influence)


def inverse_kernel(energy_scale, lines_ref, along_x_ref, along_z_ref, out_ref, energy_ref):
    waves = jnp.concatenate(
        [lines_ref[pl.ds(0, 128, stride=2), :], lines_ref[pl.ds(256, 128, stride=2), :]], axis=1
    ).astype(bf16)
    half = dot(along_x_ref[...], waves).astype(bf16)
    field = dot(half, along_z_ref[...]).astype(bf16)
    for gx in range(4):
        for gz in range(4):
            out_ref[gx, gz] = field[gx * 64 : (gx + 1) * 64, gz * 128 : (gz + 1) * 128]
    power = jnp.sum(lines_ref[pl.ds(1, 256, stride=2), :], axis=0, keepdims=True)
    energy_ref[...] = jnp.broadcast_to(power * energy_scale, (8, 128))


def inverse_xz(lines, along_x, along_z, energy_scale):
    return pl.pallas_call(
        functools.partial(inverse_kernel, energy_scale),
        in_specs=[VM] * 3,
        out_specs=[VM, VM],
        compiler_params=SMALL,
        out_shape=[
            jax.ShapeDtypeStruct((4, 4, 64, 128), bf16),
            jax.ShapeDtypeStruct((8, 128), f32),
        ],
        cost_estimate=pl.CostEstimate(
            flops=2 * 256 * 256 * 640, bytes_accessed=900000, transcendentals=0
        ),
        name="inverse_xz",
    )(lines, along_x, along_z)


def interpolate_kernel(
    field_scale, field_ref, place_ref, stored_ref, rows_ref, before_ref, after_ref,
    out_ref, own_ref, weight_ref, slope_ref, sems
):
    pairs = [
        (rows_ref, slope_ref.at[:, pl.ds(1, 2)]),
        (before_ref, slope_ref.at[:, pl.ds(0, 1)]),
        (after_ref, slope_ref.at[:, pl.ds(3, 1)]),
        (stored_ref.at[pl.ds(0, 3)], weight_ref.at[pl.ds(0, 3)]),
        (stored_ref.at[pl.ds(3, 3)], weight_ref.at[pl.ds(3, 3)]),
    ]
    copies = [
        pltpu.make_async_copy(source, target, sems.at[i])
        for i, (source, target) in enumerate(pairs)
    ]
    for copy in copies:
        copy.start()
    block = lax.broadcasted_iota(jnp.int32, (128, 128), 0) // PC

    def gather(step, carry):
        ax, half = step // 2, 3 * (step % 2)
        field = field_ref[:, pl.ds(pl.multiple_of(ax * PC, PC), PC), :].reshape(PC * PC, 128)
        for third in range(3):
            cz = half + third
            place = place_ref[ax * 6 + cz]
            row_x = spline_row(place[0:1])
            row_y = spline_row(place[1:2])
            row_z = spline_row(place[2:3])
            right = jnp.where(block == cz + 1, jnp.tile(row_z, (8, 1)), 0.0).astype(bf16)
            partial = dot(field, right)
            left = (row_y[:, None, :] * row_x[None, :, :]).reshape(PC * PC, 128)
            out_ref[pl.ds(ax * 6 + cz, 1), :] = (
                jnp.sum(partial * left, axis=0, keepdims=True) * field_scale
            )
        return carry

    lax.fori_loop(0, 8, gather, 0)
    own_ref[0:4, :] = out_ref[7:11, :]
    own_ref[4:8, :] = out_ref[13:17, :]
    for copy in copies:
        copy.wait()


def interpolate(field, place, weights, slopes, field_scale):
    return pl.pallas_call(
        functools.partial(interpolate_kernel, field_scale),
        in_specs=[VM] * 2 + [ANY] * 4,
        out_specs=[VM] * 4,
        compiler_params=MIDDLE,
        out_shape=[
            jax.ShapeDtypeStruct((24, 128), f32),
            jax.ShapeDtypeStruct((8, 128), f32),
            jax.ShapeDtypeStruct((6, 8, 128, 768), bf16),
            jax.ShapeDtypeStruct((3, 4, 6, 128, 128), bf16),
        ],
        scratch_shapes=[pltpu.SemaphoreType.DMA((5,))],
        cost_estimate=pl.CostEstimate(
            flops=24 * 2 * 256 * 128 * 128, bytes_accessed=400000, transcendentals=0
        ),
        name="interpolate",
    )(field, place, weights, *slopes)


def combination_of(t):
    return jnp.where(t < 4, 1 + t // 2, 3 * (t - 4)), t % 2


def scaled(columns, cell, slope):
    return (columns[:, cell : cell + 1] * slope.astype(f32)).astype(bf16)


def beside_kernel(
    weight_ref, slope_ref, potential_ref, total_ref, own_out, near_ref
):
    columns = jnp.transpose(potential_ref[...])
    for x in range(4):
        for z in range(6):
            near_ref[x, z] = scaled(columns, x * 6 + z, slope_ref[1, x, z])
    own_out[...] = near_ref[1:3, 1:5]
    total_ref[...] = jnp.zeros_like(total_ref)

    def combination(t, carry):
        x, a = combination_of(t)
        for pair, (start, stop, first, width) in enumerate(SPANS):
            part = dot(
                weight_ref[t, start:stop, :, 512:768].reshape(width * 128, 256),
                near_ref[x, 2 * pair : 2 * pair + 2].reshape(256, 128),
            )
            total_ref[a, first : first + width] += part.reshape(width, 128, 128)
        return carry

    lax.fori_loop(0, 6, combination, 0)


def beside(weights, slopes, potential):
    return pl.pallas_call(
        beside_kernel,
        in_specs=[VM] * 3,
        out_specs=[VM] * 2,
        out_shape=[
            jax.ShapeDtypeStruct((2, 4, 128, 128), f32),
            jax.ShapeDtypeStruct((2, 4, 128, 128), bf16),
        ],
        scratch_shapes=[
            pltpu.VMEM((4, 6, 128, 128), bf16),
        ],
        cost_estimate=pl.CostEstimate(
            flops=3000000000, bytes_accessed=12000000, transcendentals=0
        ),
        compiler_params=SMALL,
        name="beside",
    )(weights, slopes, potential)


def backward_kernel(
    weight_ref, slope_ref, part_ref, own_ref, below_ref, above_ref, msg_ref, self_ref, out_ref,
    near_ref, total_ref, potential_ref
):
    potential_ref[0] = below_ref[...]
    potential_ref[1] = above_ref[...]

    def scale(side, carry):
        columns = jnp.transpose(potential_ref[side])
        for x in range(4):
            for z in range(6):
                near_ref[side, x, z] = scaled(columns, x * 6 + z, slope_ref[2 * side, x, z])
        return carry

    lax.fori_loop(0, 2, scale, 0)
    total_ref[...] = part_ref[...]

    def combination(t, carry):
        x, a = combination_of(t)
        for pair, (start, stop, first, width) in enumerate(SPANS):
            near = jnp.concatenate(
                [
                    near_ref[side, x, 2 * pair : 2 * pair + 2].reshape(256, 128)
                    for side in range(2)
                ],
                axis=0,
            )
            part = dot(weight_ref[t, start:stop, :, 0:512].reshape(width * 128, 512), near)
            total_ref[a, first : first + width] += part.reshape(width, 128, 128)
        return carry

    lax.fori_loop(0, 6, combination, 0)

    def finish(a, carry):
        back = total_ref[a].reshape(512, 128).astype(bf16)
        own = own_ref[a].reshape(512, 128)
        out_ref[a] = (dot_t(back, msg_ref[...]) + dot_t(own, self_ref[...])).reshape(4, 128, 128)
        return carry

    lax.fori_loop(0, 2, finish, 0)


def backward(weights, slope, part, own, below, above, msg_weight, self_weight):
    return pl.pallas_call(
        backward_kernel,
        in_specs=[VM] * 8,
        out_specs=VM,
        out_shape=jax.ShapeDtypeStruct((2, 4, 128, 128), f32),
        scratch_shapes=[
            pltpu.VMEM((2, 4, 6, 128, 128), bf16),
            pltpu.VMEM((2, 4, 128, 128), f32),
            pltpu.VMEM((2, 24, 128), f32),
        ],
        cost_estimate=pl.CostEstimate(
            flops=4000000000, bytes_accessed=12000000, transcendentals=0
        ),
        compiler_params=SMALL,
        name="backward",
    )(weights, slope, part, own, below, above, msg_weight, self_weight)


def wave_tables(size_x, size_y, size_z):
    i16 = np.arange(16)
    points_x = np.array([g * 32 + a * 16 + i for a in range(2) for g in range(4) for i in i16])
    along_x = cas(np.arange(size_x), points_x, size_x)
    points_y = np.array(
        [gy * 16 + gx * 4 + gz for gx in range(4) for gy in range(16) for gz in range(4)]
    )
    into_y = cas(np.arange(size_y), points_y, size_y)
    back_x = np.array(
        [((2 * g - 1 + a) % 8) * 16 + i for g in range(4) for a in range(4) for i in i16]
    )
    back_z = np.array(
        [((4 * g - 2 + c) % 16) * 16 + k for g in range(4) for c in range(8) for k in i16]
    )
    tables = (
        cas(np.arange(size_z), np.arange(size_z), size_z),
        along_x,
        into_y,
        cas(back_x, np.arange(size_x), size_x),
        cas(np.arange(size_z), back_z, size_z),
    )
    return [jnp.asarray(np.ascontiguousarray(t), dtype=bf16) for t in tables]


def influence_of(size_x, size_y, size_z):
    device = lax.axis_index(everyone)

    def wave(index, size):
        signed = jnp.where(2 * index >= size, index - size, index)
        return signed.astype(f32) * (PC / size)

    wave_x = wave(device % size_x, size_x)
    wave_y = wave(jnp.arange(size_y, dtype=jnp.int32), size_y)[:, None]
    wave_z = wave(
        device // size_x * 128 + jnp.arange(size_z // 2, dtype=jnp.int32), size_z
    )[None, :]
    squared = wave_x * wave_x + wave_y * wave_y + wave_z * wave_z
    safe = jnp.where(squared > 0, squared, 1.0)
    return jnp.where(squared > 0, jnp.exp(-((math.pi * spread_width) ** 2) * squared) / safe, 0.0)


def swapped(value, axis):
    return lax.all_to_all(value, axis, split_axis=0, concat_axis=0, tiled=True)


def body(features, msg_weight, self_weight, charge_weight, spline_corner, spline_fraction):
    cells_x, cells_y, cells_z, slots, width = features.shape
    size_x = cells_x * PC * lax.axis_size("gx")
    size_y = cells_y * PC * lax.axis_size("gy")
    size_z = cells_z * PC * lax.axis_size("gz")
    volume = size_x // PC * (size_y // PC) * (size_z // PC)
    natoms = volume * slots
    cells = cells_x * cells_z

    features_own = features.reshape(cells, slots, width)
    own = project(
        features_own, msg_weight, spline_corner.swapaxes(2, 3), spline_fraction.swapaxes(2, 3)
    )
    own = own.reshape(cells_x, cells_z, slots + 16, width)
    sides, ends, outer, corners = early_halo(own)
    weights, part = inside_pairs(own, sides, features_own, self_weight)
    weights, part = ends_pairs(own, sides, ends, outer, part, weights)
    influence = influence_of(size_x, size_y, size_z)
    along_z, along_x, into_y, back_x, back_z = wave_tables(size_x, size_y, size_z)

    read = charge_weight[None, :]
    weights, preact, mesh, row_place = message_layer(
        own, ends, outer, corners, part, read, weights
    )
    mesh = swapped(mesh, plane).reshape(4, 4, PC, 128)
    slope_near = late_halo(slope_of(preact, read))
    lines = swapped(forward_xz(mesh, along_z, along_x), everyone)
    lines = swapped(filter_y(lines, into_y, influence), everyone)
    field, energy = inverse_xz(lines, back_x, back_z, coupling / (2.0 * volume * natoms))
    field = swapped(field.reshape(16, 64, 128), plane)
    potential, atom_potential, weights, slopes = interpolate(
        field, row_place.reshape(24, 8, slots), weights, slope_near, coupling / volume
    )
    below, above = moved(potential, "gy", 1), moved(potential, "gy", -1)
    total, cotangent = beside(weights, slopes, potential)
    grad = backward(weights, slopes, total, cotangent, below, above, msg_weight, self_weight)
    return (
        grad.reshape(features.shape),
        atom_potential.reshape(cells_x, cells_y, cells_z, slots),
        energy[0, 0],
    )


def solution(mesh):
    in_specs = (
        P("gx", "gy", "gz", None, None),
        P(),
        P(),
        P(),
        P("gx", "gy", "gz", None, None),
        P("gx", "gy", "gz", None, None),
    )
    out_specs = (P("gx", "gy", "gz", None, None), P("gx", "gy", "gz", None), P())
    return jax.shard_map(body, mesh=mesh, in_specs=in_specs, out_specs=out_specs, check_vma=False)
```

```python
import functools
import math

import jax
import jax.numpy as jnp
import numpy as np
from jax import lax
from jax.experimental import pallas as pl
from jax.experimental.pallas import tpu as pltpu
from jax.sharding import PartitionSpec as P

PC = 16
pair_scale = 0.1
coupling = 0.125
spread_width = 0.0625
f32 = jnp.float32
bf16 = jnp.bfloat16
plane = ("gx", "gz")
everyone = ("gx", "gy", "gz")


def dot(a, b):
    return jnp.dot(a, b, preferred_element_type=f32)


def dot_t(a, b, precision=None):
    return lax.dot_general(
        a, b, (((1,), (1,)), ((), ())), preferred_element_type=f32, precision=precision
    )


def whole(shape):
    zeros = (0,) * len(shape)
    return pl.BlockSpec(shape, lambda *_: zeros)


VM = pl.BlockSpec(memory_space=pltpu.VMEM)
ANY = pl.BlockSpec(memory_space=pl.ANY)
SMALL = pltpu.CompilerParams(vmem_limit_bytes=20 << 20)
FIRST = pltpu.CompilerParams(vmem_limit_bytes=60 << 20)
LARGE = pltpu.CompilerParams(vmem_limit_bytes=50 << 20)
MIDDLE = pltpu.CompilerParams(vmem_limit_bytes=40 << 20)
FIELD = pltpu.CompilerParams(vmem_limit_bytes=44 << 20)


def cas(rows, columns, size):
    turns = np.outer(rows, columns) % size
    angle = 2.0 * np.pi / size * turns
    return np.cos(angle) + np.sin(angle)


def moved(value, axis, step):
    count = lax.axis_size(axis)
    pairs = [(i, (i + step) % count) for i in range(count)]
    return lax.ppermute(value.reshape(-1, 128), axis, pairs).reshape(value.shape)


def early_halo(own):
    last_x, last_z = own.shape[0] - 1, own.shape[1] - 1
    below, above = moved(own, "gy", 1), moved(own, "gy", -1)
    beside = [moved(own[last_x:], "gx", 1), moved(own[:1], "gx", -1)]
    sides = jnp.stack([below, above])
    rows = [below, own, above]
    left = moved(jnp.stack([row[:, last_z:] for row in rows]), "gz", 1)
    right = moved(jnp.stack([row[:, :1] for row in rows]), "gz", -1)
    aside = [moved(sides[:, last_x:], "gx", 1), moved(sides[:, :1], "gx", -1)]
    corners = [
        moved(jnp.concatenate([left[:, at : at + 1], right[:, at : at + 1]], axis=2), "gx", step)
        for at, step in ((last_x, 1), (0, -1))
    ]
    return [below, above], [left, right], beside + aside, corners


def project_kernel(features_ref, weight_ref, corner_ref, fraction_ref, out_ref):
    value = dot(features_ref[...].reshape(1024, 128), weight_ref[...]).astype(bf16)
    out_ref[:, :128, :] = value.reshape(8, 128, 128)
    none = jnp.zeros((5, 128), f32)
    for x in range(2):
        place = corner_ref[x, 0].astype(f32) + 1.0 + fraction_ref[x, 0]
        high = place.astype(bf16).astype(f32)
        rest = place - high
        middle = rest.astype(bf16).astype(f32)
        low = rest - middle
        for z in range(4):
            rows = [part[d, z : z + 1] for part in (high, low) for d in range(3)]
            rows += [none[:2]] + [middle[d, z : z + 1] for d in range(3)] + [none]
            out_ref[x * 4 + z, 128:, :] = jnp.concatenate(rows, axis=0).astype(bf16)


def project(features, weight, corner, fraction):
    return pl.pallas_call(
        project_kernel,
        grid=(1,),
        in_specs=[whole((8, 128, 128)), whole((128, 128))]
        + [whole((2, 1, 3, 4, 128))] * 2,
        out_specs=whole((8, 144, 128)),
        out_shape=jax.ShapeDtypeStruct((8, 144, 128), bf16),
        compiler_params=FIRST,
        name="project",
    )(features, weight, corner, fraction)


def place_of(rows):
    rows = rows.astype(f32)
    return rows[0:8] + rows[8:16] + pltpu.roll(rows[0:8], 5, 0)


BLOCKS = ((0, 0), (0, 1), (1, 0), (1, 1), (1, 2), (1, 3), (2, 2), (2, 3))
SPANS = ((0, 2, 0, 2), (2, 6, 0, 4), (6, 8, 2, 2))
ORDER_Y = (0, 2, 1)


def position_of(rows):
    return (place_of(rows) * (1.0 / PC)).astype(bf16).astype(f32)


def weigh(centres, a, shift, near, store, pairs):
    for c in range(4):
        columns = jnp.transpose(centres[a, c])
        centre_x = jnp.broadcast_to(columns[:, 0:1], (128, 128))
        centre_y = jnp.broadcast_to(columns[:, 1:2], (128, 128))
        centre_z = jnp.broadcast_to(columns[:, 2:3], (128, 128))
        for block, (pair, owner) in enumerate(BLOCKS):
            if owner != c or pair not in pairs:
                continue
            for at, dy in enumerate(ORDER_Y):
                for half in range(2):
                    dz = 2 * pair + half - c - 1
                    if abs(dz) > 1:
                        tile = jnp.zeros((128, 128), bf16)
                    else:
                        row = near(dy, 2 * pair + half)
                        gap_x = (row[0:1] + shift) - centre_x
                        gap_y = (row[1:2] + (dy - 1.0)) - centre_y
                        gap_z = (row[2:3] + float(dz)) - centre_z
                        squared = gap_x * gap_x + gap_y * gap_y + gap_z * gap_z
                        inside = jnp.maximum(1.0 - squared, 0.0)
                        tile = (pair_scale * inside * inside).astype(bf16)
                    store(block, (at * 2 + half) * 128, tile)


def add_near(weight_ref, t, a, cell, total_ref, pairs):
    for pair in pairs:
        start, stop, first, width = SPANS[pair]
        near = jnp.concatenate(
            [cell(dy, 2 * pair + half)[0:128, :] for dy in ORDER_Y for half in range(2)], axis=0
        )
        part = dot(weight_ref[t, start:stop].reshape(width * 128, 768), near)
        total_ref[a, first : first + width] += part.reshape(width, 128, 128)


def columns_kernel(first, count, weight_ref, weight_out, sems, slot, spans):
    return [
        pltpu.make_async_copy(
            weight_ref.at[pl.ds(first, count), pl.ds(start, size)],
            weight_out.at[pl.ds(first, count), pl.ds(start, size)],
            sems.at[slot + i],
        )
        for i, (start, size) in enumerate(spans)
    ]


INSIDE = (1,)
ENDS = (0, 2)
INSIDE_BLOCKS = ((2, 4),)
END_BLOCKS = ((0, 2), (6, 2))


def centres_of(own_ref, centre_ref):
    def one(cell, carry):
        x, z = cell // 4, cell % 4
        centre_ref[x, z] = position_of(own_ref[x, z, 128:144, :])
        return carry

    lax.fori_loop(0, 8, one, 0)


def inside_kernel(
    own_ref, below_ref, above_ref, features_ref, self_ref,
    weight_out, total_ref, weight_ref, position_ref, sems
):
    refs = (below_ref, own_ref, above_ref)

    def positions(x, carry):
        for dy in range(3):
            for z in range(4):
                position_ref[dy, x, z] = position_of(refs[dy][x, z, 128:144, :])
        return carry

    lax.fori_loop(0, 2, positions, 0)
    total_ref[...] = dot(features_ref[...].reshape(1024, 128), self_ref[...]).reshape(
        2, 4, 128, 128
    )

    def column(t, carry):
        x, a = t // 2, t % 2

        def store(block, lane, tile):
            weight_ref[t, block, :, lane : lane + 128] = tile

        def near(dy, z):
            return position_ref[dy, x, z - 1]

        weigh(position_ref.at[1], a, (x - a).astype(f32), near, store, INSIDE)
        add_near(weight_ref, t, a, lambda dy, z: refs[dy].at[x, z - 1], total_ref, INSIDE)
        return carry

    lax.fori_loop(0, 4, column, 0)
    copies = columns_kernel(0, 4, weight_ref, weight_out, sems, 0, INSIDE_BLOCKS)
    for copy in copies:
        copy.start()
    for copy in copies:
        copy.wait()


def inside_pairs(own, sides, features, self_weight):
    return pl.pallas_call(
        inside_kernel,
        in_specs=[VM] * 5,
        out_specs=[ANY, VM],
        out_shape=[
            jax.ShapeDtypeStruct((6, 8, 128, 768), bf16),
            jax.ShapeDtypeStruct((2, 4, 128, 128), f32),
        ],
        scratch_shapes=[
            pltpu.VMEM((4, 8, 128, 768), bf16),
            pltpu.VMEM((3, 2, 4, 8, 128), f32),
            pltpu.SemaphoreType.DMA((1,)),
        ],
        cost_estimate=pl.CostEstimate(
            flops=5000000000, bytes_accessed=9000000, transcendentals=0
        ),
        compiler_params=LARGE,
        name="inside_pairs",
    )(own, *sides, features, self_weight)


def ends_kernel(
    own_ref, below_ref, above_ref, left_ref, right_ref,
    before_own, after_own, before_side, after_side, part_ref, _,
    weight_out, total_ref, weight_ref, centre_ref, position_ref, outer_ref, sems
):
    refs = (below_ref, own_ref, above_ref)
    outer = ((before_own, before_side), (after_own, after_side))

    def cell(dy, x, z):
        if z == 0:
            return left_ref.at[dy, x, 0]
        if z == 5:
            return right_ref.at[dy, x, 0]
        return refs[dy].at[x, z - 1]

    def outer_cell(side, dy, z):
        own, beside = outer[side]
        return own.at[0, z - 1] if dy == 1 else beside.at[dy // 2, 0, z - 1]

    centres_of(own_ref, centre_ref)

    def positions(x, carry):
        for dy in range(3):
            for z in (0, 1, 4, 5):
                position_ref[dy, x, z] = position_of(cell(dy, x, z)[128:144, :])
        return carry

    lax.fori_loop(0, 2, positions, 0)
    for side in range(2):
        for dy in range(3):
            for z in (2, 3):
                outer_ref[side, dy, z] = position_of(outer_cell(side, dy, z)[128:144, :])
    total_ref[...] = part_ref[...]

    def column(t, carry):
        x, a = t // 2, t % 2

        def store(block, lane, tile):
            weight_ref[t, block, :, lane : lane + 128] = tile

        def near(dy, z):
            return position_ref[dy, x, z]

        weigh(centre_ref, a, (x - a).astype(f32), near, store, ENDS)
        add_near(weight_ref, t, a, lambda dy, z: cell(dy, x, z), total_ref, ENDS)
        return carry

    lax.fori_loop(0, 4, column, 0)
    copies = columns_kernel(0, 4, weight_ref, weight_out, sems, 0, END_BLOCKS)
    for copy in copies:
        copy.start()

    def outer_column(side, carry):
        def store(block, lane, tile):
            weight_ref[4 + side, block, :, lane : lane + 128] = tile

        def near(dy, z):
            return outer_ref[side, dy, z]

        weigh(centre_ref, side, (2 * side - 1).astype(f32), near, store, INSIDE)
        return carry

    lax.fori_loop(0, 2, outer_column, 0)
    last = columns_kernel(4, 2, weight_ref, weight_out, sems, 2, INSIDE_BLOCKS)
    for copy in last:
        copy.start()
    for side in range(2):
        add_near(
            weight_ref, 4 + side, side, lambda dy, z: outer_cell(side, dy, z), total_ref, INSIDE
        )
    for copy in copies + last:
        copy.wait()


def ends_pairs(own, sides, ends, outer, part, weights):
    return pl.pallas_call(
        ends_kernel,
        in_specs=[VM] * 10 + [ANY],
        out_specs=[ANY, VM],
        input_output_aliases={10: 0},
        out_shape=[
            jax.ShapeDtypeStruct((6, 8, 128, 768), bf16),
            jax.ShapeDtypeStruct((2, 4, 128, 128), f32),
        ],
        scratch_shapes=[
            pltpu.VMEM((6, 8, 128, 768), bf16),
            pltpu.VMEM((2, 4, 8, 128), f32),
            pltpu.VMEM((3, 2, 6, 8, 128), f32),
            pltpu.VMEM((2, 3, 6, 8, 128), f32),
            pltpu.SemaphoreType.DMA((3,)),
        ],
        cost_estimate=pl.CostEstimate(
            flops=9000000000, bytes_accessed=9000000, transcendentals=0
        ),
        compiler_params=LARGE,
        name="ends_pairs",
    )(own, *sides, *ends, *outer, part, weights)


def spline_row(place):
    point = lax.broadcasted_iota(jnp.int32, (PC, 128), 0).astype(f32)
    away = jnp.abs(point - place)
    near = (4.0 - 6.0 * away * away + 3.0 * away * away * away) * (1.0 / 6.0)
    rest = 2.0 - away
    far = rest * rest * rest * (1.0 / 6.0)
    return jnp.where(away < 1.0, near, jnp.where(away < 2.0, far, 0.0))


def message_kernel(
    own_ref, left_ref, right_ref, before_own, after_own, before_side, after_side, before_end,
    after_end, part_ref, read_ref, _,
    weight_out, total_ref, mesh_ref, row_place_ref,
    weight_ref, position_ref, centre_ref, high_ref, low_ref, charge_ref, left_rows, right_rows, sems
):
    refs = ((before_own, before_side, before_end), (after_own, after_side, after_end))

    def cell(side, dy, z):
        own, beside, end = refs[side]
        if z in (0, 5):
            return end.at[dy, 0, z // 5]
        return own.at[0, z - 1] if dy == 1 else beside.at[dy // 2, 0, z - 1]

    centres_of(own_ref, centre_ref)
    for side in range(2):
        for dy in range(3):
            for z in (0, 1, 4, 5):
                position_ref[side, dy, z] = position_of(cell(side, dy, z)[128:144, :])
        for z in range(6):
            row_place_ref[3 * side, z] = place_of(cell(side, 1, z)[128:144, :])

    def row_places(x, carry):
        row_place_ref[1 + x, 0] = place_of(left_ref[1, x, 0, 128:144, :])
        for z in range(4):
            row_place_ref[1 + x, 1 + z] = place_of(own_ref[x, z, 128:144, :])
        row_place_ref[1 + x, 5] = place_of(right_ref[1, x, 0, 128:144, :])
        return carry

    lax.fori_loop(0, 2, row_places, 0)

    def column(side, carry):
        def store(block, lane, tile):
            weight_ref[side, block, :, lane : lane + 128] = tile

        def near(dy, z):
            return position_ref[side, dy, z]

        weigh(centre_ref, side, (2 * side - 1).astype(f32), near, store, ENDS)
        return carry

    lax.fori_loop(0, 2, column, 0)
    copies = [
        pltpu.make_async_copy(
            weight_ref.at[:, pl.ds(start, size)],
            weight_out.at[pl.ds(4, 2), pl.ds(start, size)],
            sems.at[i],
        )
        for i, (start, size) in enumerate(END_BLOCKS)
    ]
    for copy in copies:
        copy.start()
    total_ref[...] = part_ref[...]
    for side in range(2):
        add_near(weight_ref, side, side, lambda dy, z: cell(side, dy, z), total_ref, ENDS)

    def finish(index, carry):
        preact = total_ref[index // 4, index % 4]
        silu = preact * (0.5 + 0.5 * jnp.tanh(0.5 * preact))
        high = silu.astype(bf16)
        high_ref[index] = high
        low_ref[index] = (silu - high.astype(f32)).astype(bf16)
        return carry

    lax.fori_loop(0, 8, finish, 0, unroll=2)
    wide = jnp.broadcast_to(read_ref[...], (16, 128))
    charge_ref[...] = dot_t(wide, high_ref[...].reshape(1024, 128)) + dot_t(
        wide, low_ref[...].reshape(1024, 128)
    )
    block = lax.broadcasted_iota(jnp.int32, (128, 128), 0) // PC

    def spread(cell, carry):
        lanes = pl.ds(pl.multiple_of(cell * 128, 128), 128)
        place = row_place_ref[1 + cell // 4, 1 + cell % 4]
        row_x = spline_row(place[0:1])
        row_y = spline_row(place[1:2]) * charge_ref[0:1, lanes]
        row_z = spline_row(place[2:3])
        left_rows[:, lanes] = (
            (row_y[:, None, :] * row_x[None, :, :]).reshape(PC * PC, 128).astype(bf16)
        )
        right_rows[:, lanes] = jnp.where(block == cell, jnp.tile(row_z, (8, 1)), 0.0).astype(bf16)
        return carry

    lax.fori_loop(0, 8, spread, 0)
    mesh_ref[...] = dot_t(left_rows[...], right_rows[...]).reshape(PC, PC, 128).astype(bf16)
    for copy in copies:
        copy.wait()


def message_layer(own, ends, outer, corners, part, read, weights):
    return pl.pallas_call(
        message_kernel,
        in_specs=[VM] * 11 + [ANY],
        out_specs=[ANY, VM, VM, VM],
        input_output_aliases={11: 0},
        out_shape=[
            jax.ShapeDtypeStruct((6, 8, 128, 768), bf16),
            jax.ShapeDtypeStruct((2, 4, 128, 128), f32),
            jax.ShapeDtypeStruct((PC, PC, 128), bf16),
            jax.ShapeDtypeStruct((4, 6, 8, 128), f32),
        ],
        scratch_shapes=[
            pltpu.VMEM((2, 8, 128, 768), bf16),
            pltpu.VMEM((2, 3, 6, 8, 128), f32),
            pltpu.VMEM((2, 4, 8, 128), f32),
            pltpu.VMEM((8, 128, 128), bf16),
            pltpu.VMEM((8, 128, 128), bf16),
            pltpu.VMEM((16, 1024), f32),
            pltpu.VMEM((PC * PC, 1024), bf16),
            pltpu.VMEM((128, 1024), bf16),
            pltpu.SemaphoreType.DMA((2,)),
        ],
        cost_estimate=pl.CostEstimate(
            flops=5000000000, bytes_accessed=6000000, transcendentals=8 * 16384
        ),
        compiler_params=LARGE,
        name="message",
    )(own, *ends, *outer, *corners, part, read, weights)


def slope_kernel(total_ref, read_ref, out_ref):
    read = read_ref[...].astype(f32)

    def one(index, carry):
        a, c = index // 4, index % 4
        preact = total_ref[a, c]
        sigma = 0.5 + 0.5 * jnp.tanh(0.5 * preact)
        out_ref[a, c] = (read * (sigma * (1.0 + preact * (1.0 - sigma)))).astype(bf16)
        return carry

    lax.fori_loop(0, 8, one, 0, unroll=2)


def slope_of(total, read):
    return pl.pallas_call(
        slope_kernel,
        in_specs=[VM] * 2,
        out_specs=VM,
        out_shape=jax.ShapeDtypeStruct(total.shape, bf16),
        cost_estimate=pl.CostEstimate(
            flops=8 * 16384 * 8, bytes_accessed=900000, transcendentals=8 * 16384
        ),
        compiler_params=SMALL,
        name="slope",
    )(total, read)


def forward_kernel(mesh_ref, along_z_ref, along_x_ref, out_ref):
    lane = lax.broadcasted_iota(jnp.int32, (64, 128), 1)
    total = jnp.zeros((128, 256), f32)
    for g in range(4):
        mesh = mesh_ref[:, g].reshape(64, 128)
        none = jnp.zeros_like(mesh)
        halves = jnp.concatenate(
            [jnp.where(lane < 64, mesh, none), jnp.where(lane < 64, none, mesh)], axis=0
        )
        table = along_z_ref[g * 64 : (g + 1) * 64, :]
        total = total + dot(halves, jnp.concatenate([table, table], axis=0))
    lines = total.astype(bf16)
    waves = dot(along_x_ref[...], lines)
    out_ref[0:128, :] = waves[:, :128]
    out_ref[128:256, :] = waves[:, 128:]


def forward_xz(mesh, along_z, along_x):
    return pl.pallas_call(
        forward_kernel,
        in_specs=[VM] * 3,
        out_specs=VM,
        compiler_params=SMALL,
        out_shape=jax.ShapeDtypeStruct((256, 128), f32),
        cost_estimate=pl.CostEstimate(
            flops=2 * 64 * 512 * 512, bytes_accessed=800000, transcendentals=0
        ),
        name="forward_xz",
    )(mesh, along_z, along_x)


def filter_kernel(lines_ref, into_ref, influence_ref, out_ref):
    waves = dot(into_ref[...], lines_ref[...].astype(bf16))
    scaled = influence_ref[...] * waves
    power = jnp.sum(jnp.sum(scaled * waves, axis=0, keepdims=True), axis=1, keepdims=True)
    out_ref[pl.ds(0, 256, stride=2), :] = lax.dot_general(
        into_ref[...],
        scaled.astype(bf16),
        (((0,), (0,)), ((), ())),
        preferred_element_type=f32,
    )
    out_ref[pl.ds(1, 256, stride=2), :] = jnp.broadcast_to(power, (256, 128))


def filter_y(lines, into, influence):
    return pl.pallas_call(
        filter_kernel,
        in_specs=[VM] * 3,
        out_specs=VM,
        compiler_params=SMALL,
        out_shape=jax.ShapeDtypeStruct((512, 128), f32),
        cost_estimate=pl.CostEstimate(
            flops=4 * 256 * 256 * 128, bytes_accessed=700000, transcendentals=0
        ),
        name="filter_y",
    )(lines, into, influence)


def inverse_kernel(energy_scale, lines_ref, along_x_ref, along_z_ref, out_ref, energy_ref):
    waves = jnp.concatenate(
        [lines_ref[pl.ds(0, 128, stride=2), :], lines_ref[pl.ds(256, 128, stride=2), :]], axis=1
    ).astype(bf16)
    half = dot(along_x_ref[...], waves).astype(bf16)
    field = dot(half, along_z_ref[...]).astype(bf16)
    for gx in range(4):
        for gz in range(4):
            out_ref[gx, gz] = field[gx * 64 : (gx + 1) * 64, gz * 128 : (gz + 1) * 128]
    power = jnp.sum(lines_ref[pl.ds(1, 256, stride=2), :], axis=0, keepdims=True)
    energy_ref[...] = jnp.broadcast_to(power * energy_scale, (8, 128))


def inverse_xz(lines, along_x, along_z, energy_scale):
    return pl.pallas_call(
        functools.partial(inverse_kernel, energy_scale),
        in_specs=[VM] * 3,
        out_specs=[VM, VM],
        compiler_params=SMALL,
        out_shape=[
            jax.ShapeDtypeStruct((4, 4, 64, 128), bf16),
            jax.ShapeDtypeStruct((8, 128), f32),
        ],
        cost_estimate=pl.CostEstimate(
            flops=2 * 256 * 256 * 640, bytes_accessed=900000, transcendentals=0
        ),
        name="inverse_xz",
    )(lines, along_x, along_z)


def interpolate_kernel(
    field_scale, field_ref, place_ref, stored_ref, rows_ref, before_ref, after_ref,
    out_ref, own_ref, weight_ref, slope_ref, sems
):
    pairs = [
        (rows_ref, slope_ref.at[:, pl.ds(1, 2)]),
        (before_ref, slope_ref.at[:, pl.ds(0, 1)]),
        (after_ref, slope_ref.at[:, pl.ds(3, 1)]),
        (stored_ref.at[:, :, :, pl.ds(512, 256)], weight_ref),
    ]
    copies = [
        pltpu.make_async_copy(source, target, sems.at[i])
        for i, (source, target) in enumerate(pairs)
    ]
    for copy in copies:
        copy.start()
    block = lax.broadcasted_iota(jnp.int32, (128, 128), 0) // PC

    def gather(step, carry):
        ax, half = step // 2, 3 * (step % 2)
        field = field_ref[:, pl.ds(pl.multiple_of(ax * PC, PC), PC), :].reshape(PC * PC, 128)
        for third in range(3):
            cz = half + third
            place = place_ref[ax * 6 + cz]
            row_x = spline_row(place[0:1])
            row_y = spline_row(place[1:2])
            row_z = spline_row(place[2:3])
            right = jnp.where(block == cz + 1, jnp.tile(row_z, (8, 1)), 0.0).astype(bf16)
            partial = dot(field, right)
            left = (row_y[:, None, :] * row_x[None, :, :]).reshape(PC * PC, 128)
            out_ref[pl.ds(ax * 6 + cz, 1), :] = (
                jnp.sum(partial * left, axis=0, keepdims=True) * field_scale
            )
        return carry

    lax.fori_loop(0, 8, gather, 0)
    own_ref[0:4, :] = out_ref[7:11, :]
    own_ref[4:8, :] = out_ref[13:17, :]
    for copy in copies:
        copy.wait()


def interpolate(field, place, weights, slopes, field_scale):
    return pl.pallas_call(
        functools.partial(interpolate_kernel, field_scale),
        in_specs=[VM] * 2 + [ANY] * 4,
        out_specs=[VM] * 4,
        compiler_params=FIELD,
        out_shape=[
            jax.ShapeDtypeStruct((24, 128), f32),
            jax.ShapeDtypeStruct((8, 128), f32),
            jax.ShapeDtypeStruct((6, 8, 128, 256), bf16),
            jax.ShapeDtypeStruct((3, 4, 6, 128, 128), bf16),
        ],
        scratch_shapes=[pltpu.SemaphoreType.DMA((4,))],
        cost_estimate=pl.CostEstimate(
            flops=24 * 2 * 256 * 128 * 128, bytes_accessed=400000, transcendentals=0
        ),
        name="interpolate",
    )(field, place, weights, *slopes)


def combination_of(t):
    return jnp.where(t < 4, 1 + t // 2, 3 * (t - 4)), t % 2


def scaled(columns, cell, slope):
    return (columns[:, cell : cell + 1] * slope.astype(f32)).astype(bf16)


def beside_kernel(
    stored_ref, weight_ref, slope_ref, potential_ref, rest_ref, total_ref, own_out, near_ref, sems
):
    copies = [
        pltpu.make_async_copy(
            stored_ref.at[pl.ds(i, 3), :, :, pl.ds(0, 512)], rest_ref.at[pl.ds(i, 3)], sems.at[i // 3]
        )
        for i in (0, 3)
    ]
    for copy in copies:
        copy.start()
    columns = jnp.transpose(potential_ref[...])
    for x in range(4):
        for z in range(6):
            near_ref[x, z] = scaled(columns, x * 6 + z, slope_ref[1, x, z])
    own_out[...] = near_ref[1:3, 1:5]
    total_ref[...] = jnp.zeros_like(total_ref)

    def combination(t, carry):
        x, a = combination_of(t)
        for pair, (start, stop, first, width) in enumerate(SPANS):
            part = dot(
                weight_ref[t, start:stop].reshape(width * 128, 256),
                near_ref[x, 2 * pair : 2 * pair + 2].reshape(256, 128),
            )
            total_ref[a, first : first + width] += part.reshape(width, 128, 128)
        return carry

    lax.fori_loop(0, 6, combination, 0)
    for copy in copies:
        copy.wait()


def beside(stored, weights, slopes, potential):
    return pl.pallas_call(
        beside_kernel,
        in_specs=[ANY] + [VM] * 3,
        out_specs=[VM] * 3,
        out_shape=[
            jax.ShapeDtypeStruct((6, 8, 128, 512), bf16),
            jax.ShapeDtypeStruct((2, 4, 128, 128), f32),
            jax.ShapeDtypeStruct((2, 4, 128, 128), bf16),
        ],
        scratch_shapes=[
            pltpu.VMEM((4, 6, 128, 128), bf16),
            pltpu.SemaphoreType.DMA((2,)),
        ],
        cost_estimate=pl.CostEstimate(
            flops=3000000000, bytes_accessed=12000000, transcendentals=0
        ),
        compiler_params=MIDDLE,
        name="beside",
    )(stored, weights, slopes, potential)


def backward_kernel(
    weight_ref, slope_ref, part_ref, own_ref, below_ref, above_ref, msg_ref, self_ref, out_ref,
    near_ref, total_ref, potential_ref
):
    potential_ref[0] = below_ref[...]
    potential_ref[1] = above_ref[...]

    def scale(side, carry):
        columns = jnp.transpose(potential_ref[side])
        for x in range(4):
            for z in range(6):
                near_ref[side, x, z] = scaled(columns, x * 6 + z, slope_ref[2 * side, x, z])
        return carry

    lax.fori_loop(0, 2, scale, 0)
    total_ref[...] = part_ref[...]

    def combination(t, carry):
        x, a = combination_of(t)
        for pair, (start, stop, first, width) in enumerate(SPANS):
            near = jnp.concatenate(
                [
                    near_ref[side, x, 2 * pair : 2 * pair + 2].reshape(256, 128)
                    for side in range(2)
                ],
                axis=0,
            )
            part = dot(weight_ref[t, start:stop].reshape(width * 128, 512), near)
            total_ref[a, first : first + width] += part.reshape(width, 128, 128)
        return carry

    lax.fori_loop(0, 6, combination, 0)

    def finish(a, carry):
        back = total_ref[a].reshape(512, 128).astype(bf16)
        own = own_ref[a].reshape(512, 128)
        out_ref[a] = (dot_t(back, msg_ref[...]) + dot_t(own, self_ref[...])).reshape(4, 128, 128)
        return carry

    lax.fori_loop(0, 2, finish, 0)


def backward(weights, slope, part, own, below, above, msg_weight, self_weight):
    return pl.pallas_call(
        backward_kernel,
        in_specs=[VM] * 8,
        out_specs=VM,
        out_shape=jax.ShapeDtypeStruct((2, 4, 128, 128), f32),
        scratch_shapes=[
            pltpu.VMEM((2, 4, 6, 128, 128), bf16),
            pltpu.VMEM((2, 4, 128, 128), f32),
            pltpu.VMEM((2, 24, 128), f32),
        ],
        cost_estimate=pl.CostEstimate(
            flops=4000000000, bytes_accessed=12000000, transcendentals=0
        ),
        compiler_params=SMALL,
        name="backward",
    )(weights, slope, part, own, below, above, msg_weight, self_weight)


def wave_tables(size_x, size_y, size_z):
    i16 = np.arange(16)
    points_x = np.array([g * 32 + a * 16 + i for a in range(2) for g in range(4) for i in i16])
    along_x = cas(np.arange(size_x), points_x, size_x)
    points_y = np.array(
        [gy * 16 + gx * 4 + gz for gx in range(4) for gy in range(16) for gz in range(4)]
    )
    into_y = cas(np.arange(size_y), points_y, size_y)
    back_x = np.array(
        [((2 * g - 1 + a) % 8) * 16 + i for g in range(4) for a in range(4) for i in i16]
    )
    back_z = np.array(
        [((4 * g - 2 + c) % 16) * 16 + k for g in range(4) for c in range(8) for k in i16]
    )
    tables = (
        cas(np.arange(size_z), np.arange(size_z), size_z),
        along_x,
        into_y,
        cas(back_x, np.arange(size_x), size_x),
        cas(np.arange(size_z), back_z, size_z),
    )
    return [jnp.asarray(np.ascontiguousarray(t), dtype=bf16) for t in tables]


def influence_of(size_x, size_y, size_z):
    device = lax.axis_index(everyone)

    def wave(index, size):
        signed = jnp.where(2 * index >= size, index - size, index)
        return signed.astype(f32) * (PC / size)

    wave_x = wave(device % size_x, size_x)
    wave_y = wave(jnp.arange(size_y, dtype=jnp.int32), size_y)[:, None]
    wave_z = wave(
        device // size_x * 128 + jnp.arange(size_z // 2, dtype=jnp.int32), size_z
    )[None, :]
    squared = wave_x * wave_x + wave_y * wave_y + wave_z * wave_z
    safe = jnp.where(squared > 0, squared, 1.0)
    return jnp.where(squared > 0, jnp.exp(-((math.pi * spread_width) ** 2) * squared) / safe, 0.0)


def swapped(value, axis):
    return lax.all_to_all(value, axis, split_axis=0, concat_axis=0, tiled=True)


def body(features, msg_weight, self_weight, charge_weight, spline_corner, spline_fraction):
    cells_x, cells_y, cells_z, slots, width = features.shape
    size_x = cells_x * PC * lax.axis_size("gx")
    size_y = cells_y * PC * lax.axis_size("gy")
    size_z = cells_z * PC * lax.axis_size("gz")
    volume = size_x // PC * (size_y // PC) * (size_z // PC)
    natoms = volume * slots
    cells = cells_x * cells_z

    features_own = features.reshape(cells, slots, width)
    own = project(
        features_own, msg_weight, spline_corner.swapaxes(2, 3), spline_fraction.swapaxes(2, 3)
    )
    own = own.reshape(cells_x, cells_z, slots + 16, width)
    sides, ends, outer, corners = early_halo(own)
    weights, part = inside_pairs(own, sides, features_own, self_weight)
    weights, part = ends_pairs(own, sides, ends, outer, part, weights)
    influence = influence_of(size_x, size_y, size_z)
    along_z, along_x, into_y, back_x, back_z = wave_tables(size_x, size_y, size_z)

    read = charge_weight[None, :]
    weights, preact, mesh, row_place = message_layer(
        own, ends, outer, corners, part, read, weights
    )
    slope = slope_of(preact, read)
    left, right = moved(slope[:, cells_z - 1 :], "gz", 1), moved(slope[:, :1], "gz", -1)
    mesh, left, right = lax.optimization_barrier((swapped(mesh, plane), left, right))
    row = jnp.concatenate([left, slope, right], axis=1)
    waves = forward_xz(mesh.reshape(4, 4, PC, 128), along_z, along_x)
    waves, row = lax.optimization_barrier((waves, row))
    below = [moved(part, "gy", 1) for part in (row[:1], row[1:])]
    above = [moved(part, "gy", -1) for part in (row[:1], row[1:])]
    lines, *parts = lax.optimization_barrier((swapped(waves, everyone), *below, *above))
    below, above = jnp.concatenate(parts[:2]), jnp.concatenate(parts[2:])
    rows = jnp.stack([below, row, above])
    before, after = moved(rows[:, cells_x - 1 :], "gx", 1), moved(rows[:, :1], "gx", -1)
    lines = swapped(filter_y(lines, into_y, influence), everyone)
    field, energy = inverse_xz(lines, back_x, back_z, coupling / (2.0 * volume * natoms))
    field = swapped(field.reshape(16, 64, 128), plane)
    potential, atom_potential, own_weights, slopes = interpolate(
        field, row_place.reshape(24, 8, slots), weights, (rows, before, after), coupling / volume
    )
    below, above = moved(potential, "gy", 1), moved(potential, "gy", -1)
    weights, total, cotangent = beside(weights, own_weights, slopes, potential)
    grad = backward(weights, slopes, total, cotangent, below, above, msg_weight, self_weight)
    return (
        grad.reshape(features.shape),
        atom_potential.reshape(cells_x, cells_y, cells_z, slots),
        energy[0, 0],
    )


def solution(mesh):
    in_specs = (
        P("gx", "gy", "gz", None, None),
        P(),
        P(),
        P(),
        P("gx", "gy", "gz", None, None),
        P("gx", "gy", "gz", None, None),
    )
    out_specs = (P("gx", "gy", "gz", None, None), P("gx", "gy", "gz", None), P())
    return jax.shard_map(body, mesh=mesh, in_specs=in_specs, out_specs=out_specs, check_vma=False)
```

```python
import functools
import math

import jax
import jax.numpy as jnp
import numpy as np
from jax import lax
from jax.experimental import pallas as pl
from jax.experimental.pallas import tpu as pltpu
from jax.sharding import PartitionSpec as P

PC = 16
pair_scale = 0.1
coupling = 0.125
spread_width = 0.0625
f32 = jnp.float32
bf16 = jnp.bfloat16
plane = ("gx", "gz")
everyone = ("gx", "gy", "gz")


def dot(a, b):
    return jnp.dot(a, b, preferred_element_type=f32)


def dot_t(a, b, precision=None):
    return lax.dot_general(
        a, b, (((1,), (1,)), ((), ())), preferred_element_type=f32, precision=precision
    )


def whole(shape):
    zeros = (0,) * len(shape)
    return pl.BlockSpec(shape, lambda *_: zeros)


VM = pl.BlockSpec(memory_space=pltpu.VMEM)
ANY = pl.BlockSpec(memory_space=pl.ANY)
SMALL = pltpu.CompilerParams(vmem_limit_bytes=20 << 20)
FIRST = pltpu.CompilerParams(vmem_limit_bytes=60 << 20)
LARGE = pltpu.CompilerParams(vmem_limit_bytes=50 << 20)
MIDDLE = pltpu.CompilerParams(vmem_limit_bytes=40 << 20)
FIELD = pltpu.CompilerParams(vmem_limit_bytes=44 << 20)


def cas(rows, columns, size):
    turns = np.outer(rows, columns) % size
    angle = 2.0 * np.pi / size * turns
    return np.cos(angle) + np.sin(angle)


def moved(value, axis, step):
    count = lax.axis_size(axis)
    pairs = [(i, (i + step) % count) for i in range(count)]
    return lax.ppermute(value.reshape(-1, 128), axis, pairs).reshape(value.shape)


def late_halo(own):
    last_x, last_z = own.shape[0] - 1, own.shape[1] - 1
    left, right = moved(own[:, last_z:], "gz", 1), moved(own[:, :1], "gz", -1)
    row = jnp.concatenate([left, own, right], axis=1)
    rows = jnp.stack([moved(row, "gy", 1), row, moved(row, "gy", -1)])
    return [rows, moved(rows[:, last_x:], "gx", 1), moved(rows[:, :1], "gx", -1)]


def early_halo(own):
    last_x, last_z = own.shape[0] - 1, own.shape[1] - 1
    below, above = moved(own, "gy", 1), moved(own, "gy", -1)
    beside = [moved(own[last_x:], "gx", 1), moved(own[:1], "gx", -1)]
    sides = jnp.stack([below, above])
    rows = [below, own, above]
    left = moved(jnp.stack([row[:, last_z:] for row in rows]), "gz", 1)
    right = moved(jnp.stack([row[:, :1] for row in rows]), "gz", -1)
    aside = [moved(sides[:, last_x:], "gx", 1), moved(sides[:, :1], "gx", -1)]
    corners = [
        moved(jnp.concatenate([left[:, at : at + 1], right[:, at : at + 1]], axis=2), "gx", step)
        for at, step in ((last_x, 1), (0, -1))
    ]
    return [below, above], [left, right], beside + aside, corners


def project_kernel(features_ref, weight_ref, corner_ref, fraction_ref, out_ref):
    value = dot(features_ref[...].reshape(1024, 128), weight_ref[...]).astype(bf16)
    out_ref[:, :128, :] = value.reshape(8, 128, 128)
    none = jnp.zeros((5, 128), f32)
    for x in range(2):
        place = corner_ref[x, 0].astype(f32) + 1.0 + fraction_ref[x, 0]
        high = place.astype(bf16).astype(f32)
        rest = place - high
        middle = rest.astype(bf16).astype(f32)
        low = rest - middle
        for z in range(4):
            rows = [part[d, z : z + 1] for part in (high, low) for d in range(3)]
            rows += [none[:2]] + [middle[d, z : z + 1] for d in range(3)] + [none]
            out_ref[x * 4 + z, 128:, :] = jnp.concatenate(rows, axis=0).astype(bf16)


def project(features, weight, corner, fraction):
    return pl.pallas_call(
        project_kernel,
        grid=(1,),
        in_specs=[whole((8, 128, 128)), whole((128, 128))]
        + [whole((2, 1, 3, 4, 128))] * 2,
        out_specs=whole((8, 144, 128)),
        out_shape=jax.ShapeDtypeStruct((8, 144, 128), bf16),
        compiler_params=FIRST,
        name="project",
    )(features, weight, corner, fraction)


def place_of(rows):
    rows = rows.astype(f32)
    return rows[0:8] + rows[8:16] + pltpu.roll(rows[0:8], 5, 0)


BLOCKS = ((0, 0), (0, 1), (1, 0), (1, 1), (1, 2), (1, 3), (2, 2), (2, 3))
SPANS = ((0, 2, 0, 2), (2, 6, 0, 4), (6, 8, 2, 2))
ORDER_Y = (0, 2, 1)


def position_of(rows):
    return (place_of(rows) * (1.0 / PC)).astype(bf16).astype(f32)


def weigh(centres, a, shift, near, store, pairs):
    for c in range(4):
        columns = jnp.transpose(centres[a, c])
        centre_x = jnp.broadcast_to(columns[:, 0:1], (128, 128))
        centre_y = jnp.broadcast_to(columns[:, 1:2], (128, 128))
        centre_z = jnp.broadcast_to(columns[:, 2:3], (128, 128))
        for block, (pair, owner) in enumerate(BLOCKS):
            if owner != c or pair not in pairs:
                continue
            for at, dy in enumerate(ORDER_Y):
                for half in range(2):
                    dz = 2 * pair + half - c - 1
                    if abs(dz) > 1:
                        tile = jnp.zeros((128, 128), bf16)
                    else:
                        row = near(dy, 2 * pair + half)
                        gap_x = (row[0:1] + shift) - centre_x
                        gap_y = (row[1:2] + (dy - 1.0)) - centre_y
                        gap_z = (row[2:3] + float(dz)) - centre_z
                        squared = gap_x * gap_x + gap_y * gap_y + gap_z * gap_z
                        inside = jnp.maximum(1.0 - squared, 0.0)
                        tile = (pair_scale * inside * inside).astype(bf16)
                    store(block, (at * 2 + half) * 128, tile)


def add_near(weight_ref, t, a, cell, total_ref, pairs):
    for pair in pairs:
        start, stop, first, width = SPANS[pair]
        near = jnp.concatenate(
            [cell(dy, 2 * pair + half)[0:128, :] for dy in ORDER_Y for half in range(2)], axis=0
        )
        part = dot(weight_ref[t, start:stop].reshape(width * 128, 768), near)
        total_ref[a, first : first + width] += part.reshape(width, 128, 128)


def columns_kernel(first, count, weight_ref, weight_out, sems, slot, spans):
    return [
        pltpu.make_async_copy(
            weight_ref.at[pl.ds(first, count), pl.ds(start, size)],
            weight_out.at[pl.ds(first, count), pl.ds(start, size)],
            sems.at[slot + i],
        )
        for i, (start, size) in enumerate(spans)
    ]


INSIDE = (1,)
ENDS = (0, 2)
INSIDE_BLOCKS = ((2, 4),)
END_BLOCKS = ((0, 2), (6, 2))


def centres_of(own_ref, centre_ref):
    def one(cell, carry):
        x, z = cell // 4, cell % 4
        centre_ref[x, z] = position_of(own_ref[x, z, 128:144, :])
        return carry

    lax.fori_loop(0, 8, one, 0)


def inside_kernel(
    own_ref, below_ref, above_ref, features_ref, self_ref,
    weight_out, total_ref, weight_ref, position_ref, sems
):
    refs = (below_ref, own_ref, above_ref)

    def positions(x, carry):
        for dy in range(3):
            for z in range(4):
                position_ref[dy, x, z] = position_of(refs[dy][x, z, 128:144, :])
        return carry

    lax.fori_loop(0, 2, positions, 0)
    total_ref[...] = dot(features_ref[...].reshape(1024, 128), self_ref[...]).reshape(
        2, 4, 128, 128
    )

    def column(t, carry):
        x, a = t // 2, t % 2

        def store(block, lane, tile):
            weight_ref[t, block, :, lane : lane + 128] = tile

        def near(dy, z):
            return position_ref[dy, x, z - 1]

        weigh(position_ref.at[1], a, (x - a).astype(f32), near, store, INSIDE)
        add_near(weight_ref, t, a, lambda dy, z: refs[dy].at[x, z - 1], total_ref, INSIDE)
        return carry

    lax.fori_loop(0, 4, column, 0)
    copies = columns_kernel(0, 4, weight_ref, weight_out, sems, 0, INSIDE_BLOCKS)
    for copy in copies:
        copy.start()
    for copy in copies:
        copy.wait()


def inside_pairs(own, sides, features, self_weight):
    return pl.pallas_call(
        inside_kernel,
        in_specs=[VM] * 5,
        out_specs=[ANY, VM],
        out_shape=[
            jax.ShapeDtypeStruct((6, 8, 128, 768), bf16),
            jax.ShapeDtypeStruct((2, 4, 128, 128), f32),
        ],
        scratch_shapes=[
            pltpu.VMEM((4, 8, 128, 768), bf16),
            pltpu.VMEM((3, 2, 4, 8, 128), f32),
            pltpu.SemaphoreType.DMA((1,)),
        ],
        cost_estimate=pl.CostEstimate(
            flops=5000000000, bytes_accessed=9000000, transcendentals=0
        ),
        compiler_params=LARGE,
        name="inside_pairs",
    )(own, *sides, features, self_weight)


def ends_kernel(
    own_ref, below_ref, above_ref, left_ref, right_ref,
    part_ref, _, weight_out, total_ref, weight_ref, centre_ref, position_ref, sems
):
    refs = (below_ref, own_ref, above_ref)

    def cell(dy, x, z):
        if z == 0:
            return left_ref.at[dy, x, 0]
        if z == 5:
            return right_ref.at[dy, x, 0]
        return refs[dy].at[x, z - 1]

    centres_of(own_ref, centre_ref)

    def positions(x, carry):
        for dy in range(3):
            for z in (0, 1, 4, 5):
                position_ref[dy, x, z] = position_of(cell(dy, x, z)[128:144, :])
        return carry

    lax.fori_loop(0, 2, positions, 0)
    total_ref[...] = part_ref[...]

    def column(t, carry):
        x, a = t // 2, t % 2

        def store(block, lane, tile):
            weight_ref[t, block, :, lane : lane + 128] = tile

        def near(dy, z):
            return position_ref[dy, x, z]

        weigh(centre_ref, a, (x - a).astype(f32), near, store, ENDS)
        add_near(weight_ref, t, a, lambda dy, z: cell(dy, x, z), total_ref, ENDS)
        return carry

    lax.fori_loop(0, 4, column, 0)
    copies = columns_kernel(0, 4, weight_ref, weight_out, sems, 0, END_BLOCKS)
    for copy in copies:
        copy.start()

    for copy in copies:
        copy.wait()


def ends_pairs(own, sides, ends, part, weights):
    return pl.pallas_call(
        ends_kernel,
        in_specs=[VM] * 6 + [ANY],
        out_specs=[ANY, VM],
        input_output_aliases={6: 0},
        out_shape=[
            jax.ShapeDtypeStruct((6, 8, 128, 768), bf16),
            jax.ShapeDtypeStruct((2, 4, 128, 128), f32),
        ],
        scratch_shapes=[
            pltpu.VMEM((4, 8, 128, 768), bf16),
            pltpu.VMEM((2, 4, 8, 128), f32),
            pltpu.VMEM((3, 2, 6, 8, 128), f32),
            pltpu.SemaphoreType.DMA((2,)),
        ],
        cost_estimate=pl.CostEstimate(
            flops=6000000000, bytes_accessed=9000000, transcendentals=0
        ),
        compiler_params=LARGE,
        name="ends_pairs",
    )(own, *sides, *ends, part, weights)


def spline_row(place):
    point = lax.broadcasted_iota(jnp.int32, (PC, 128), 0).astype(f32)
    away = jnp.abs(point - place)
    near = (4.0 - 6.0 * away * away + 3.0 * away * away * away) * (1.0 / 6.0)
    rest = 2.0 - away
    far = rest * rest * rest * (1.0 / 6.0)
    return jnp.where(away < 1.0, near, jnp.where(away < 2.0, far, 0.0))


def message_kernel(
    own_ref, left_ref, right_ref, before_own, after_own, before_side, after_side, before_end,
    after_end, part_ref, read_ref, _,
    weight_out, total_ref, mesh_ref, row_place_ref,
    weight_ref, position_ref, centre_ref, high_ref, low_ref, charge_ref, left_rows, right_rows, sems
):
    refs = ((before_own, before_side, before_end), (after_own, after_side, after_end))

    def cell(side, dy, z):
        own, beside, end = refs[side]
        if z in (0, 5):
            return end.at[dy, 0, z // 5]
        return own.at[0, z - 1] if dy == 1 else beside.at[dy // 2, 0, z - 1]

    centres_of(own_ref, centre_ref)
    for side in range(2):
        for dy in range(3):
            for z in range(6):
                position_ref[side, dy, z] = position_of(cell(side, dy, z)[128:144, :])
        for z in range(6):
            row_place_ref[3 * side, z] = place_of(cell(side, 1, z)[128:144, :])

    def row_places(x, carry):
        row_place_ref[1 + x, 0] = place_of(left_ref[1, x, 0, 128:144, :])
        for z in range(4):
            row_place_ref[1 + x, 1 + z] = place_of(own_ref[x, z, 128:144, :])
        row_place_ref[1 + x, 5] = place_of(right_ref[1, x, 0, 128:144, :])
        return carry

    lax.fori_loop(0, 2, row_places, 0)

    def column(side, carry):
        def store(block, lane, tile):
            weight_ref[side, block, :, lane : lane + 128] = tile

        def near(dy, z):
            return position_ref[side, dy, z]

        weigh(centre_ref, side, (2 * side - 1).astype(f32), near, store, ENDS + INSIDE)
        return carry

    lax.fori_loop(0, 2, column, 0)
    copies = [pltpu.make_async_copy(weight_ref, weight_out.at[pl.ds(4, 2)], sems.at[0])]
    for copy in copies:
        copy.start()
    total_ref[...] = part_ref[...]
    for side in range(2):
        add_near(
            weight_ref, side, side, lambda dy, z: cell(side, dy, z), total_ref, ENDS + INSIDE
        )

    def finish(index, carry):
        preact = total_ref[index // 4, index % 4]
        silu = preact * (0.5 + 0.5 * jnp.tanh(0.5 * preact))
        high = silu.astype(bf16)
        high_ref[index] = high
        low_ref[index] = (silu - high.astype(f32)).astype(bf16)
        return carry

    lax.fori_loop(0, 8, finish, 0, unroll=2)
    wide = jnp.broadcast_to(read_ref[...], (16, 128))
    charge_ref[...] = dot_t(wide, high_ref[...].reshape(1024, 128)) + dot_t(
        wide, low_ref[...].reshape(1024, 128)
    )
    block = lax.broadcasted_iota(jnp.int32, (128, 128), 0) // PC

    def spread(cell, carry):
        lanes = pl.ds(pl.multiple_of(cell * 128, 128), 128)
        place = row_place_ref[1 + cell // 4, 1 + cell % 4]
        row_x = spline_row(place[0:1])
        row_y = spline_row(place[1:2]) * charge_ref[0:1, lanes]
        row_z = spline_row(place[2:3])
        left_rows[:, lanes] = (
            (row_y[:, None, :] * row_x[None, :, :]).reshape(PC * PC, 128).astype(bf16)
        )
        right_rows[:, lanes] = jnp.where(block == cell, jnp.tile(row_z, (8, 1)), 0.0).astype(bf16)
        return carry

    lax.fori_loop(0, 8, spread, 0)
    mesh_ref[...] = dot_t(left_rows[...], right_rows[...]).reshape(PC, PC, 128).astype(bf16)
    for copy in copies:
        copy.wait()


def message_layer(own, ends, outer, corners, part, read, weights):
    return pl.pallas_call(
        message_kernel,
        in_specs=[VM] * 11 + [ANY],
        out_specs=[ANY, VM, VM, VM],
        input_output_aliases={11: 0},
        out_shape=[
            jax.ShapeDtypeStruct((6, 8, 128, 768), bf16),
            jax.ShapeDtypeStruct((2, 4, 128, 128), f32),
            jax.ShapeDtypeStruct((PC, PC, 128), bf16),
            jax.ShapeDtypeStruct((4, 6, 8, 128), f32),
        ],
        scratch_shapes=[
            pltpu.VMEM((2, 8, 128, 768), bf16),
            pltpu.VMEM((2, 3, 6, 8, 128), f32),
            pltpu.VMEM((2, 4, 8, 128), f32),
            pltpu.VMEM((8, 128, 128), bf16),
            pltpu.VMEM((8, 128, 128), bf16),
            pltpu.VMEM((16, 1024), f32),
            pltpu.VMEM((PC * PC, 1024), bf16),
            pltpu.VMEM((128, 1024), bf16),
            pltpu.SemaphoreType.DMA((1,)),
        ],
        cost_estimate=pl.CostEstimate(
            flops=5000000000, bytes_accessed=6000000, transcendentals=8 * 16384
        ),
        compiler_params=LARGE,
        name="message",
    )(own, *ends, *outer, *corners, part, read, weights)


def slope_kernel(total_ref, read_ref, out_ref):
    read = read_ref[...].astype(f32)

    def one(index, carry):
        a, c = index // 4, index % 4
        preact = total_ref[a, c]
        sigma = 0.5 + 0.5 * jnp.tanh(0.5 * preact)
        out_ref[a, c] = (read * (sigma * (1.0 + preact * (1.0 - sigma)))).astype(bf16)
        return carry

    lax.fori_loop(0, 8, one, 0, unroll=2)


def slope_of(total, read):
    return pl.pallas_call(
        slope_kernel,
        in_specs=[VM] * 2,
        out_specs=VM,
        out_shape=jax.ShapeDtypeStruct(total.shape, bf16),
        cost_estimate=pl.CostEstimate(
            flops=8 * 16384 * 8, bytes_accessed=900000, transcendentals=8 * 16384
        ),
        compiler_params=SMALL,
        name="slope",
    )(total, read)


def forward_kernel(mesh_ref, along_z_ref, along_x_ref, out_ref):
    lane = lax.broadcasted_iota(jnp.int32, (64, 128), 1)
    total = jnp.zeros((128, 256), f32)
    for g in range(4):
        mesh = mesh_ref[:, g].reshape(64, 128)
        none = jnp.zeros_like(mesh)
        halves = jnp.concatenate(
            [jnp.where(lane < 64, mesh, none), jnp.where(lane < 64, none, mesh)], axis=0
        )
        table = along_z_ref[g * 64 : (g + 1) * 64, :]
        total = total + dot(halves, jnp.concatenate([table, table], axis=0))
    lines = total.astype(bf16)
    waves = dot(along_x_ref[...], lines)
    out_ref[0:128, :] = waves[:, :128]
    out_ref[128:256, :] = waves[:, 128:]


def forward_xz(mesh, along_z, along_x):
    return pl.pallas_call(
        forward_kernel,
        in_specs=[VM] * 3,
        out_specs=VM,
        compiler_params=SMALL,
        out_shape=jax.ShapeDtypeStruct((256, 128), f32),
        cost_estimate=pl.CostEstimate(
            flops=2 * 64 * 512 * 512, bytes_accessed=800000, transcendentals=0
        ),
        name="forward_xz",
    )(mesh, along_z, along_x)


def filter_kernel(lines_ref, into_ref, influence_ref, out_ref):
    waves = dot(into_ref[...], lines_ref[...].astype(bf16))
    scaled = influence_ref[...] * waves
    power = jnp.sum(jnp.sum(scaled * waves, axis=0, keepdims=True), axis=1, keepdims=True)
    out_ref[pl.ds(0, 256, stride=2), :] = lax.dot_general(
        into_ref[...],
        scaled.astype(bf16),
        (((0,), (0,)), ((), ())),
        preferred_element_type=f32,
    )
    out_ref[pl.ds(1, 256, stride=2), :] = jnp.broadcast_to(power, (256, 128))


def filter_y(lines, into, influence):
    return pl.pallas_call(
        filter_kernel,
        in_specs=[VM] * 3,
        out_specs=VM,
        compiler_params=SMALL,
        out_shape=jax.ShapeDtypeStruct((512, 128), f32),
        cost_estimate=pl.CostEstimate(
            flops=4 * 256 * 256 * 128, bytes_accessed=700000, transcendentals=0
        ),
        name="filter_y",
    )(lines, into, influence)


def inverse_kernel(energy_scale, lines_ref, along_x_ref, along_z_ref, out_ref, energy_ref):
    waves = jnp.concatenate(
        [lines_ref[pl.ds(0, 128, stride=2), :], lines_ref[pl.ds(256, 128, stride=2), :]], axis=1
    ).astype(bf16)
    half = dot(along_x_ref[...], waves).astype(bf16)
    field = dot(half, along_z_ref[...]).astype(bf16)
    for gx in range(4):
        for gz in range(4):
            out_ref[gx, gz] = field[gx * 64 : (gx + 1) * 64, gz * 128 : (gz + 1) * 128]
    power = jnp.sum(lines_ref[pl.ds(1, 256, stride=2), :], axis=0, keepdims=True)
    energy_ref[...] = jnp.broadcast_to(power * energy_scale, (8, 128))


def inverse_xz(lines, along_x, along_z, energy_scale):
    return pl.pallas_call(
        functools.partial(inverse_kernel, energy_scale),
        in_specs=[VM] * 3,
        out_specs=[VM, VM],
        compiler_params=SMALL,
        out_shape=[
            jax.ShapeDtypeStruct((4, 4, 64, 128), bf16),
            jax.ShapeDtypeStruct((8, 128), f32),
        ],
        cost_estimate=pl.CostEstimate(
            flops=2 * 256 * 256 * 640, bytes_accessed=900000, transcendentals=0
        ),
        name="inverse_xz",
    )(lines, along_x, along_z)


def interpolate_kernel(
    field_scale, field_ref, place_ref, stored_ref, rows_ref, before_ref, after_ref,
    out_ref, own_ref, weight_ref, slope_ref, sems
):
    pairs = [
        (rows_ref, slope_ref.at[:, pl.ds(1, 2)]),
        (before_ref, slope_ref.at[:, pl.ds(0, 1)]),
        (after_ref, slope_ref.at[:, pl.ds(3, 1)]),
        (stored_ref.at[:, :, :, pl.ds(512, 256)], weight_ref),
    ]
    copies = [
        pltpu.make_async_copy(source, target, sems.at[i])
        for i, (source, target) in enumerate(pairs)
    ]
    for copy in copies:
        copy.start()
    block = lax.broadcasted_iota(jnp.int32, (128, 128), 0) // PC

    def gather(step, carry):
        ax, half = step // 2, 3 * (step % 2)
        field = field_ref[:, pl.ds(pl.multiple_of(ax * PC, PC), PC), :].reshape(PC * PC, 128)
        for third in range(3):
            cz = half + third
            place = place_ref[ax * 6 + cz]
            row_x = spline_row(place[0:1])
            row_y = spline_row(place[1:2])
            row_z = spline_row(place[2:3])
            right = jnp.where(block == cz + 1, jnp.tile(row_z, (8, 1)), 0.0).astype(bf16)
            partial = dot(field, right)
            left = (row_y[:, None, :] * row_x[None, :, :]).reshape(PC * PC, 128)
            out_ref[pl.ds(ax * 6 + cz, 1), :] = (
                jnp.sum(partial * left, axis=0, keepdims=True) * field_scale
            )
        return carry

    lax.fori_loop(0, 8, gather, 0)
    own_ref[0:4, :] = out_ref[7:11, :]
    own_ref[4:8, :] = out_ref[13:17, :]
    for copy in copies:
        copy.wait()


def interpolate(field, place, weights, slopes, field_scale):
    return pl.pallas_call(
        functools.partial(interpolate_kernel, field_scale),
        in_specs=[VM] * 2 + [ANY] * 4,
        out_specs=[VM] * 4,
        compiler_params=FIELD,
        out_shape=[
            jax.ShapeDtypeStruct((24, 128), f32),
            jax.ShapeDtypeStruct((8, 128), f32),
            jax.ShapeDtypeStruct((6, 8, 128, 256), bf16),
            jax.ShapeDtypeStruct((3, 4, 6, 128, 128), bf16),
        ],
        scratch_shapes=[pltpu.SemaphoreType.DMA((4,))],
        cost_estimate=pl.CostEstimate(
            flops=24 * 2 * 256 * 128 * 128, bytes_accessed=400000, transcendentals=0
        ),
        name="interpolate",
    )(field, place, weights, *slopes)


def combination_of(t):
    return jnp.where(t < 4, 1 + t // 2, 3 * (t - 4)), t % 2


def scaled(columns, cell, slope):
    return (columns[:, cell : cell + 1] * slope.astype(f32)).astype(bf16)


def beside_kernel(
    stored_ref, weight_ref, slope_ref, potential_ref, rest_ref, total_ref, own_out, near_ref, sems
):
    copies = [
        pltpu.make_async_copy(
            stored_ref.at[pl.ds(i, 3), :, :, pl.ds(0, 512)], rest_ref.at[pl.ds(i, 3)], sems.at[i // 3]
        )
        for i in (0, 3)
    ]
    for copy in copies:
        copy.start()
    columns = jnp.transpose(potential_ref[...])
    for x in range(4):
        for z in range(6):
            near_ref[x, z] = scaled(columns, x * 6 + z, slope_ref[1, x, z])
    own_out[...] = near_ref[1:3, 1:5]
    total_ref[...] = jnp.zeros_like(total_ref)

    def combination(t, carry):
        x, a = combination_of(t)
        for pair, (start, stop, first, width) in enumerate(SPANS):
            part = dot(
                weight_ref[t, start:stop].reshape(width * 128, 256),
                near_ref[x, 2 * pair : 2 * pair + 2].reshape(256, 128),
            )
            total_ref[a, first : first + width] += part.reshape(width, 128, 128)
        return carry

    lax.fori_loop(0, 6, combination, 0)
    for copy in copies:
        copy.wait()


def beside(stored, weights, slopes, potential):
    return pl.pallas_call(
        beside_kernel,
        in_specs=[ANY] + [VM] * 3,
        out_specs=[VM] * 3,
        out_shape=[
            jax.ShapeDtypeStruct((6, 8, 128, 512), bf16),
            jax.ShapeDtypeStruct((2, 4, 128, 128), f32),
            jax.ShapeDtypeStruct((2, 4, 128, 128), bf16),
        ],
        scratch_shapes=[
            pltpu.VMEM((4, 6, 128, 128), bf16),
            pltpu.SemaphoreType.DMA((2,)),
        ],
        cost_estimate=pl.CostEstimate(
            flops=3000000000, bytes_accessed=12000000, transcendentals=0
        ),
        compiler_params=MIDDLE,
        name="beside",
    )(stored, weights, slopes, potential)


def backward_kernel(
    weight_ref, slope_ref, part_ref, own_ref, below_ref, above_ref, msg_ref, self_ref, out_ref,
    near_ref, total_ref, potential_ref
):
    potential_ref[0] = below_ref[...]
    potential_ref[1] = above_ref[...]

    def scale(side, carry):
        columns = jnp.transpose(potential_ref[side])
        for x in range(4):
            for z in range(6):
                near_ref[side, x, z] = scaled(columns, x * 6 + z, slope_ref[2 * side, x, z])
        return carry

    lax.fori_loop(0, 2, scale, 0)
    total_ref[...] = part_ref[...]

    def combination(t, carry):
        x, a = combination_of(t)
        for pair, (start, stop, first, width) in enumerate(SPANS):
            near = jnp.concatenate(
                [
                    near_ref[side, x, 2 * pair : 2 * pair + 2].reshape(256, 128)
                    for side in range(2)
                ],
                axis=0,
            )
            part = dot(weight_ref[t, start:stop].reshape(width * 128, 512), near)
            total_ref[a, first : first + width] += part.reshape(width, 128, 128)
        return carry

    lax.fori_loop(0, 6, combination, 0, unroll=2)

    def finish(a, carry):
        back = total_ref[a].reshape(512, 128).astype(bf16)
        own = own_ref[a].reshape(512, 128)
        out_ref[a] = (dot_t(back, msg_ref[...]) + dot_t(own, self_ref[...])).reshape(4, 128, 128)
        return carry

    lax.fori_loop(0, 2, finish, 0)


def backward(weights, slope, part, own, below, above, msg_weight, self_weight):
    return pl.pallas_call(
        backward_kernel,
        in_specs=[VM] * 8,
        out_specs=VM,
        out_shape=jax.ShapeDtypeStruct((2, 4, 128, 128), f32),
        scratch_shapes=[
            pltpu.VMEM((2, 4, 6, 128, 128), bf16),
            pltpu.VMEM((2, 4, 128, 128), f32),
            pltpu.VMEM((2, 24, 128), f32),
        ],
        cost_estimate=pl.CostEstimate(
            flops=4000000000, bytes_accessed=12000000, transcendentals=0
        ),
        compiler_params=SMALL,
        name="backward",
    )(weights, slope, part, own, below, above, msg_weight, self_weight)


def wave_tables(size_x, size_y, size_z):
    i16 = np.arange(16)
    points_x = np.array([g * 32 + a * 16 + i for a in range(2) for g in range(4) for i in i16])
    along_x = cas(np.arange(size_x), points_x, size_x)
    points_y = np.array(
        [gy * 16 + gx * 4 + gz for gx in range(4) for gy in range(16) for gz in range(4)]
    )
    into_y = cas(np.arange(size_y), points_y, size_y)
    back_x = np.array(
        [((2 * g - 1 + a) % 8) * 16 + i for g in range(4) for a in range(4) for i in i16]
    )
    back_z = np.array(
        [((4 * g - 2 + c) % 16) * 16 + k for g in range(4) for c in range(8) for k in i16]
    )
    tables = (
        cas(np.arange(size_z), np.arange(size_z), size_z),
        along_x,
        into_y,
        cas(back_x, np.arange(size_x), size_x),
        cas(np.arange(size_z), back_z, size_z),
    )
    return [jnp.asarray(np.ascontiguousarray(t), dtype=bf16) for t in tables]


def influence_of(size_x, size_y, size_z):
    device = lax.axis_index(everyone)

    def wave(index, size):
        signed = jnp.where(2 * index >= size, index - size, index)
        return signed.astype(f32) * (PC / size)

    wave_x = wave(device % size_x, size_x)
    wave_y = wave(jnp.arange(size_y, dtype=jnp.int32), size_y)[:, None]
    wave_z = wave(
        device // size_x * 128 + jnp.arange(size_z // 2, dtype=jnp.int32), size_z
    )[None, :]
    squared = wave_x * wave_x + wave_y * wave_y + wave_z * wave_z
    safe = jnp.where(squared > 0, squared, 1.0)
    return jnp.where(squared > 0, jnp.exp(-((math.pi * spread_width) ** 2) * squared) / safe, 0.0)


def swapped(value, axis):
    return lax.all_to_all(value, axis, split_axis=0, concat_axis=0, tiled=True)


def body(features, msg_weight, self_weight, charge_weight, spline_corner, spline_fraction):
    cells_x, cells_y, cells_z, slots, width = features.shape
    size_x = cells_x * PC * lax.axis_size("gx")
    size_y = cells_y * PC * lax.axis_size("gy")
    size_z = cells_z * PC * lax.axis_size("gz")
    volume = size_x // PC * (size_y // PC) * (size_z // PC)
    natoms = volume * slots
    cells = cells_x * cells_z

    features_own = features.reshape(cells, slots, width)
    own = project(
        features_own, msg_weight, spline_corner.swapaxes(2, 3), spline_fraction.swapaxes(2, 3)
    )
    own = own.reshape(cells_x, cells_z, slots + 16, width)
    sides, ends, outer, corners = early_halo(own)
    weights, part = inside_pairs(own, sides, features_own, self_weight)
    weights, part = ends_pairs(own, sides, ends, part, weights)
    influence = influence_of(size_x, size_y, size_z)
    along_z, along_x, into_y, back_x, back_z = wave_tables(size_x, size_y, size_z)

    read = charge_weight[None, :]
    weights, preact, mesh, row_place = message_layer(
        own, ends, outer, corners, part, read, weights
    )
    mesh = swapped(mesh, plane).reshape(4, 4, PC, 128)
    slope_near = late_halo(slope_of(preact, read))
    lines = swapped(forward_xz(mesh, along_z, along_x), everyone)
    lines = swapped(filter_y(lines, into_y, influence), everyone)
    field, energy = inverse_xz(lines, back_x, back_z, coupling / (2.0 * volume * natoms))
    field = swapped(field.reshape(16, 64, 128), plane)
    potential, atom_potential, own_weights, slopes = interpolate(
        field, row_place.reshape(24, 8, slots), weights, slope_near, coupling / volume
    )
    below, above = moved(potential, "gy", 1), moved(potential, "gy", -1)
    weights, total, cotangent = beside(weights, own_weights, slopes, potential)
    grad = backward(weights, slopes, total, cotangent, below, above, msg_weight, self_weight)
    return (
        grad.reshape(features.shape),
        atom_potential.reshape(cells_x, cells_y, cells_z, slots),
        energy[0, 0],
    )


def solution(mesh):
    in_specs = (
        P("gx", "gy", "gz", None, None),
        P(),
        P(),
        P(),
        P("gx", "gy", "gz", None, None),
        P("gx", "gy", "gz", None, None),
    )
    out_specs = (P("gx", "gy", "gz", None, None), P("gx", "gy", "gz", None), P())
    return jax.shard_map(body, mesh=mesh, in_specs=in_specs, out_specs=out_specs, check_vma=False)
```

```python
import functools
import math

import jax
import jax.numpy as jnp
import numpy as np
from jax import lax
from jax.experimental import pallas as pl
from jax.experimental.pallas import tpu as pltpu
from jax.sharding import PartitionSpec as P

PC = 16
pair_scale = 0.1
coupling = 0.125
spread_width = 0.0625
f32 = jnp.float32
bf16 = jnp.bfloat16
plane = ("gx", "gz")
everyone = ("gx", "gy", "gz")


def dot(a, b):
    return jnp.dot(a, b, preferred_element_type=f32)


def dot_t(a, b, precision=None):
    return lax.dot_general(
        a, b, (((1,), (1,)), ((), ())), preferred_element_type=f32, precision=precision
    )


def whole(shape):
    zeros = (0,) * len(shape)
    return pl.BlockSpec(shape, lambda *_: zeros)


VM = pl.BlockSpec(memory_space=pltpu.VMEM)
ANY = pl.BlockSpec(memory_space=pl.ANY)
SMALL = pltpu.CompilerParams(vmem_limit_bytes=20 << 20)
FIRST = pltpu.CompilerParams(vmem_limit_bytes=60 << 20)
LARGE = pltpu.CompilerParams(vmem_limit_bytes=50 << 20)
MIDDLE = pltpu.CompilerParams(vmem_limit_bytes=40 << 20)
FIELD = pltpu.CompilerParams(vmem_limit_bytes=44 << 20)


def cas(rows, columns, size):
    turns = np.outer(rows, columns) % size
    angle = 2.0 * np.pi / size * turns
    return np.cos(angle) + np.sin(angle)


def moved(value, axis, step):
    count = lax.axis_size(axis)
    pairs = [(i, (i + step) % count) for i in range(count)]
    return lax.ppermute(value.reshape(-1, 128), axis, pairs).reshape(value.shape)


def partners(value):
    count = lax.axis_size("gy")
    across = [(i, (i + 1 if i % 2 else i - 1) % count) for i in range(count)]
    within = [(i, i ^ 1) for i in range(count)]
    flat = value.reshape(-1, 128)
    return [lax.ppermute(flat, "gy", pairs).reshape(value.shape) for pairs in (across, within)]


def late_halo(own):
    last_x, last_z = own.shape[0] - 1, own.shape[1] - 1
    left, right = moved(own[:, last_z:], "gz", 1), moved(own[:, :1], "gz", -1)
    row = jnp.concatenate([left, own, right], axis=1)
    across, within = partners(row)
    rows = jnp.stack([across, row, within])
    return [rows, moved(rows[:, last_x:], "gx", 1), moved(rows[:, :1], "gx", -1)]


def early_halo(own):
    last_x, last_z = own.shape[0] - 1, own.shape[1] - 1
    below, above = partners(own)
    beside = [moved(own[last_x:], "gx", 1), moved(own[:1], "gx", -1)]
    sides = jnp.stack([below, above])
    rows = [below, own, above]
    left = moved(jnp.stack([row[:, last_z:] for row in rows]), "gz", 1)
    right = moved(jnp.stack([row[:, :1] for row in rows]), "gz", -1)
    aside = [moved(sides[:, last_x:], "gx", 1), moved(sides[:, :1], "gx", -1)]
    corners = [
        moved(jnp.concatenate([left[:, at : at + 1], right[:, at : at + 1]], axis=2), "gx", step)
        for at, step in ((last_x, 1), (0, -1))
    ]
    return [below, above], [left, right], beside + aside, corners


def project_kernel(features_ref, weight_ref, corner_ref, fraction_ref, out_ref):
    value = dot(features_ref[...].reshape(1024, 128), weight_ref[...]).astype(bf16)
    out_ref[:, :128, :] = value.reshape(8, 128, 128)
    none = jnp.zeros((5, 128), f32)
    for x in range(2):
        place = corner_ref[x, 0].astype(f32) + 1.0 + fraction_ref[x, 0]
        high = place.astype(bf16).astype(f32)
        rest = place - high
        middle = rest.astype(bf16).astype(f32)
        low = rest - middle
        for z in range(4):
            rows = [part[d, z : z + 1] for part in (high, low) for d in range(3)]
            rows += [none[:2]] + [middle[d, z : z + 1] for d in range(3)] + [none]
            out_ref[x * 4 + z, 128:, :] = jnp.concatenate(rows, axis=0).astype(bf16)


def project(features, weight, corner, fraction):
    return pl.pallas_call(
        project_kernel,
        grid=(1,),
        in_specs=[whole((8, 128, 128)), whole((128, 128))]
        + [whole((2, 1, 3, 4, 128))] * 2,
        out_specs=whole((8, 144, 128)),
        out_shape=jax.ShapeDtypeStruct((8, 144, 128), bf16),
        compiler_params=FIRST,
        name="project",
    )(features, weight, corner, fraction)


def place_of(rows):
    rows = rows.astype(f32)
    return rows[0:8] + rows[8:16] + pltpu.roll(rows[0:8], 5, 0)


BLOCKS = ((0, 0), (0, 1), (1, 0), (1, 1), (1, 2), (1, 3), (2, 2), (2, 3))
SPANS = ((0, 2, 0, 2), (2, 6, 0, 4), (6, 8, 2, 2))
ORDER_Y = (0, 2, 1)


def position_of(rows):
    return (place_of(rows) * (1.0 / PC)).astype(bf16).astype(f32)


def weigh(centres, a, shift, side, near, store, pairs):
    for c in range(4):
        columns = jnp.transpose(centres[a, c])
        centre_x = jnp.broadcast_to(columns[:, 0:1], (128, 128))
        centre_y = jnp.broadcast_to(columns[:, 1:2], (128, 128))
        centre_z = jnp.broadcast_to(columns[:, 2:3], (128, 128))
        for block, (pair, owner) in enumerate(BLOCKS):
            if owner != c or pair not in pairs:
                continue
            for at, dy in enumerate(ORDER_Y):
                for half in range(2):
                    dz = 2 * pair + half - c - 1
                    if abs(dz) > 1:
                        tile = jnp.zeros((128, 128), bf16)
                    else:
                        row = near(dy, 2 * pair + half)
                        gap_x = (row[0:1] + shift) - centre_x
                        gap_y = (row[1:2] + (dy - 1.0) * side) - centre_y
                        gap_z = (row[2:3] + float(dz)) - centre_z
                        squared = gap_x * gap_x + gap_y * gap_y + gap_z * gap_z
                        inside = jnp.maximum(1.0 - squared, 0.0)
                        tile = (pair_scale * inside * inside).astype(bf16)
                    store(block, (at * 2 + half) * 128, tile)


def add_near(weight_ref, t, a, cell, total_ref, pairs):
    for pair in pairs:
        start, stop, first, width = SPANS[pair]
        near = jnp.concatenate(
            [cell(dy, 2 * pair + half)[0:128, :] for dy in ORDER_Y for half in range(2)], axis=0
        )
        part = dot(weight_ref[t, start:stop].reshape(width * 128, 768), near)
        total_ref[a, first : first + width] += part.reshape(width, 128, 128)


def columns_kernel(first, count, weight_ref, weight_out, sems, slot, spans):
    return [
        pltpu.make_async_copy(
            weight_ref.at[pl.ds(first, count), pl.ds(start, size)],
            weight_out.at[pl.ds(first, count), pl.ds(start, size)],
            sems.at[slot + i],
        )
        for i, (start, size) in enumerate(spans)
    ]


INSIDE = (1,)
ENDS = (0, 2)
INSIDE_BLOCKS = ((2, 4),)
END_BLOCKS = ((0, 2), (6, 2))


def centres_of(own_ref, centre_ref):
    def one(cell, carry):
        x, z = cell // 4, cell % 4
        centre_ref[x, z] = position_of(own_ref[x, z, 128:144, :])
        return carry

    lax.fori_loop(0, 8, one, 0)


def inside_kernel(
    side_ref, own_ref, below_ref, above_ref, features_ref, self_ref,
    weight_out, total_ref, weight_ref, position_ref, sems
):
    refs = (below_ref, own_ref, above_ref)

    def positions(x, carry):
        for dy in range(3):
            for z in range(4):
                position_ref[dy, x, z] = position_of(refs[dy][x, z, 128:144, :])
        return carry

    lax.fori_loop(0, 2, positions, 0)
    total_ref[...] = dot(features_ref[...].reshape(1024, 128), self_ref[...]).reshape(
        2, 4, 128, 128
    )

    def column(t, carry):
        x, a = t // 2, t % 2

        def store(block, lane, tile):
            weight_ref[t, block, :, lane : lane + 128] = tile

        def near(dy, z):
            return position_ref[dy, x, z - 1]

        weigh(position_ref.at[1], a, (x - a).astype(f32), side_ref[...], near, store, INSIDE)
        add_near(weight_ref, t, a, lambda dy, z: refs[dy].at[x, z - 1], total_ref, INSIDE)
        return carry

    lax.fori_loop(0, 4, column, 0)
    copies = columns_kernel(0, 4, weight_ref, weight_out, sems, 0, INSIDE_BLOCKS)
    for copy in copies:
        copy.start()
    for copy in copies:
        copy.wait()


def inside_pairs(side, own, sides, features, self_weight):
    return pl.pallas_call(
        inside_kernel,
        in_specs=[VM] * 6,
        out_specs=[ANY, VM],
        out_shape=[
            jax.ShapeDtypeStruct((6, 8, 128, 768), bf16),
            jax.ShapeDtypeStruct((2, 4, 128, 128), f32),
        ],
        scratch_shapes=[
            pltpu.VMEM((4, 8, 128, 768), bf16),
            pltpu.VMEM((3, 2, 4, 8, 128), f32),
            pltpu.SemaphoreType.DMA((1,)),
        ],
        cost_estimate=pl.CostEstimate(
            flops=5000000000, bytes_accessed=9000000, transcendentals=0
        ),
        compiler_params=LARGE,
        name="inside_pairs",
    )(side, own, *sides, features, self_weight)


def ends_kernel(
    side_ref, own_ref, below_ref, above_ref, left_ref, right_ref,
    part_ref, _, weight_out, total_ref, weight_ref, centre_ref, position_ref, sems
):
    refs = (below_ref, own_ref, above_ref)

    def cell(dy, x, z):
        if z == 0:
            return left_ref.at[dy, x, 0]
        if z == 5:
            return right_ref.at[dy, x, 0]
        return refs[dy].at[x, z - 1]

    centres_of(own_ref, centre_ref)

    def positions(x, carry):
        for dy in range(3):
            for z in (0, 1, 4, 5):
                position_ref[dy, x, z] = position_of(cell(dy, x, z)[128:144, :])
        return carry

    lax.fori_loop(0, 2, positions, 0)
    total_ref[...] = part_ref[...]

    def column(t, carry):
        x, a = t // 2, t % 2

        def store(block, lane, tile):
            weight_ref[t, block, :, lane : lane + 128] = tile

        def near(dy, z):
            return position_ref[dy, x, z]

        weigh(centre_ref, a, (x - a).astype(f32), side_ref[...], near, store, ENDS)
        add_near(weight_ref, t, a, lambda dy, z: cell(dy, x, z), total_ref, ENDS)
        return carry

    lax.fori_loop(0, 4, column, 0)
    copies = columns_kernel(0, 4, weight_ref, weight_out, sems, 0, END_BLOCKS)
    for copy in copies:
        copy.start()

    for copy in copies:
        copy.wait()


def ends_pairs(side, own, sides, ends, part, weights):
    return pl.pallas_call(
        ends_kernel,
        in_specs=[VM] * 7 + [ANY],
        out_specs=[ANY, VM],
        input_output_aliases={7: 0},
        out_shape=[
            jax.ShapeDtypeStruct((6, 8, 128, 768), bf16),
            jax.ShapeDtypeStruct((2, 4, 128, 128), f32),
        ],
        scratch_shapes=[
            pltpu.VMEM((4, 8, 128, 768), bf16),
            pltpu.VMEM((2, 4, 8, 128), f32),
            pltpu.VMEM((3, 2, 6, 8, 128), f32),
            pltpu.SemaphoreType.DMA((2,)),
        ],
        cost_estimate=pl.CostEstimate(
            flops=6000000000, bytes_accessed=9000000, transcendentals=0
        ),
        compiler_params=LARGE,
        name="ends_pairs",
    )(side, own, *sides, *ends, part, weights)


def spline_row(place):
    point = lax.broadcasted_iota(jnp.int32, (PC, 128), 0).astype(f32)
    away = jnp.abs(point - place)
    near = (4.0 - 6.0 * away * away + 3.0 * away * away * away) * (1.0 / 6.0)
    rest = 2.0 - away
    far = rest * rest * rest * (1.0 / 6.0)
    return jnp.where(away < 1.0, near, jnp.where(away < 2.0, far, 0.0))


def message_kernel(
    side_ref, own_ref, left_ref, right_ref, before_own, after_own, before_side, after_side, before_end,
    after_end, part_ref, read_ref, _,
    weight_out, total_ref, mesh_ref, row_place_ref,
    weight_ref, position_ref, centre_ref, high_ref, low_ref, charge_ref, left_rows, right_rows, sems
):
    refs = ((before_own, before_side, before_end), (after_own, after_side, after_end))

    def cell(side, dy, z):
        own, beside, end = refs[side]
        if z in (0, 5):
            return end.at[dy, 0, z // 5]
        return own.at[0, z - 1] if dy == 1 else beside.at[dy // 2, 0, z - 1]

    centres_of(own_ref, centre_ref)
    for side in range(2):
        for dy in range(3):
            for z in range(6):
                position_ref[side, dy, z] = position_of(cell(side, dy, z)[128:144, :])
        for z in range(6):
            row_place_ref[3 * side, z] = place_of(cell(side, 1, z)[128:144, :])

    def row_places(x, carry):
        row_place_ref[1 + x, 0] = place_of(left_ref[1, x, 0, 128:144, :])
        for z in range(4):
            row_place_ref[1 + x, 1 + z] = place_of(own_ref[x, z, 128:144, :])
        row_place_ref[1 + x, 5] = place_of(right_ref[1, x, 0, 128:144, :])
        return carry

    lax.fori_loop(0, 2, row_places, 0)

    def column(side, carry):
        def store(block, lane, tile):
            weight_ref[side, block, :, lane : lane + 128] = tile

        def near(dy, z):
            return position_ref[side, dy, z]

        weigh(centre_ref, side, (2 * side - 1).astype(f32), side_ref[...], near, store, ENDS + INSIDE)
        return carry

    lax.fori_loop(0, 2, column, 0)
    copies = [pltpu.make_async_copy(weight_ref, weight_out.at[pl.ds(4, 2)], sems.at[0])]
    for copy in copies:
        copy.start()
    total_ref[...] = part_ref[...]
    for side in range(2):
        add_near(
            weight_ref, side, side, lambda dy, z: cell(side, dy, z), total_ref, ENDS + INSIDE
        )

    def finish(index, carry):
        preact = total_ref[index // 4, index % 4]
        silu = preact * (0.5 + 0.5 * jnp.tanh(0.5 * preact))
        high = silu.astype(bf16)
        high_ref[index] = high
        low_ref[index] = (silu - high.astype(f32)).astype(bf16)
        return carry

    lax.fori_loop(0, 8, finish, 0, unroll=2)
    wide = jnp.broadcast_to(read_ref[...], (16, 128))
    charge_ref[...] = dot_t(wide, high_ref[...].reshape(1024, 128)) + dot_t(
        wide, low_ref[...].reshape(1024, 128)
    )
    block = lax.broadcasted_iota(jnp.int32, (128, 128), 0) // PC

    def spread(cell, carry):
        lanes = pl.ds(pl.multiple_of(cell * 128, 128), 128)
        place = row_place_ref[1 + cell // 4, 1 + cell % 4]
        row_x = spline_row(place[0:1])
        row_y = spline_row(place[1:2]) * charge_ref[0:1, lanes]
        row_z = spline_row(place[2:3])
        left_rows[:, lanes] = (
            (row_y[:, None, :] * row_x[None, :, :]).reshape(PC * PC, 128).astype(bf16)
        )
        right_rows[:, lanes] = jnp.where(block == cell, jnp.tile(row_z, (8, 1)), 0.0).astype(bf16)
        return carry

    lax.fori_loop(0, 8, spread, 0)
    mesh_ref[...] = dot_t(left_rows[...], right_rows[...]).reshape(PC, PC, 128).astype(bf16)
    for copy in copies:
        copy.wait()


def message_layer(side, own, ends, outer, corners, part, read, weights):
    return pl.pallas_call(
        message_kernel,
        in_specs=[VM] * 12 + [ANY],
        out_specs=[ANY, VM, VM, VM],
        input_output_aliases={12: 0},
        out_shape=[
            jax.ShapeDtypeStruct((6, 8, 128, 768), bf16),
            jax.ShapeDtypeStruct((2, 4, 128, 128), f32),
            jax.ShapeDtypeStruct((PC, PC, 128), bf16),
            jax.ShapeDtypeStruct((4, 6, 8, 128), f32),
        ],
        scratch_shapes=[
            pltpu.VMEM((2, 8, 128, 768), bf16),
            pltpu.VMEM((2, 3, 6, 8, 128), f32),
            pltpu.VMEM((2, 4, 8, 128), f32),
            pltpu.VMEM((8, 128, 128), bf16),
            pltpu.VMEM((8, 128, 128), bf16),
            pltpu.VMEM((16, 1024), f32),
            pltpu.VMEM((PC * PC, 1024), bf16),
            pltpu.VMEM((128, 1024), bf16),
            pltpu.SemaphoreType.DMA((1,)),
        ],
        cost_estimate=pl.CostEstimate(
            flops=5000000000, bytes_accessed=6000000, transcendentals=8 * 16384
        ),
        compiler_params=LARGE,
        name="message",
    )(side, own, *ends, *outer, *corners, part, read, weights)


def slope_kernel(total_ref, read_ref, out_ref):
    read = read_ref[...].astype(f32)

    def one(index, carry):
        a, c = index // 4, index % 4
        preact = total_ref[a, c]
        sigma = 0.5 + 0.5 * jnp.tanh(0.5 * preact)
        out_ref[a, c] = (read * (sigma * (1.0 + preact * (1.0 - sigma)))).astype(bf16)
        return carry

    lax.fori_loop(0, 8, one, 0, unroll=2)


def slope_of(total, read):
    return pl.pallas_call(
        slope_kernel,
        in_specs=[VM] * 2,
        out_specs=VM,
        out_shape=jax.ShapeDtypeStruct(total.shape, bf16),
        cost_estimate=pl.CostEstimate(
            flops=8 * 16384 * 8, bytes_accessed=900000, transcendentals=8 * 16384
        ),
        compiler_params=SMALL,
        name="slope",
    )(total, read)


def forward_kernel(mesh_ref, along_z_ref, along_x_ref, out_ref):
    lane = lax.broadcasted_iota(jnp.int32, (64, 128), 1)
    total = jnp.zeros((128, 256), f32)
    for g in range(4):
        mesh = mesh_ref[:, g].reshape(64, 128)
        none = jnp.zeros_like(mesh)
        halves = jnp.concatenate(
            [jnp.where(lane < 64, mesh, none), jnp.where(lane < 64, none, mesh)], axis=0
        )
        table = along_z_ref[g * 64 : (g + 1) * 64, :]
        total = total + dot(halves, jnp.concatenate([table, table], axis=0))
    lines = total.astype(bf16)
    waves = dot(along_x_ref[...], lines)
    out_ref[0:128, :] = waves[:, :128]
    out_ref[128:256, :] = waves[:, 128:]


def forward_xz(mesh, along_z, along_x):
    return pl.pallas_call(
        forward_kernel,
        in_specs=[VM] * 3,
        out_specs=VM,
        compiler_params=SMALL,
        out_shape=jax.ShapeDtypeStruct((256, 128), f32),
        cost_estimate=pl.CostEstimate(
            flops=2 * 64 * 512 * 512, bytes_accessed=800000, transcendentals=0
        ),
        name="forward_xz",
    )(mesh, along_z, along_x)


def filter_kernel(lines_ref, into_ref, influence_ref, out_ref):
    waves = dot(into_ref[...], lines_ref[...].astype(bf16))
    scaled = influence_ref[...] * waves
    power = jnp.sum(jnp.sum(scaled * waves, axis=0, keepdims=True), axis=1, keepdims=True)
    out_ref[pl.ds(0, 256, stride=2), :] = lax.dot_general(
        into_ref[...],
        scaled.astype(bf16),
        (((0,), (0,)), ((), ())),
        preferred_element_type=f32,
    )
    out_ref[pl.ds(1, 256, stride=2), :] = jnp.broadcast_to(power, (256, 128))


def filter_y(lines, into, influence):
    return pl.pallas_call(
        filter_kernel,
        in_specs=[VM] * 3,
        out_specs=VM,
        compiler_params=SMALL,
        out_shape=jax.ShapeDtypeStruct((512, 128), f32),
        cost_estimate=pl.CostEstimate(
            flops=4 * 256 * 256 * 128, bytes_accessed=700000, transcendentals=0
        ),
        name="filter_y",
    )(lines, into, influence)


def inverse_kernel(energy_scale, lines_ref, along_x_ref, along_z_ref, out_ref, energy_ref):
    waves = jnp.concatenate(
        [lines_ref[pl.ds(0, 128, stride=2), :], lines_ref[pl.ds(256, 128, stride=2), :]], axis=1
    ).astype(bf16)
    half = dot(along_x_ref[...], waves).astype(bf16)
    field = dot(half, along_z_ref[...]).astype(bf16)
    for gx in range(4):
        for gz in range(4):
            out_ref[gx, gz] = field[gx * 64 : (gx + 1) * 64, gz * 128 : (gz + 1) * 128]
    power = jnp.sum(lines_ref[pl.ds(1, 256, stride=2), :], axis=0, keepdims=True)
    energy_ref[...] = jnp.broadcast_to(power * energy_scale, (8, 128))


def inverse_xz(lines, along_x, along_z, energy_scale):
    return pl.pallas_call(
        functools.partial(inverse_kernel, energy_scale),
        in_specs=[VM] * 3,
        out_specs=[VM, VM],
        compiler_params=SMALL,
        out_shape=[
            jax.ShapeDtypeStruct((4, 4, 64, 128), bf16),
            jax.ShapeDtypeStruct((8, 128), f32),
        ],
        cost_estimate=pl.CostEstimate(
            flops=2 * 256 * 256 * 640, bytes_accessed=900000, transcendentals=0
        ),
        name="inverse_xz",
    )(lines, along_x, along_z)


def interpolate_kernel(
    field_scale, field_ref, place_ref, stored_ref, rows_ref, before_ref, after_ref,
    out_ref, own_ref, weight_ref, slope_ref, sems
):
    pairs = [
        (rows_ref, slope_ref.at[:, pl.ds(1, 2)]),
        (before_ref, slope_ref.at[:, pl.ds(0, 1)]),
        (after_ref, slope_ref.at[:, pl.ds(3, 1)]),
        (stored_ref.at[:, :, :, pl.ds(512, 256)], weight_ref),
    ]
    copies = [
        pltpu.make_async_copy(source, target, sems.at[i])
        for i, (source, target) in enumerate(pairs)
    ]
    for copy in copies:
        copy.start()
    block = lax.broadcasted_iota(jnp.int32, (128, 128), 0) // PC

    def gather(step, carry):
        ax, half = step // 2, 3 * (step % 2)
        field = field_ref[:, pl.ds(pl.multiple_of(ax * PC, PC), PC), :].reshape(PC * PC, 128)
        for third in range(3):
            cz = half + third
            place = place_ref[ax * 6 + cz]
            row_x = spline_row(place[0:1])
            row_y = spline_row(place[1:2])
            row_z = spline_row(place[2:3])
            right = jnp.where(block == cz + 1, jnp.tile(row_z, (8, 1)), 0.0).astype(bf16)
            partial = dot(field, right)
            left = (row_y[:, None, :] * row_x[None, :, :]).reshape(PC * PC, 128)
            out_ref[pl.ds(ax * 6 + cz, 1), :] = (
                jnp.sum(partial * left, axis=0, keepdims=True) * field_scale
            )
        return carry

    lax.fori_loop(0, 8, gather, 0)
    own_ref[0:4, :] = out_ref[7:11, :]
    own_ref[4:8, :] = out_ref[13:17, :]
    for copy in copies:
        copy.wait()


def interpolate(field, place, weights, slopes, field_scale):
    return pl.pallas_call(
        functools.partial(interpolate_kernel, field_scale),
        in_specs=[VM] * 2 + [ANY] * 4,
        out_specs=[VM] * 4,
        compiler_params=FIELD,
        out_shape=[
            jax.ShapeDtypeStruct((24, 128), f32),
            jax.ShapeDtypeStruct((8, 128), f32),
            jax.ShapeDtypeStruct((6, 8, 128, 256), bf16),
            jax.ShapeDtypeStruct((3, 4, 6, 128, 128), bf16),
        ],
        scratch_shapes=[pltpu.SemaphoreType.DMA((4,))],
        cost_estimate=pl.CostEstimate(
            flops=24 * 2 * 256 * 128 * 128, bytes_accessed=400000, transcendentals=0
        ),
        name="interpolate",
    )(field, place, weights, *slopes)


def combination_of(t):
    return jnp.where(t < 4, 1 + t // 2, 3 * (t - 4)), t % 2


def scaled(columns, cell, slope):
    return (columns[:, cell : cell + 1] * slope.astype(f32)).astype(bf16)


def beside_kernel(
    stored_ref, weight_ref, slope_ref, potential_ref, rest_ref, total_ref, own_out, near_ref, sems
):
    copies = [
        pltpu.make_async_copy(
            stored_ref.at[pl.ds(i, 3), :, :, pl.ds(0, 512)], rest_ref.at[pl.ds(i, 3)], sems.at[i // 3]
        )
        for i in (0, 3)
    ]
    for copy in copies:
        copy.start()
    columns = jnp.transpose(potential_ref[...])
    for x in range(4):
        for z in range(6):
            near_ref[x, z] = scaled(columns, x * 6 + z, slope_ref[1, x, z])
    own_out[...] = near_ref[1:3, 1:5]
    total_ref[...] = jnp.zeros_like(total_ref)

    def combination(t, carry):
        x, a = combination_of(t)
        for pair, (start, stop, first, width) in enumerate(SPANS):
            part = dot(
                weight_ref[t, start:stop].reshape(width * 128, 256),
                near_ref[x, 2 * pair : 2 * pair + 2].reshape(256, 128),
            )
            total_ref[a, first : first + width] += part.reshape(width, 128, 128)
        return carry

    lax.fori_loop(0, 6, combination, 0)
    for copy in copies:
        copy.wait()


def beside(stored, weights, slopes, potential):
    return pl.pallas_call(
        beside_kernel,
        in_specs=[ANY] + [VM] * 3,
        out_specs=[VM] * 3,
        out_shape=[
            jax.ShapeDtypeStruct((6, 8, 128, 512), bf16),
            jax.ShapeDtypeStruct((2, 4, 128, 128), f32),
            jax.ShapeDtypeStruct((2, 4, 128, 128), bf16),
        ],
        scratch_shapes=[
            pltpu.VMEM((4, 6, 128, 128), bf16),
            pltpu.SemaphoreType.DMA((2,)),
        ],
        cost_estimate=pl.CostEstimate(
            flops=3000000000, bytes_accessed=12000000, transcendentals=0
        ),
        compiler_params=MIDDLE,
        name="beside",
    )(stored, weights, slopes, potential)


def backward_kernel(
    weight_ref, slope_ref, part_ref, own_ref, below_ref, above_ref, msg_ref, self_ref, out_ref,
    near_ref, total_ref, potential_ref
):
    potential_ref[0] = below_ref[...]
    potential_ref[1] = above_ref[...]

    def scale(side, carry):
        columns = jnp.transpose(potential_ref[side])
        for x in range(4):
            for z in range(6):
                near_ref[side, x, z] = scaled(columns, x * 6 + z, slope_ref[2 * side, x, z])
        return carry

    lax.fori_loop(0, 2, scale, 0)
    total_ref[...] = part_ref[...]

    def combination(t, carry):
        x, a = combination_of(t)
        for pair, (start, stop, first, width) in enumerate(SPANS):
            near = jnp.concatenate(
                [
                    near_ref[side, x, 2 * pair : 2 * pair + 2].reshape(256, 128)
                    for side in range(2)
                ],
                axis=0,
            )
            part = dot(weight_ref[t, start:stop].reshape(width * 128, 512), near)
            total_ref[a, first : first + width] += part.reshape(width, 128, 128)
        return carry

    lax.fori_loop(0, 6, combination, 0, unroll=2)

    def finish(a, carry):
        back = total_ref[a].reshape(512, 128).astype(bf16)
        own = own_ref[a].reshape(512, 128)
        out_ref[a] = (dot_t(back, msg_ref[...]) + dot_t(own, self_ref[...])).reshape(4, 128, 128)
        return carry

    lax.fori_loop(0, 2, finish, 0)


def backward(weights, slope, part, own, below, above, msg_weight, self_weight):
    return pl.pallas_call(
        backward_kernel,
        in_specs=[VM] * 8,
        out_specs=VM,
        out_shape=jax.ShapeDtypeStruct((2, 4, 128, 128), f32),
        scratch_shapes=[
            pltpu.VMEM((2, 4, 6, 128, 128), bf16),
            pltpu.VMEM((2, 4, 128, 128), f32),
            pltpu.VMEM((2, 24, 128), f32),
        ],
        cost_estimate=pl.CostEstimate(
            flops=4000000000, bytes_accessed=12000000, transcendentals=0
        ),
        compiler_params=SMALL,
        name="backward",
    )(weights, slope, part, own, below, above, msg_weight, self_weight)


def wave_tables(size_x, size_y, size_z):
    i16 = np.arange(16)
    points_x = np.array([g * 32 + a * 16 + i for a in range(2) for g in range(4) for i in i16])
    along_x = cas(np.arange(size_x), points_x, size_x)
    points_y = np.array(
        [gy * 16 + gx * 4 + gz for gx in range(4) for gy in range(16) for gz in range(4)]
    )
    into_y = cas(np.arange(size_y), points_y, size_y)
    back_x = np.array(
        [((2 * g - 1 + a) % 8) * 16 + i for g in range(4) for a in range(4) for i in i16]
    )
    back_z = np.array(
        [((4 * g - 2 + c) % 16) * 16 + k for g in range(4) for c in range(8) for k in i16]
    )
    tables = (
        cas(np.arange(size_z), np.arange(size_z), size_z),
        along_x,
        into_y,
        cas(back_x, np.arange(size_x), size_x),
        cas(np.arange(size_z), back_z, size_z),
    )
    return [jnp.asarray(np.ascontiguousarray(t), dtype=bf16) for t in tables]


def influence_of(size_x, size_y, size_z):
    device = lax.axis_index(everyone)

    def wave(index, size):
        signed = jnp.where(2 * index >= size, index - size, index)
        return signed.astype(f32) * (PC / size)

    wave_x = wave(device % size_x, size_x)
    wave_y = wave(jnp.arange(size_y, dtype=jnp.int32), size_y)[:, None]
    wave_z = wave(
        device // size_x * 128 + jnp.arange(size_z // 2, dtype=jnp.int32), size_z
    )[None, :]
    squared = wave_x * wave_x + wave_y * wave_y + wave_z * wave_z
    safe = jnp.where(squared > 0, squared, 1.0)
    return jnp.where(squared > 0, jnp.exp(-((math.pi * spread_width) ** 2) * squared) / safe, 0.0)


def swapped(value, axis):
    return lax.all_to_all(value, axis, split_axis=0, concat_axis=0, tiled=True)


def body(features, msg_weight, self_weight, charge_weight, spline_corner, spline_fraction):
    cells_x, cells_y, cells_z, slots, width = features.shape
    size_x = cells_x * PC * lax.axis_size("gx")
    size_y = cells_y * PC * lax.axis_size("gy")
    size_z = cells_z * PC * lax.axis_size("gz")
    volume = size_x // PC * (size_y // PC) * (size_z // PC)
    natoms = volume * slots
    cells = cells_x * cells_z

    features_own = features.reshape(cells, slots, width)
    own = project(
        features_own, msg_weight, spline_corner.swapaxes(2, 3), spline_fraction.swapaxes(2, 3)
    )
    own = own.reshape(cells_x, cells_z, slots + 16, width)
    sides, ends, outer, corners = early_halo(own)
    side = jnp.full((1, slots), 1 - 2 * (lax.axis_index("gy") % 2), f32)
    weights, part = inside_pairs(side, own, sides, features_own, self_weight)
    weights, part = ends_pairs(side, own, sides, ends, part, weights)
    influence = influence_of(size_x, size_y, size_z)
    along_z, along_x, into_y, back_x, back_z = wave_tables(size_x, size_y, size_z)

    read = charge_weight[None, :]
    weights, preact, mesh, row_place = message_layer(
        side, own, ends, outer, corners, part, read, weights
    )
    mesh = swapped(mesh, plane).reshape(4, 4, PC, 128)
    slope_near = late_halo(slope_of(preact, read))
    lines = swapped(forward_xz(mesh, along_z, along_x), everyone)
    lines = swapped(filter_y(lines, into_y, influence), everyone)
    field, energy = inverse_xz(lines, back_x, back_z, coupling / (2.0 * volume * natoms))
    field = swapped(field.reshape(16, 64, 128), plane)
    potential, atom_potential, own_weights, slopes = interpolate(
        field, row_place.reshape(24, 8, slots), weights, slope_near, coupling / volume
    )
    below, above = partners(potential)
    weights, total, cotangent = beside(weights, own_weights, slopes, potential)
    grad = backward(weights, slopes, total, cotangent, below, above, msg_weight, self_weight)
    return (
        grad.reshape(features.shape),
        atom_potential.reshape(cells_x, cells_y, cells_z, slots),
        energy[0, 0],
    )


def solution(mesh):
    in_specs = (
        P("gx", "gy", "gz", None, None),
        P(),
        P(),
        P(),
        P("gx", "gy", "gz", None, None),
        P("gx", "gy", "gz", None, None),
    )
    out_specs = (P("gx", "gy", "gz", None, None), P("gx", "gy", "gz", None), P())
    return jax.shard_map(body, mesh=mesh, in_specs=in_specs, out_specs=out_specs, check_vma=False)
```

```python
import functools
import math

import jax
import jax.numpy as jnp
import numpy as np
from jax import lax
from jax.experimental import pallas as pl
from jax.experimental.pallas import tpu as pltpu
from jax.sharding import PartitionSpec as P

PC = 16
pair_scale = 0.1
coupling = 0.125
spread_width = 0.0625
f32 = jnp.float32
bf16 = jnp.bfloat16
plane = ("gx", "gz")
everyone = ("gx", "gy", "gz")


def dot(a, b):
    return jnp.dot(a, b, preferred_element_type=f32)


def dot_t(a, b, precision=None):
    return lax.dot_general(
        a, b, (((1,), (1,)), ((), ())), preferred_element_type=f32, precision=precision
    )


def whole(shape):
    zeros = (0,) * len(shape)
    return pl.BlockSpec(shape, lambda *_: zeros)


VM = pl.BlockSpec(memory_space=pltpu.VMEM)
ANY = pl.BlockSpec(memory_space=pl.ANY)
SMALL = pltpu.CompilerParams(vmem_limit_bytes=20 << 20)
FIRST = pltpu.CompilerParams(vmem_limit_bytes=60 << 20)
LARGE = pltpu.CompilerParams(vmem_limit_bytes=50 << 20)
MIDDLE = pltpu.CompilerParams(vmem_limit_bytes=40 << 20)
FIELD = pltpu.CompilerParams(vmem_limit_bytes=44 << 20)


def cas(rows, columns, size):
    turns = np.outer(rows, columns) % size
    angle = 2.0 * np.pi / size * turns
    return np.cos(angle) + np.sin(angle)


def moved(value, axis, step):
    count = lax.axis_size(axis)
    pairs = [(i, (i + step) % count) for i in range(count)]
    return lax.ppermute(value.reshape(-1, 128), axis, pairs).reshape(value.shape)


def partners(value):
    count = lax.axis_size("gy")
    across = [(i, (i + 1 if i % 2 else i - 1) % count) for i in range(count)]
    within = [(i, i ^ 1) for i in range(count)]
    flat = value.reshape(-1, 128)
    return [lax.ppermute(flat, "gy", pairs).reshape(value.shape) for pairs in (across, within)]


def late_halo(own):
    last_x, last_z = own.shape[0] - 1, own.shape[1] - 1
    left, right = moved(own[:, last_z:], "gz", 1), moved(own[:, :1], "gz", -1)
    row = jnp.concatenate([left, own, right], axis=1)
    below, above = moved(row, "gy", 1), moved(row, "gy", -1)
    even = lax.axis_index("gy") % 2 == 0
    across, within = jnp.where(even, below, above), jnp.where(even, above, below)
    rows = jnp.stack([across, row, within])
    return [rows, moved(rows[:, last_x:], "gx", 1), moved(rows[:, :1], "gx", -1)]


def early_halo(own):
    last_x, last_z = own.shape[0] - 1, own.shape[1] - 1
    below, above = partners(own)
    beside = [moved(own[last_x:], "gx", 1), moved(own[:1], "gx", -1)]
    sides = jnp.stack([below, above])
    rows = [below, own, above]
    left = moved(jnp.stack([row[:, last_z:] for row in rows]), "gz", 1)
    right = moved(jnp.stack([row[:, :1] for row in rows]), "gz", -1)
    aside = [moved(sides[:, last_x:], "gx", 1), moved(sides[:, :1], "gx", -1)]
    corners = [
        moved(jnp.concatenate([left[:, at : at + 1], right[:, at : at + 1]], axis=2), "gx", step)
        for at, step in ((last_x, 1), (0, -1))
    ]
    return [below, above], [left, right], beside + aside, corners


def project_kernel(features_ref, weight_ref, corner_ref, fraction_ref, out_ref):
    value = dot(features_ref[...].reshape(1024, 128), weight_ref[...]).astype(bf16)
    out_ref[:, :128, :] = value.reshape(8, 128, 128)
    none = jnp.zeros((5, 128), f32)
    for x in range(2):
        place = corner_ref[x, 0].astype(f32) + 1.0 + fraction_ref[x, 0]
        high = place.astype(bf16).astype(f32)
        rest = place - high
        middle = rest.astype(bf16).astype(f32)
        low = rest - middle
        for z in range(4):
            rows = [part[d, z : z + 1] for part in (high, low) for d in range(3)]
            rows += [none[:2]] + [middle[d, z : z + 1] for d in range(3)] + [none]
            out_ref[x * 4 + z, 128:, :] = jnp.concatenate(rows, axis=0).astype(bf16)


def project(features, weight, corner, fraction):
    return pl.pallas_call(
        project_kernel,
        grid=(1,),
        in_specs=[whole((8, 128, 128)), whole((128, 128))]
        + [whole((2, 1, 3, 4, 128))] * 2,
        out_specs=whole((8, 144, 128)),
        out_shape=jax.ShapeDtypeStruct((8, 144, 128), bf16),
        compiler_params=FIRST,
        name="project",
    )(features, weight, corner, fraction)


def place_of(rows):
    rows = rows.astype(f32)
    return rows[0:8] + rows[8:16] + pltpu.roll(rows[0:8], 5, 0)


BLOCKS = ((0, 0), (0, 1), (1, 0), (1, 1), (1, 2), (1, 3), (2, 2), (2, 3))
SPANS = ((0, 2, 0, 2), (2, 6, 0, 4), (6, 8, 2, 2))
ORDER_Y = (0, 2, 1)


def position_of(rows):
    return (place_of(rows) * (1.0 / PC)).astype(bf16).astype(f32)


def weigh(centres, a, shift, side, near, store, pairs):
    for c in range(4):
        columns = jnp.transpose(centres[a, c])
        centre_x = jnp.broadcast_to(columns[:, 0:1], (128, 128))
        centre_y = jnp.broadcast_to(columns[:, 1:2], (128, 128))
        centre_z = jnp.broadcast_to(columns[:, 2:3], (128, 128))
        for block, (pair, owner) in enumerate(BLOCKS):
            if owner != c or pair not in pairs:
                continue
            for at, dy in enumerate(ORDER_Y):
                for half in range(2):
                    dz = 2 * pair + half - c - 1
                    if abs(dz) > 1:
                        tile = jnp.zeros((128, 128), bf16)
                    else:
                        row = near(dy, 2 * pair + half)
                        gap_x = (row[0:1] + shift) - centre_x
                        gap_y = (row[1:2] + (dy - 1.0) * side) - centre_y
                        gap_z = (row[2:3] + float(dz)) - centre_z
                        squared = gap_x * gap_x + gap_y * gap_y + gap_z * gap_z
                        inside = jnp.maximum(1.0 - squared, 0.0)
                        tile = (pair_scale * inside * inside).astype(bf16)
                    store(block, (at * 2 + half) * 128, tile)


def add_near(weight_ref, t, a, cell, total_ref, pairs):
    for pair in pairs:
        start, stop, first, width = SPANS[pair]
        near = jnp.concatenate(
            [cell(dy, 2 * pair + half)[0:128, :] for dy in ORDER_Y for half in range(2)], axis=0
        )
        part = dot(weight_ref[t, start:stop].reshape(width * 128, 768), near)
        total_ref[a, first : first + width] += part.reshape(width, 128, 128)


def columns_kernel(first, count, weight_ref, weight_out, sems, slot, spans):
    return [
        pltpu.make_async_copy(
            weight_ref.at[pl.ds(first, count), pl.ds(start, size)],
            weight_out.at[pl.ds(first, count), pl.ds(start, size)],
            sems.at[slot + i],
        )
        for i, (start, size) in enumerate(spans)
    ]


INSIDE = (1,)
ENDS = (0, 2)
INSIDE_BLOCKS = ((2, 4),)
END_BLOCKS = ((0, 2), (6, 2))


def centres_of(own_ref, centre_ref):
    def one(cell, carry):
        x, z = cell // 4, cell % 4
        centre_ref[x, z] = position_of(own_ref[x, z, 128:144, :])
        return carry

    lax.fori_loop(0, 8, one, 0)


def inside_kernel(
    side_ref, own_ref, below_ref, above_ref, features_ref, self_ref,
    weight_out, total_ref, weight_ref, position_ref, sems
):
    refs = (below_ref, own_ref, above_ref)

    def positions(x, carry):
        for dy in range(3):
            for z in range(4):
                position_ref[dy, x, z] = position_of(refs[dy][x, z, 128:144, :])
        return carry

    lax.fori_loop(0, 2, positions, 0)
    total_ref[...] = dot(features_ref[...].reshape(1024, 128), self_ref[...]).reshape(
        2, 4, 128, 128
    )

    def column(t, carry):
        x, a = t // 2, t % 2

        def store(block, lane, tile):
            weight_ref[t, block, :, lane : lane + 128] = tile

        def near(dy, z):
            return position_ref[dy, x, z - 1]

        weigh(position_ref.at[1], a, (x - a).astype(f32), side_ref[...], near, store, INSIDE)
        add_near(weight_ref, t, a, lambda dy, z: refs[dy].at[x, z - 1], total_ref, INSIDE)
        return carry

    lax.fori_loop(0, 4, column, 0)
    copies = columns_kernel(0, 4, weight_ref, weight_out, sems, 0, INSIDE_BLOCKS)
    for copy in copies:
        copy.start()
    for copy in copies:
        copy.wait()


def inside_pairs(side, own, sides, features, self_weight):
    return pl.pallas_call(
        inside_kernel,
        in_specs=[VM] * 6,
        out_specs=[ANY, VM],
        out_shape=[
            jax.ShapeDtypeStruct((6, 8, 128, 768), bf16),
            jax.ShapeDtypeStruct((2, 4, 128, 128), f32),
        ],
        scratch_shapes=[
            pltpu.VMEM((4, 8, 128, 768), bf16),
            pltpu.VMEM((3, 2, 4, 8, 128), f32),
            pltpu.SemaphoreType.DMA((1,)),
        ],
        cost_estimate=pl.CostEstimate(
            flops=5000000000, bytes_accessed=9000000, transcendentals=0
        ),
        compiler_params=LARGE,
        name="inside_pairs",
    )(side, own, *sides, features, self_weight)


def ends_kernel(
    side_ref, own_ref, below_ref, above_ref, left_ref, right_ref,
    part_ref, _, weight_out, total_ref, weight_ref, centre_ref, position_ref, sems
):
    refs = (below_ref, own_ref, above_ref)

    def cell(dy, x, z):
        if z == 0:
            return left_ref.at[dy, x, 0]
        if z == 5:
            return right_ref.at[dy, x, 0]
        return refs[dy].at[x, z - 1]

    centres_of(own_ref, centre_ref)

    def positions(x, carry):
        for dy in range(3):
            for z in (0, 1, 4, 5):
                position_ref[dy, x, z] = position_of(cell(dy, x, z)[128:144, :])
        return carry

    lax.fori_loop(0, 2, positions, 0)
    total_ref[...] = part_ref[...]

    def column(t, carry):
        x, a = t // 2, t % 2

        def store(block, lane, tile):
            weight_ref[t, block, :, lane : lane + 128] = tile

        def near(dy, z):
            return position_ref[dy, x, z]

        weigh(centre_ref, a, (x - a).astype(f32), side_ref[...], near, store, ENDS)
        add_near(weight_ref, t, a, lambda dy, z: cell(dy, x, z), total_ref, ENDS)
        return carry

    lax.fori_loop(0, 4, column, 0)
    copies = columns_kernel(0, 4, weight_ref, weight_out, sems, 0, END_BLOCKS)
    for copy in copies:
        copy.start()

    for copy in copies:
        copy.wait()


def ends_pairs(side, own, sides, ends, part, weights):
    return pl.pallas_call(
        ends_kernel,
        in_specs=[VM] * 7 + [ANY],
        out_specs=[ANY, VM],
        input_output_aliases={7: 0},
        out_shape=[
            jax.ShapeDtypeStruct((6, 8, 128, 768), bf16),
            jax.ShapeDtypeStruct((2, 4, 128, 128), f32),
        ],
        scratch_shapes=[
            pltpu.VMEM((4, 8, 128, 768), bf16),
            pltpu.VMEM((2, 4, 8, 128), f32),
            pltpu.VMEM((3, 2, 6, 8, 128), f32),
            pltpu.SemaphoreType.DMA((2,)),
        ],
        cost_estimate=pl.CostEstimate(
            flops=6000000000, bytes_accessed=9000000, transcendentals=0
        ),
        compiler_params=LARGE,
        name="ends_pairs",
    )(side, own, *sides, *ends, part, weights)


def spline_row(place):
    point = lax.broadcasted_iota(jnp.int32, (PC, 128), 0).astype(f32)
    away = jnp.abs(point - place)
    near = (4.0 - 6.0 * away * away + 3.0 * away * away * away) * (1.0 / 6.0)
    rest = 2.0 - away
    far = rest * rest * rest * (1.0 / 6.0)
    return jnp.where(away < 1.0, near, jnp.where(away < 2.0, far, 0.0))


def message_kernel(
    side_ref, own_ref, left_ref, right_ref, before_own, after_own, before_side, after_side, before_end,
    after_end, part_ref, read_ref, _,
    weight_out, total_ref, mesh_ref, row_place_ref,
    weight_ref, position_ref, centre_ref, high_ref, low_ref, charge_ref, left_rows, right_rows, sems
):
    refs = ((before_own, before_side, before_end), (after_own, after_side, after_end))

    def cell(side, dy, z):
        own, beside, end = refs[side]
        if z in (0, 5):
            return end.at[dy, 0, z // 5]
        return own.at[0, z - 1] if dy == 1 else beside.at[dy // 2, 0, z - 1]

    centres_of(own_ref, centre_ref)
    for side in range(2):
        for dy in range(3):
            for z in range(6):
                position_ref[side, dy, z] = position_of(cell(side, dy, z)[128:144, :])
        for z in range(6):
            row_place_ref[3 * side, z] = place_of(cell(side, 1, z)[128:144, :])

    def row_places(x, carry):
        row_place_ref[1 + x, 0] = place_of(left_ref[1, x, 0, 128:144, :])
        for z in range(4):
            row_place_ref[1 + x, 1 + z] = place_of(own_ref[x, z, 128:144, :])
        row_place_ref[1 + x, 5] = place_of(right_ref[1, x, 0, 128:144, :])
        return carry

    lax.fori_loop(0, 2, row_places, 0)

    def column(side, carry):
        def store(block, lane, tile):
            weight_ref[side, block, :, lane : lane + 128] = tile

        def near(dy, z):
            return position_ref[side, dy, z]

        weigh(centre_ref, side, (2 * side - 1).astype(f32), side_ref[...], near, store, ENDS + INSIDE)
        return carry

    lax.fori_loop(0, 2, column, 0)
    copies = [pltpu.make_async_copy(weight_ref, weight_out.at[pl.ds(4, 2)], sems.at[0])]
    for copy in copies:
        copy.start()
    total_ref[...] = part_ref[...]
    for side in range(2):
        add_near(
            weight_ref, side, side, lambda dy, z: cell(side, dy, z), total_ref, ENDS + INSIDE
        )

    def finish(index, carry):
        preact = total_ref[index // 4, index % 4]
        silu = preact * (0.5 + 0.5 * jnp.tanh(0.5 * preact))
        high = silu.astype(bf16)
        high_ref[index] = high
        low_ref[index] = (silu - high.astype(f32)).astype(bf16)
        return carry

    lax.fori_loop(0, 8, finish, 0, unroll=2)
    wide = jnp.broadcast_to(read_ref[...], (16, 128))
    charge_ref[...] = dot_t(wide, high_ref[...].reshape(1024, 128)) + dot_t(
        wide, low_ref[...].reshape(1024, 128)
    )
    block = lax.broadcasted_iota(jnp.int32, (128, 128), 0) // PC

    def spread(cell, carry):
        lanes = pl.ds(pl.multiple_of(cell * 128, 128), 128)
        place = row_place_ref[1 + cell // 4, 1 + cell % 4]
        row_x = spline_row(place[0:1])
        row_y = spline_row(place[1:2]) * charge_ref[0:1, lanes]
        row_z = spline_row(place[2:3])
        left_rows[:, lanes] = (
            (row_y[:, None, :] * row_x[None, :, :]).reshape(PC * PC, 128).astype(bf16)
        )
        right_rows[:, lanes] = jnp.where(block == cell, jnp.tile(row_z, (8, 1)), 0.0).astype(bf16)
        return carry

    lax.fori_loop(0, 8, spread, 0)
    mesh_ref[...] = dot_t(left_rows[...], right_rows[...]).reshape(PC, PC, 128).astype(bf16)
    for copy in copies:
        copy.wait()


def message_layer(side, own, ends, outer, corners, part, read, weights):
    return pl.pallas_call(
        message_kernel,
        in_specs=[VM] * 12 + [ANY],
        out_specs=[ANY, VM, VM, VM],
        input_output_aliases={12: 0},
        out_shape=[
            jax.ShapeDtypeStruct((6, 8, 128, 768), bf16),
            jax.ShapeDtypeStruct((2, 4, 128, 128), f32),
            jax.ShapeDtypeStruct((PC, PC, 128), bf16),
            jax.ShapeDtypeStruct((4, 6, 8, 128), f32),
        ],
        scratch_shapes=[
            pltpu.VMEM((2, 8, 128, 768), bf16),
            pltpu.VMEM((2, 3, 6, 8, 128), f32),
            pltpu.VMEM((2, 4, 8, 128), f32),
            pltpu.VMEM((8, 128, 128), bf16),
            pltpu.VMEM((8, 128, 128), bf16),
            pltpu.VMEM((16, 1024), f32),
            pltpu.VMEM((PC * PC, 1024), bf16),
            pltpu.VMEM((128, 1024), bf16),
            pltpu.SemaphoreType.DMA((1,)),
        ],
        cost_estimate=pl.CostEstimate(
            flops=5000000000, bytes_accessed=6000000, transcendentals=8 * 16384
        ),
        compiler_params=LARGE,
        name="message",
    )(side, own, *ends, *outer, *corners, part, read, weights)


def slope_kernel(total_ref, read_ref, out_ref):
    read = read_ref[...].astype(f32)

    def one(index, carry):
        a, c = index // 4, index % 4
        preact = total_ref[a, c]
        sigma = 0.5 + 0.5 * jnp.tanh(0.5 * preact)
        out_ref[a, c] = (read * (sigma * (1.0 + preact * (1.0 - sigma)))).astype(bf16)
        return carry

    lax.fori_loop(0, 8, one, 0, unroll=2)


def slope_of(total, read):
    return pl.pallas_call(
        slope_kernel,
        in_specs=[VM] * 2,
        out_specs=VM,
        out_shape=jax.ShapeDtypeStruct(total.shape, bf16),
        cost_estimate=pl.CostEstimate(
            flops=8 * 16384 * 8, bytes_accessed=900000, transcendentals=8 * 16384
        ),
        compiler_params=SMALL,
        name="slope",
    )(total, read)


def forward_kernel(mesh_ref, along_z_ref, along_x_ref, out_ref):
    lane = lax.broadcasted_iota(jnp.int32, (64, 128), 1)
    total = jnp.zeros((128, 256), f32)
    for g in range(4):
        mesh = mesh_ref[:, g].reshape(64, 128)
        none = jnp.zeros_like(mesh)
        halves = jnp.concatenate(
            [jnp.where(lane < 64, mesh, none), jnp.where(lane < 64, none, mesh)], axis=0
        )
        table = along_z_ref[g * 64 : (g + 1) * 64, :]
        total = total + dot(halves, jnp.concatenate([table, table], axis=0))
    lines = total.astype(bf16)
    waves = dot(along_x_ref[...], lines)
    out_ref[0:128, :] = waves[:, :128]
    out_ref[128:256, :] = waves[:, 128:]


def forward_xz(mesh, along_z, along_x):
    return pl.pallas_call(
        forward_kernel,
        in_specs=[VM] * 3,
        out_specs=VM,
        compiler_params=SMALL,
        out_shape=jax.ShapeDtypeStruct((256, 128), f32),
        cost_estimate=pl.CostEstimate(
            flops=2 * 64 * 512 * 512, bytes_accessed=800000, transcendentals=0
        ),
        name="forward_xz",
    )(mesh, along_z, along_x)


def filter_kernel(lines_ref, into_ref, influence_ref, out_ref):
    waves = dot(into_ref[...], lines_ref[...].astype(bf16))
    scaled = influence_ref[...] * waves
    power = jnp.sum(jnp.sum(scaled * waves, axis=0, keepdims=True), axis=1, keepdims=True)
    out_ref[pl.ds(0, 256, stride=2), :] = lax.dot_general(
        into_ref[...],
        scaled.astype(bf16),
        (((0,), (0,)), ((), ())),
        preferred_element_type=f32,
    )
    out_ref[pl.ds(1, 256, stride=2), :] = jnp.broadcast_to(power, (256, 128))


def filter_y(lines, into, influence):
    return pl.pallas_call(
        filter_kernel,
        in_specs=[VM] * 3,
        out_specs=VM,
        compiler_params=SMALL,
        out_shape=jax.ShapeDtypeStruct((512, 128), f32),
        cost_estimate=pl.CostEstimate(
            flops=4 * 256 * 256 * 128, bytes_accessed=700000, transcendentals=0
        ),
        name="filter_y",
    )(lines, into, influence)


def inverse_kernel(energy_scale, lines_ref, along_x_ref, along_z_ref, out_ref, energy_ref):
    waves = jnp.concatenate(
        [lines_ref[pl.ds(0, 128, stride=2), :], lines_ref[pl.ds(256, 128, stride=2), :]], axis=1
    ).astype(bf16)
    half = dot(along_x_ref[...], waves).astype(bf16)
    field = dot(half, along_z_ref[...]).astype(bf16)
    for gx in range(4):
        for gz in range(4):
            out_ref[gx, gz] = field[gx * 64 : (gx + 1) * 64, gz * 128 : (gz + 1) * 128]
    power = jnp.sum(lines_ref[pl.ds(1, 256, stride=2), :], axis=0, keepdims=True)
    energy_ref[...] = jnp.broadcast_to(power * energy_scale, (8, 128))


def inverse_xz(lines, along_x, along_z, energy_scale):
    return pl.pallas_call(
        functools.partial(inverse_kernel, energy_scale),
        in_specs=[VM] * 3,
        out_specs=[VM, VM],
        compiler_params=SMALL,
        out_shape=[
            jax.ShapeDtypeStruct((4, 4, 64, 128), bf16),
            jax.ShapeDtypeStruct((8, 128), f32),
        ],
        cost_estimate=pl.CostEstimate(
            flops=2 * 256 * 256 * 640, bytes_accessed=900000, transcendentals=0
        ),
        name="inverse_xz",
    )(lines, along_x, along_z)


def interpolate_kernel(
    field_scale, field_ref, place_ref, stored_ref, rows_ref, before_ref, after_ref,
    out_ref, own_ref, weight_ref, slope_ref, sems
):
    pairs = [
        (rows_ref, slope_ref.at[:, pl.ds(1, 2)]),
        (before_ref, slope_ref.at[:, pl.ds(0, 1)]),
        (after_ref, slope_ref.at[:, pl.ds(3, 1)]),
        (stored_ref.at[:, :, :, pl.ds(512, 256)], weight_ref),
    ]
    copies = [
        pltpu.make_async_copy(source, target, sems.at[i])
        for i, (source, target) in enumerate(pairs)
    ]
    for copy in copies:
        copy.start()
    block = lax.broadcasted_iota(jnp.int32, (128, 128), 0) // PC

    def gather(step, carry):
        ax, half = step // 2, 3 * (step % 2)
        field = field_ref[:, pl.ds(pl.multiple_of(ax * PC, PC), PC), :].reshape(PC * PC, 128)
        for third in range(3):
            cz = half + third
            place = place_ref[ax * 6 + cz]
            row_x = spline_row(place[0:1])
            row_y = spline_row(place[1:2])
            row_z = spline_row(place[2:3])
            right = jnp.where(block == cz + 1, jnp.tile(row_z, (8, 1)), 0.0).astype(bf16)
            partial = dot(field, right)
            left = (row_y[:, None, :] * row_x[None, :, :]).reshape(PC * PC, 128)
            out_ref[pl.ds(ax * 6 + cz, 1), :] = (
                jnp.sum(partial * left, axis=0, keepdims=True) * field_scale
            )
        return carry

    lax.fori_loop(0, 8, gather, 0)
    own_ref[0:4, :] = out_ref[7:11, :]
    own_ref[4:8, :] = out_ref[13:17, :]
    for copy in copies:
        copy.wait()


def interpolate(field, place, weights, slopes, field_scale):
    return pl.pallas_call(
        functools.partial(interpolate_kernel, field_scale),
        in_specs=[VM] * 2 + [ANY] * 4,
        out_specs=[VM] * 4,
        compiler_params=FIELD,
        out_shape=[
            jax.ShapeDtypeStruct((24, 128), f32),
            jax.ShapeDtypeStruct((8, 128), f32),
            jax.ShapeDtypeStruct((6, 8, 128, 256), bf16),
            jax.ShapeDtypeStruct((3, 4, 6, 128, 128), bf16),
        ],
        scratch_shapes=[pltpu.SemaphoreType.DMA((4,))],
        cost_estimate=pl.CostEstimate(
            flops=24 * 2 * 256 * 128 * 128, bytes_accessed=400000, transcendentals=0
        ),
        name="interpolate",
    )(field, place, weights, *slopes)


def combination_of(t):
    return jnp.where(t < 4, 1 + t // 2, 3 * (t - 4)), t % 2


def scaled(columns, cell, slope):
    return (columns[:, cell : cell + 1] * slope.astype(f32)).astype(bf16)


def beside_kernel(
    stored_ref, weight_ref, slope_ref, potential_ref, rest_ref, total_ref, own_out, near_ref, sems
):
    copies = [
        pltpu.make_async_copy(
            stored_ref.at[pl.ds(i, 3), :, :, pl.ds(0, 512)], rest_ref.at[pl.ds(i, 3)], sems.at[i // 3]
        )
        for i in (0, 3)
    ]
    for copy in copies:
        copy.start()
    columns = jnp.transpose(potential_ref[...])
    for x in range(4):
        for z in range(6):
            near_ref[x, z] = scaled(columns, x * 6 + z, slope_ref[1, x, z])
    own_out[...] = near_ref[1:3, 1:5]
    total_ref[...] = jnp.zeros_like(total_ref)

    def combination(t, carry):
        x, a = combination_of(t)
        for pair, (start, stop, first, width) in enumerate(SPANS):
            part = dot(
                weight_ref[t, start:stop].reshape(width * 128, 256),
                near_ref[x, 2 * pair : 2 * pair + 2].reshape(256, 128),
            )
            total_ref[a, first : first + width] += part.reshape(width, 128, 128)
        return carry

    lax.fori_loop(0, 6, combination, 0)
    for copy in copies:
        copy.wait()


def beside(stored, weights, slopes, potential):
    return pl.pallas_call(
        beside_kernel,
        in_specs=[ANY] + [VM] * 3,
        out_specs=[VM] * 3,
        out_shape=[
            jax.ShapeDtypeStruct((6, 8, 128, 512), bf16),
            jax.ShapeDtypeStruct((2, 4, 128, 128), f32),
            jax.ShapeDtypeStruct((2, 4, 128, 128), bf16),
        ],
        scratch_shapes=[
            pltpu.VMEM((4, 6, 128, 128), bf16),
            pltpu.SemaphoreType.DMA((2,)),
        ],
        cost_estimate=pl.CostEstimate(
            flops=3000000000, bytes_accessed=12000000, transcendentals=0
        ),
        compiler_params=MIDDLE,
        name="beside",
    )(stored, weights, slopes, potential)


def backward_kernel(
    weight_ref, slope_ref, part_ref, own_ref, below_ref, above_ref, msg_ref, self_ref, out_ref,
    near_ref, total_ref, potential_ref
):
    potential_ref[0] = below_ref[...]
    potential_ref[1] = above_ref[...]

    def scale(side, carry):
        columns = jnp.transpose(potential_ref[side])
        for x in range(4):
            for z in range(6):
                near_ref[side, x, z] = scaled(columns, x * 6 + z, slope_ref[2 * side, x, z])
        return carry

    lax.fori_loop(0, 2, scale, 0)
    total_ref[...] = part_ref[...]

    def combination(t, carry):
        x, a = combination_of(t)
        for pair, (start, stop, first, width) in enumerate(SPANS):
            near = jnp.concatenate(
                [
                    near_ref[side, x, 2 * pair : 2 * pair + 2].reshape(256, 128)
                    for side in range(2)
                ],
                axis=0,
            )
            part = dot(weight_ref[t, start:stop].reshape(width * 128, 512), near)
            total_ref[a, first : first + width] += part.reshape(width, 128, 128)
        return carry

    lax.fori_loop(0, 6, combination, 0, unroll=2)

    def finish(a, carry):
        back = total_ref[a].reshape(512, 128).astype(bf16)
        own = own_ref[a].reshape(512, 128)
        out_ref[a] = (dot_t(back, msg_ref[...]) + dot_t(own, self_ref[...])).reshape(4, 128, 128)
        return carry

    lax.fori_loop(0, 2, finish, 0)


def backward(weights, slope, part, own, below, above, msg_weight, self_weight):
    return pl.pallas_call(
        backward_kernel,
        in_specs=[VM] * 8,
        out_specs=VM,
        out_shape=jax.ShapeDtypeStruct((2, 4, 128, 128), f32),
        scratch_shapes=[
            pltpu.VMEM((2, 4, 6, 128, 128), bf16),
            pltpu.VMEM((2, 4, 128, 128), f32),
            pltpu.VMEM((2, 24, 128), f32),
        ],
        cost_estimate=pl.CostEstimate(
            flops=4000000000, bytes_accessed=12000000, transcendentals=0
        ),
        compiler_params=SMALL,
        name="backward",
    )(weights, slope, part, own, below, above, msg_weight, self_weight)


def wave_tables(size_x, size_y, size_z):
    i16 = np.arange(16)
    points_x = np.array([g * 32 + a * 16 + i for a in range(2) for g in range(4) for i in i16])
    along_x = cas(np.arange(size_x), points_x, size_x)
    points_y = np.array(
        [gy * 16 + gx * 4 + gz for gx in range(4) for gy in range(16) for gz in range(4)]
    )
    into_y = cas(np.arange(size_y), points_y, size_y)
    back_x = np.array(
        [((2 * g - 1 + a) % 8) * 16 + i for g in range(4) for a in range(4) for i in i16]
    )
    back_z = np.array(
        [((4 * g - 2 + c) % 16) * 16 + k for g in range(4) for c in range(8) for k in i16]
    )
    tables = (
        cas(np.arange(size_z), np.arange(size_z), size_z),
        along_x,
        into_y,
        cas(back_x, np.arange(size_x), size_x),
        cas(np.arange(size_z), back_z, size_z),
    )
    return [jnp.asarray(np.ascontiguousarray(t), dtype=bf16) for t in tables]


def influence_of(size_x, size_y, size_z):
    device = lax.axis_index(everyone)

    def wave(index, size):
        signed = jnp.where(2 * index >= size, index - size, index)
        return signed.astype(f32) * (PC / size)

    wave_x = wave(device % size_x, size_x)
    wave_y = wave(jnp.arange(size_y, dtype=jnp.int32), size_y)[:, None]
    wave_z = wave(
        device // size_x * 128 + jnp.arange(size_z // 2, dtype=jnp.int32), size_z
    )[None, :]
    squared = wave_x * wave_x + wave_y * wave_y + wave_z * wave_z
    safe = jnp.where(squared > 0, squared, 1.0)
    return jnp.where(squared > 0, jnp.exp(-((math.pi * spread_width) ** 2) * squared) / safe, 0.0)


def swapped(value, axis):
    return lax.all_to_all(value, axis, split_axis=0, concat_axis=0, tiled=True)


def body(features, msg_weight, self_weight, charge_weight, spline_corner, spline_fraction):
    cells_x, cells_y, cells_z, slots, width = features.shape
    size_x = cells_x * PC * lax.axis_size("gx")
    size_y = cells_y * PC * lax.axis_size("gy")
    size_z = cells_z * PC * lax.axis_size("gz")
    volume = size_x // PC * (size_y // PC) * (size_z // PC)
    natoms = volume * slots
    cells = cells_x * cells_z

    features_own = features.reshape(cells, slots, width)
    own = project(
        features_own, msg_weight, spline_corner.swapaxes(2, 3), spline_fraction.swapaxes(2, 3)
    )
    own = own.reshape(cells_x, cells_z, slots + 16, width)
    sides, ends, outer, corners = early_halo(own)
    side = jnp.full((1, slots), 1 - 2 * (lax.axis_index("gy") % 2), f32)
    weights, part = inside_pairs(side, own, sides, features_own, self_weight)
    weights, part = ends_pairs(side, own, sides, ends, part, weights)
    influence = influence_of(size_x, size_y, size_z)
    along_z, along_x, into_y, back_x, back_z = wave_tables(size_x, size_y, size_z)

    read = charge_weight[None, :]
    weights, preact, mesh, row_place = message_layer(
        side, own, ends, outer, corners, part, read, weights
    )
    mesh = swapped(mesh, plane).reshape(4, 4, PC, 128)
    slope_near = late_halo(slope_of(preact, read))
    lines = swapped(forward_xz(mesh, along_z, along_x), everyone)
    lines = swapped(filter_y(lines, into_y, influence), everyone)
    field, energy = inverse_xz(lines, back_x, back_z, coupling / (2.0 * volume * natoms))
    field = swapped(field.reshape(16, 64, 128), plane)
    potential, atom_potential, own_weights, slopes = interpolate(
        field, row_place.reshape(24, 8, slots), weights, slope_near, coupling / volume
    )
    below, above = partners(potential)
    weights, total, cotangent = beside(weights, own_weights, slopes, potential)
    grad = backward(weights, slopes, total, cotangent, below, above, msg_weight, self_weight)
    return (
        grad.reshape(features.shape),
        atom_potential.reshape(cells_x, cells_y, cells_z, slots),
        energy[0, 0],
    )


def solution(mesh):
    in_specs = (
        P("gx", "gy", "gz", None, None),
        P(),
        P(),
        P(),
        P("gx", "gy", "gz", None, None),
        P("gx", "gy", "gz", None, None),
    )
    out_specs = (P("gx", "gy", "gz", None, None), P("gx", "gy", "gz", None), P())
    return jax.shard_map(body, mesh=mesh, in_specs=in_specs, out_specs=out_specs, check_vma=False)
```

```python
import functools
import math

import jax
import jax.numpy as jnp
import numpy as np
from jax import lax
from jax.experimental import pallas as pl
from jax.experimental.pallas import tpu as pltpu
from jax.sharding import PartitionSpec as P

PC = 16
pair_scale = 0.1
coupling = 0.125
spread_width = 0.0625
f32 = jnp.float32
bf16 = jnp.bfloat16
plane = ("gx", "gz")
everyone = ("gx", "gy", "gz")


def dot(a, b):
    return jnp.dot(a, b, preferred_element_type=f32)


def dot_t(a, b, precision=None):
    return lax.dot_general(
        a, b, (((1,), (1,)), ((), ())), preferred_element_type=f32, precision=precision
    )


def whole(shape):
    zeros = (0,) * len(shape)
    return pl.BlockSpec(shape, lambda *_: zeros)


VM = pl.BlockSpec(memory_space=pltpu.VMEM)
ANY = pl.BlockSpec(memory_space=pl.ANY)
SMALL = pltpu.CompilerParams(vmem_limit_bytes=20 << 20)
FIRST = pltpu.CompilerParams(vmem_limit_bytes=60 << 20)
LARGE = pltpu.CompilerParams(vmem_limit_bytes=50 << 20)
MIDDLE = pltpu.CompilerParams(vmem_limit_bytes=40 << 20)
FIELD = pltpu.CompilerParams(vmem_limit_bytes=44 << 20)


def cas(rows, columns, size):
    turns = np.outer(rows, columns) % size
    angle = 2.0 * np.pi / size * turns
    return np.cos(angle) + np.sin(angle)


def moved(value, axis, step):
    count = lax.axis_size(axis)
    pairs = [(i, (i + step) % count) for i in range(count)]
    return lax.ppermute(value.reshape(-1, 128), axis, pairs).reshape(value.shape)


def partners(value):
    count = lax.axis_size("gy")
    across = [(i, (i + 1 if i % 2 else i - 1) % count) for i in range(count)]
    within = [(i, i ^ 1) for i in range(count)]
    return [lax.ppermute(value, "gy", pairs) for pairs in (across, within)]


def late_halo(own):
    last_x, last_z = own.shape[0] - 1, own.shape[1] - 1
    left, right = moved(own[:, last_z:], "gz", 1), moved(own[:, :1], "gz", -1)
    row = jnp.concatenate([left, own, right], axis=1)
    rows = jnp.stack([moved(row, "gy", 1), row, moved(row, "gy", -1)])
    return [rows, moved(rows[:, last_x:], "gx", 1), moved(rows[:, :1], "gx", -1)]


def early_halo(own):
    last_x, last_z = own.shape[0] - 1, own.shape[1] - 1
    below, above = moved(own, "gy", 1), moved(own, "gy", -1)
    beside = [moved(own[last_x:], "gx", 1), moved(own[:1], "gx", -1)]
    sides = jnp.stack([below, above])
    rows = [below, own, above]
    left = moved(jnp.stack([row[:, last_z:] for row in rows]), "gz", 1)
    right = moved(jnp.stack([row[:, :1] for row in rows]), "gz", -1)
    aside = [moved(sides[:, last_x:], "gx", 1), moved(sides[:, :1], "gx", -1)]
    corners = [
        moved(jnp.concatenate([left[:, at : at + 1], right[:, at : at + 1]], axis=2), "gx", step)
        for at, step in ((last_x, 1), (0, -1))
    ]
    return [below, above], [left, right], beside + aside, corners


def project_kernel(features_ref, weight_ref, corner_ref, fraction_ref, out_ref):
    value = dot(features_ref[...].reshape(1024, 128), weight_ref[...]).astype(bf16)
    out_ref[:, :128, :] = value.reshape(8, 128, 128)
    none = jnp.zeros((5, 128), f32)
    for x in range(2):
        place = corner_ref[x, 0].astype(f32) + 1.0 + fraction_ref[x, 0]
        high = place.astype(bf16).astype(f32)
        rest = place - high
        middle = rest.astype(bf16).astype(f32)
        low = rest - middle
        for z in range(4):
            rows = [part[d, z : z + 1] for part in (high, low) for d in range(3)]
            rows += [none[:2]] + [middle[d, z : z + 1] for d in range(3)] + [none]
            out_ref[x * 4 + z, 128:, :] = jnp.concatenate(rows, axis=0).astype(bf16)


def project(features, weight, corner, fraction):
    return pl.pallas_call(
        project_kernel,
        grid=(1,),
        in_specs=[whole((8, 128, 128)), whole((128, 128))]
        + [whole((2, 1, 3, 4, 128))] * 2,
        out_specs=whole((8, 144, 128)),
        out_shape=jax.ShapeDtypeStruct((8, 144, 128), bf16),
        compiler_params=FIRST,
        name="project",
    )(features, weight, corner, fraction)


def place_of(rows):
    rows = rows.astype(f32)
    return rows[0:8] + rows[8:16] + pltpu.roll(rows[0:8], 5, 0)


BLOCKS = ((0, 0), (0, 1), (1, 0), (1, 1), (1, 2), (1, 3), (2, 2), (2, 3))
SPANS = ((0, 2, 0, 2), (2, 6, 0, 4), (6, 8, 2, 2))
ORDER_Y = (0, 2, 1)


def position_of(rows):
    return (place_of(rows) * (1.0 / PC)).astype(bf16).astype(f32)


def weigh(centres, a, shift, near, store, pairs):
    for c in range(4):
        columns = jnp.transpose(centres[a, c])
        centre_x = jnp.broadcast_to(columns[:, 0:1], (128, 128))
        centre_y = jnp.broadcast_to(columns[:, 1:2], (128, 128))
        centre_z = jnp.broadcast_to(columns[:, 2:3], (128, 128))
        for block, (pair, owner) in enumerate(BLOCKS):
            if owner != c or pair not in pairs:
                continue
            for at, dy in enumerate(ORDER_Y):
                for half in range(2):
                    dz = 2 * pair + half - c - 1
                    if abs(dz) > 1:
                        tile = jnp.zeros((128, 128), bf16)
                    else:
                        row = near(dy, 2 * pair + half)
                        gap_x = (row[0:1] + shift) - centre_x
                        gap_y = (row[1:2] + (dy - 1.0)) - centre_y
                        gap_z = (row[2:3] + float(dz)) - centre_z
                        squared = gap_x * gap_x + gap_y * gap_y + gap_z * gap_z
                        inside = jnp.maximum(1.0 - squared, 0.0)
                        tile = (pair_scale * inside * inside).astype(bf16)
                    store(block, (at * 2 + half) * 128, tile)


def add_near(weight_ref, t, a, cell, total_ref, pairs):
    for pair in pairs:
        start, stop, first, width = SPANS[pair]
        near = jnp.concatenate(
            [cell(dy, 2 * pair + half)[0:128, :] for dy in ORDER_Y for half in range(2)], axis=0
        )
        part = dot(weight_ref[t, start:stop].reshape(width * 128, 768), near)
        total_ref[a, first : first + width] += part.reshape(width, 128, 128)


def columns_kernel(first, count, weight_ref, weight_out, sems, slot, spans):
    return [
        pltpu.make_async_copy(
            weight_ref.at[pl.ds(first, count), pl.ds(start, size)],
            weight_out.at[pl.ds(first, count), pl.ds(start, size)],
            sems.at[slot + i],
        )
        for i, (start, size) in enumerate(spans)
    ]


INSIDE = (1,)
ENDS = (0, 2)
INSIDE_BLOCKS = ((2, 4),)
END_BLOCKS = ((0, 2), (6, 2))


def centres_of(own_ref, centre_ref):
    def one(cell, carry):
        x, z = cell // 4, cell % 4
        centre_ref[x, z] = position_of(own_ref[x, z, 128:144, :])
        return carry

    lax.fori_loop(0, 8, one, 0)


def inside_kernel(
    own_ref, below_ref, above_ref, features_ref, self_ref,
    weight_out, total_ref, weight_ref, position_ref, sems
):
    refs = (below_ref, own_ref, above_ref)

    def positions(x, carry):
        for dy in range(3):
            for z in range(4):
                position_ref[dy, x, z] = position_of(refs[dy][x, z, 128:144, :])
        return carry

    lax.fori_loop(0, 2, positions, 0)
    total_ref[...] = dot(features_ref[...].reshape(1024, 128), self_ref[...]).reshape(
        2, 4, 128, 128
    )

    def column(t, carry):
        x, a = t // 2, t % 2

        def store(block, lane, tile):
            weight_ref[t, block, :, lane : lane + 128] = tile

        def near(dy, z):
            return position_ref[dy, x, z - 1]

        weigh(position_ref.at[1], a, (x - a).astype(f32), near, store, INSIDE)
        add_near(weight_ref, t, a, lambda dy, z: refs[dy].at[x, z - 1], total_ref, INSIDE)
        return carry

    lax.fori_loop(0, 4, column, 0)
    copies = columns_kernel(0, 4, weight_ref, weight_out, sems, 0, INSIDE_BLOCKS)
    for copy in copies:
        copy.start()
    for copy in copies:
        copy.wait()


def inside_pairs(own, sides, features, self_weight):
    return pl.pallas_call(
        inside_kernel,
        in_specs=[VM] * 5,
        out_specs=[ANY, VM],
        out_shape=[
            jax.ShapeDtypeStruct((6, 8, 128, 768), bf16),
            jax.ShapeDtypeStruct((2, 4, 128, 128), f32),
        ],
        scratch_shapes=[
            pltpu.VMEM((4, 8, 128, 768), bf16),
            pltpu.VMEM((3, 2, 4, 8, 128), f32),
            pltpu.SemaphoreType.DMA((1,)),
        ],
        cost_estimate=pl.CostEstimate(
            flops=5000000000, bytes_accessed=9000000, transcendentals=0
        ),
        compiler_params=LARGE,
        name="inside_pairs",
    )(own, *sides, features, self_weight)


def ends_kernel(
    own_ref, below_ref, above_ref, left_ref, right_ref,
    part_ref, _, weight_out, total_ref, weight_ref, centre_ref, position_ref, sems
):
    refs = (below_ref, own_ref, above_ref)

    def cell(dy, x, z):
        if z == 0:
            return left_ref.at[dy, x, 0]
        if z == 5:
            return right_ref.at[dy, x, 0]
        return refs[dy].at[x, z - 1]

    centres_of(own_ref, centre_ref)

    def positions(x, carry):
        for dy in range(3):
            for z in (0, 1, 4, 5):
                position_ref[dy, x, z] = position_of(cell(dy, x, z)[128:144, :])
        return carry

    lax.fori_loop(0, 2, positions, 0)
    total_ref[...] = part_ref[...]

    def column(t, carry):
        x, a = t // 2, t % 2

        def store(block, lane, tile):
            weight_ref[t, block, :, lane : lane + 128] = tile

        def near(dy, z):
            return position_ref[dy, x, z]

        weigh(centre_ref, a, (x - a).astype(f32), near, store, ENDS)
        add_near(weight_ref, t, a, lambda dy, z: cell(dy, x, z), total_ref, ENDS)
        return carry

    lax.fori_loop(0, 4, column, 0)
    copies = columns_kernel(0, 4, weight_ref, weight_out, sems, 0, END_BLOCKS)
    for copy in copies:
        copy.start()

    for copy in copies:
        copy.wait()


def ends_pairs(own, sides, ends, part, weights):
    return pl.pallas_call(
        ends_kernel,
        in_specs=[VM] * 6 + [ANY],
        out_specs=[ANY, VM],
        input_output_aliases={6: 0},
        out_shape=[
            jax.ShapeDtypeStruct((6, 8, 128, 768), bf16),
            jax.ShapeDtypeStruct((2, 4, 128, 128), f32),
        ],
        scratch_shapes=[
            pltpu.VMEM((4, 8, 128, 768), bf16),
            pltpu.VMEM((2, 4, 8, 128), f32),
            pltpu.VMEM((3, 2, 6, 8, 128), f32),
            pltpu.SemaphoreType.DMA((2,)),
        ],
        cost_estimate=pl.CostEstimate(
            flops=6000000000, bytes_accessed=9000000, transcendentals=0
        ),
        compiler_params=LARGE,
        name="ends_pairs",
    )(own, *sides, *ends, part, weights)


def spline_row(place):
    point = lax.broadcasted_iota(jnp.int32, (PC, 128), 0).astype(f32)
    away = jnp.abs(point - place)
    near = (4.0 - 6.0 * away * away + 3.0 * away * away * away) * (1.0 / 6.0)
    rest = 2.0 - away
    far = rest * rest * rest * (1.0 / 6.0)
    return jnp.where(away < 1.0, near, jnp.where(away < 2.0, far, 0.0))


def message_kernel(
    own_ref, left_ref, right_ref, before_own, after_own, before_side, after_side, before_end,
    after_end, part_ref, read_ref, _,
    weight_out, total_ref, mesh_ref, row_place_ref,
    weight_ref, position_ref, centre_ref, high_ref, low_ref, charge_ref, left_rows, right_rows, sems
):
    refs = ((before_own, before_side, before_end), (after_own, after_side, after_end))

    def cell(side, dy, z):
        own, beside, end = refs[side]
        if z in (0, 5):
            return end.at[dy, 0, z // 5]
        return own.at[0, z - 1] if dy == 1 else beside.at[dy // 2, 0, z - 1]

    centres_of(own_ref, centre_ref)
    for side in range(2):
        for dy in range(3):
            for z in range(6):
                position_ref[side, dy, z] = position_of(cell(side, dy, z)[128:144, :])
        for z in range(6):
            row_place_ref[3 * side, z] = place_of(cell(side, 1, z)[128:144, :])

    def row_places(x, carry):
        row_place_ref[1 + x, 0] = place_of(left_ref[1, x, 0, 128:144, :])
        for z in range(4):
            row_place_ref[1 + x, 1 + z] = place_of(own_ref[x, z, 128:144, :])
        row_place_ref[1 + x, 5] = place_of(right_ref[1, x, 0, 128:144, :])
        return carry

    lax.fori_loop(0, 2, row_places, 0)

    def column(side, carry):
        def store(block, lane, tile):
            weight_ref[side, block, :, lane : lane + 128] = tile

        def near(dy, z):
            return position_ref[side, dy, z]

        weigh(centre_ref, side, (2 * side - 1).astype(f32), near, store, ENDS + INSIDE)
        return carry

    lax.fori_loop(0, 2, column, 0)
    copies = [pltpu.make_async_copy(weight_ref, weight_out.at[pl.ds(4, 2)], sems.at[0])]
    for copy in copies:
        copy.start()
    total_ref[...] = part_ref[...]
    for side in range(2):
        add_near(
            weight_ref, side, side, lambda dy, z: cell(side, dy, z), total_ref, ENDS + INSIDE
        )

    def finish(index, carry):
        preact = total_ref[index // 4, index % 4]
        silu = preact * (0.5 + 0.5 * jnp.tanh(0.5 * preact))
        high = silu.astype(bf16)
        high_ref[index] = high
        low_ref[index] = (silu - high.astype(f32)).astype(bf16)
        return carry

    lax.fori_loop(0, 8, finish, 0, unroll=2)
    wide = jnp.broadcast_to(read_ref[...], (16, 128))
    charge_ref[...] = dot_t(wide, high_ref[...].reshape(1024, 128)) + dot_t(
        wide, low_ref[...].reshape(1024, 128)
    )
    block = lax.broadcasted_iota(jnp.int32, (128, 128), 0) // PC

    def spread(cell, carry):
        lanes = pl.ds(pl.multiple_of(cell * 128, 128), 128)
        place = row_place_ref[1 + cell // 4, 1 + cell % 4]
        row_x = spline_row(place[0:1])
        row_y = spline_row(place[1:2]) * charge_ref[0:1, lanes]
        row_z = spline_row(place[2:3])
        left_rows[:, lanes] = (
            (row_y[:, None, :] * row_x[None, :, :]).reshape(PC * PC, 128).astype(bf16)
        )
        right_rows[:, lanes] = jnp.where(block == cell, jnp.tile(row_z, (8, 1)), 0.0).astype(bf16)
        return carry

    lax.fori_loop(0, 8, spread, 0)
    mesh_ref[...] = dot_t(left_rows[...], right_rows[...]).reshape(PC, PC, 128).astype(bf16)
    for copy in copies:
        copy.wait()


def message_layer(own, ends, outer, corners, part, read, weights):
    return pl.pallas_call(
        message_kernel,
        in_specs=[VM] * 11 + [ANY],
        out_specs=[ANY, VM, VM, VM],
        input_output_aliases={11: 0},
        out_shape=[
            jax.ShapeDtypeStruct((6, 8, 128, 768), bf16),
            jax.ShapeDtypeStruct((2, 4, 128, 128), f32),
            jax.ShapeDtypeStruct((PC, PC, 128), bf16),
            jax.ShapeDtypeStruct((4, 6, 8, 128), f32),
        ],
        scratch_shapes=[
            pltpu.VMEM((2, 8, 128, 768), bf16),
            pltpu.VMEM((2, 3, 6, 8, 128), f32),
            pltpu.VMEM((2, 4, 8, 128), f32),
            pltpu.VMEM((8, 128, 128), bf16),
            pltpu.VMEM((8, 128, 128), bf16),
            pltpu.VMEM((16, 1024), f32),
            pltpu.VMEM((PC * PC, 1024), bf16),
            pltpu.VMEM((128, 1024), bf16),
            pltpu.SemaphoreType.DMA((1,)),
        ],
        cost_estimate=pl.CostEstimate(
            flops=5000000000, bytes_accessed=6000000, transcendentals=8 * 16384
        ),
        compiler_params=LARGE,
        name="message",
    )(own, *ends, *outer, *corners, part, read, weights)


def slope_kernel(total_ref, read_ref, out_ref):
    read = read_ref[...].astype(f32)

    def one(index, carry):
        a, c = index // 4, index % 4
        preact = total_ref[a, c]
        sigma = 0.5 + 0.5 * jnp.tanh(0.5 * preact)
        out_ref[a, c] = (read * (sigma * (1.0 + preact * (1.0 - sigma)))).astype(bf16)
        return carry

    lax.fori_loop(0, 8, one, 0, unroll=2)


def slope_of(total, read):
    return pl.pallas_call(
        slope_kernel,
        in_specs=[VM] * 2,
        out_specs=VM,
        out_shape=jax.ShapeDtypeStruct(total.shape, bf16),
        cost_estimate=pl.CostEstimate(
            flops=8 * 16384 * 8, bytes_accessed=900000, transcendentals=8 * 16384
        ),
        compiler_params=SMALL,
        name="slope",
    )(total, read)


def forward_kernel(mesh_ref, along_z_ref, along_x_ref, out_ref):
    lane = lax.broadcasted_iota(jnp.int32, (64, 128), 1)
    total = jnp.zeros((128, 256), f32)
    for g in range(4):
        mesh = mesh_ref[:, g].reshape(64, 128)
        none = jnp.zeros_like(mesh)
        halves = jnp.concatenate(
            [jnp.where(lane < 64, mesh, none), jnp.where(lane < 64, none, mesh)], axis=0
        )
        table = along_z_ref[g * 64 : (g + 1) * 64, :]
        total = total + dot(halves, jnp.concatenate([table, table], axis=0))
    lines = total.astype(bf16)
    waves = dot(along_x_ref[...], lines)
    out_ref[0:128, :] = waves[:, :128]
    out_ref[128:256, :] = waves[:, 128:]


def forward_xz(mesh, along_z, along_x):
    return pl.pallas_call(
        forward_kernel,
        in_specs=[VM] * 3,
        out_specs=VM,
        compiler_params=SMALL,
        out_shape=jax.ShapeDtypeStruct((256, 128), f32),
        cost_estimate=pl.CostEstimate(
            flops=2 * 64 * 512 * 512, bytes_accessed=800000, transcendentals=0
        ),
        name="forward_xz",
    )(mesh, along_z, along_x)


def filter_kernel(lines_ref, into_ref, influence_ref, out_ref):
    waves = dot(into_ref[...], lines_ref[...].astype(bf16))
    scaled = influence_ref[...] * waves
    power = jnp.sum(jnp.sum(scaled * waves, axis=0, keepdims=True), axis=1, keepdims=True)
    out_ref[pl.ds(0, 256, stride=2), :] = lax.dot_general(
        into_ref[...],
        scaled.astype(bf16),
        (((0,), (0,)), ((), ())),
        preferred_element_type=f32,
    )
    out_ref[pl.ds(1, 256, stride=2), :] = jnp.broadcast_to(power, (256, 128))


def filter_y(lines, into, influence):
    return pl.pallas_call(
        filter_kernel,
        in_specs=[VM] * 3,
        out_specs=VM,
        compiler_params=SMALL,
        out_shape=jax.ShapeDtypeStruct((512, 128), f32),
        cost_estimate=pl.CostEstimate(
            flops=4 * 256 * 256 * 128, bytes_accessed=700000, transcendentals=0
        ),
        name="filter_y",
    )(lines, into, influence)


def inverse_kernel(energy_scale, lines_ref, along_x_ref, along_z_ref, out_ref, energy_ref):
    waves = jnp.concatenate(
        [lines_ref[pl.ds(0, 128, stride=2), :], lines_ref[pl.ds(256, 128, stride=2), :]], axis=1
    ).astype(bf16)
    half = dot(along_x_ref[...], waves).astype(bf16)
    field = dot(half, along_z_ref[...]).astype(bf16)
    for gx in range(4):
        for gz in range(4):
            out_ref[gx, gz] = field[gx * 64 : (gx + 1) * 64, gz * 128 : (gz + 1) * 128]
    power = jnp.sum(lines_ref[pl.ds(1, 256, stride=2), :], axis=0, keepdims=True)
    energy_ref[...] = jnp.broadcast_to(power * energy_scale, (8, 128))


def inverse_xz(lines, along_x, along_z, energy_scale):
    return pl.pallas_call(
        functools.partial(inverse_kernel, energy_scale),
        in_specs=[VM] * 3,
        out_specs=[VM, VM],
        compiler_params=SMALL,
        out_shape=[
            jax.ShapeDtypeStruct((4, 4, 64, 128), bf16),
            jax.ShapeDtypeStruct((8, 128), f32),
        ],
        cost_estimate=pl.CostEstimate(
            flops=2 * 256 * 256 * 640, bytes_accessed=900000, transcendentals=0
        ),
        name="inverse_xz",
    )(lines, along_x, along_z)


def interpolate_kernel(
    field_scale, field_ref, place_ref, stored_ref, rows_ref, before_ref, after_ref,
    out_ref, own_ref, weight_ref, slope_ref, sems
):
    pairs = [
        (rows_ref, slope_ref.at[:, pl.ds(1, 2)]),
        (before_ref, slope_ref.at[:, pl.ds(0, 1)]),
        (after_ref, slope_ref.at[:, pl.ds(3, 1)]),
        (stored_ref.at[:, :, :, pl.ds(512, 256)], weight_ref),
    ]
    copies = [
        pltpu.make_async_copy(source, target, sems.at[i])
        for i, (source, target) in enumerate(pairs)
    ]
    for copy in copies:
        copy.start()
    block = lax.broadcasted_iota(jnp.int32, (128, 128), 0) // PC

    def gather(step, carry):
        ax, half = step // 2, 3 * (step % 2)
        field = field_ref[:, pl.ds(pl.multiple_of(ax * PC, PC), PC), :].reshape(PC * PC, 128)
        for third in range(3):
            cz = half + third
            place = place_ref[ax * 6 + cz]
            row_x = spline_row(place[0:1])
            row_y = spline_row(place[1:2])
            row_z = spline_row(place[2:3])
            right = jnp.where(block == cz + 1, jnp.tile(row_z, (8, 1)), 0.0).astype(bf16)
            partial = dot(field, right)
            left = (row_y[:, None, :] * row_x[None, :, :]).reshape(PC * PC, 128)
            out_ref[pl.ds(ax * 6 + cz, 1), :] = (
                jnp.sum(partial * left, axis=0, keepdims=True) * field_scale
            )
        return carry

    lax.fori_loop(0, 8, gather, 0)
    own_ref[0:4, :] = out_ref[7:11, :]
    own_ref[4:8, :] = out_ref[13:17, :]
    for copy in copies:
        copy.wait()


def interpolate(field, place, weights, slopes, field_scale):
    return pl.pallas_call(
        functools.partial(interpolate_kernel, field_scale),
        in_specs=[VM] * 2 + [ANY] * 4,
        out_specs=[VM] * 4,
        compiler_params=FIELD,
        out_shape=[
            jax.ShapeDtypeStruct((24, 128), f32),
            jax.ShapeDtypeStruct((8, 128), f32),
            jax.ShapeDtypeStruct((6, 8, 128, 256), bf16),
            jax.ShapeDtypeStruct((3, 4, 6, 128, 128), bf16),
        ],
        scratch_shapes=[pltpu.SemaphoreType.DMA((4,))],
        cost_estimate=pl.CostEstimate(
            flops=24 * 2 * 256 * 128 * 128, bytes_accessed=400000, transcendentals=0
        ),
        name="interpolate",
    )(field, place, weights, *slopes)


def combination_of(t):
    return jnp.where(t < 4, 1 + t // 2, 3 * (t - 4)), t % 2


def scaled(columns, cell, slope):
    return (columns[:, cell : cell + 1] * slope.astype(f32)).astype(bf16)


def beside_kernel(
    stored_ref, weight_ref, slope_ref, potential_ref, rest_ref, total_ref, own_out, near_ref, sems
):
    copies = [
        pltpu.make_async_copy(
            stored_ref.at[pl.ds(i, 3), :, :, pl.ds(0, 512)], rest_ref.at[pl.ds(i, 3)], sems.at[i // 3]
        )
        for i in (0, 3)
    ]
    for copy in copies:
        copy.start()
    columns = jnp.transpose(potential_ref[...])
    for x in range(4):
        for z in range(6):
            near_ref[x, z] = scaled(columns, x * 6 + z, slope_ref[1, x, z])
    own_out[...] = near_ref[1:3, 1:5]
    total_ref[...] = jnp.zeros_like(total_ref)

    def combination(t, carry):
        x, a = combination_of(t)
        for pair, (start, stop, first, width) in enumerate(SPANS):
            part = dot(
                weight_ref[t, start:stop].reshape(width * 128, 256),
                near_ref[x, 2 * pair : 2 * pair + 2].reshape(256, 128),
            )
            total_ref[a, first : first + width] += part.reshape(width, 128, 128)
        return carry

    lax.fori_loop(0, 6, combination, 0)
    for copy in copies:
        copy.wait()


def beside(stored, weights, slopes, potential):
    return pl.pallas_call(
        beside_kernel,
        in_specs=[ANY] + [VM] * 3,
        out_specs=[VM] * 3,
        out_shape=[
            jax.ShapeDtypeStruct((6, 8, 128, 512), bf16),
            jax.ShapeDtypeStruct((2, 4, 128, 128), f32),
            jax.ShapeDtypeStruct((2, 4, 128, 128), bf16),
        ],
        scratch_shapes=[
            pltpu.VMEM((4, 6, 128, 128), bf16),
            pltpu.SemaphoreType.DMA((2,)),
        ],
        cost_estimate=pl.CostEstimate(
            flops=3000000000, bytes_accessed=12000000, transcendentals=0
        ),
        compiler_params=MIDDLE,
        name="beside",
    )(stored, weights, slopes, potential)


def backward_kernel(
    weight_ref, slope_ref, part_ref, own_ref, across_ref, within_ref, side_ref, msg_ref, self_ref,
    out_ref, near_ref, total_ref, potential_ref
):
    even = jnp.broadcast_to(side_ref[...], (24, 128)) > 0.0
    potential_ref[0] = jnp.where(even, across_ref[...], within_ref[...])
    potential_ref[1] = jnp.where(even, within_ref[...], across_ref[...])

    def scale(side, carry):
        columns = jnp.transpose(potential_ref[side])
        for x in range(4):
            for z in range(6):
                near_ref[side, x, z] = scaled(columns, x * 6 + z, slope_ref[2 * side, x, z])
        return carry

    lax.fori_loop(0, 2, scale, 0)
    total_ref[...] = part_ref[...]

    def combination(t, carry):
        x, a = combination_of(t)
        for pair, (start, stop, first, width) in enumerate(SPANS):
            near = jnp.concatenate(
                [
                    near_ref[side, x, 2 * pair : 2 * pair + 2].reshape(256, 128)
                    for side in range(2)
                ],
                axis=0,
            )
            part = dot(weight_ref[t, start:stop].reshape(width * 128, 512), near)
            total_ref[a, first : first + width] += part.reshape(width, 128, 128)
        return carry

    lax.fori_loop(0, 6, combination, 0, unroll=2)

    def finish(a, carry):
        back = total_ref[a].reshape(512, 128).astype(bf16)
        own = own_ref[a].reshape(512, 128)
        out_ref[a] = (dot_t(back, msg_ref[...]) + dot_t(own, self_ref[...])).reshape(4, 128, 128)
        return carry

    lax.fori_loop(0, 2, finish, 0)


def backward(weights, slope, part, own, across, within, side, msg_weight, self_weight):
    return pl.pallas_call(
        backward_kernel,
        in_specs=[VM] * 9,
        out_specs=VM,
        out_shape=jax.ShapeDtypeStruct((2, 4, 128, 128), f32),
        scratch_shapes=[
            pltpu.VMEM((2, 4, 6, 128, 128), bf16),
            pltpu.VMEM((2, 4, 128, 128), f32),
            pltpu.VMEM((2, 24, 128), f32),
        ],
        cost_estimate=pl.CostEstimate(
            flops=4000000000, bytes_accessed=12000000, transcendentals=0
        ),
        compiler_params=SMALL,
        name="backward",
    )(weights, slope, part, own, across, within, side, msg_weight, self_weight)


def wave_tables(size_x, size_y, size_z):
    i16 = np.arange(16)
    points_x = np.array([g * 32 + a * 16 + i for a in range(2) for g in range(4) for i in i16])
    along_x = cas(np.arange(size_x), points_x, size_x)
    points_y = np.array(
        [gy * 16 + gx * 4 + gz for gx in range(4) for gy in range(16) for gz in range(4)]
    )
    into_y = cas(np.arange(size_y), points_y, size_y)
    back_x = np.array(
        [((2 * g - 1 + a) % 8) * 16 + i for g in range(4) for a in range(4) for i in i16]
    )
    back_z = np.array(
        [((4 * g - 2 + c) % 16) * 16 + k for g in range(4) for c in range(8) for k in i16]
    )
    tables = (
        cas(np.arange(size_z), np.arange(size_z), size_z),
        along_x,
        into_y,
        cas(back_x, np.arange(size_x), size_x),
        cas(np.arange(size_z), back_z, size_z),
    )
    return [jnp.asarray(np.ascontiguousarray(t), dtype=bf16) for t in tables]


def influence_of(size_x, size_y, size_z):
    device = lax.axis_index(everyone)

    def wave(index, size):
        signed = jnp.where(2 * index >= size, index - size, index)
        return signed.astype(f32) * (PC / size)

    wave_x = wave(device % size_x, size_x)
    wave_y = wave(jnp.arange(size_y, dtype=jnp.int32), size_y)[:, None]
    wave_z = wave(
        device // size_x * 128 + jnp.arange(size_z // 2, dtype=jnp.int32), size_z
    )[None, :]
    squared = wave_x * wave_x + wave_y * wave_y + wave_z * wave_z
    safe = jnp.where(squared > 0, squared, 1.0)
    return jnp.where(squared > 0, jnp.exp(-((math.pi * spread_width) ** 2) * squared) / safe, 0.0)


def swapped(value, axis):
    return lax.all_to_all(value, axis, split_axis=0, concat_axis=0, tiled=True)


def body(features, msg_weight, self_weight, charge_weight, spline_corner, spline_fraction):
    cells_x, cells_y, cells_z, slots, width = features.shape
    size_x = cells_x * PC * lax.axis_size("gx")
    size_y = cells_y * PC * lax.axis_size("gy")
    size_z = cells_z * PC * lax.axis_size("gz")
    volume = size_x // PC * (size_y // PC) * (size_z // PC)
    natoms = volume * slots
    cells = cells_x * cells_z

    features_own = features.reshape(cells, slots, width)
    own = project(
        features_own, msg_weight, spline_corner.swapaxes(2, 3), spline_fraction.swapaxes(2, 3)
    )
    own = own.reshape(cells_x, cells_z, slots + 16, width)
    sides, ends, outer, corners = early_halo(own)
    weights, part = inside_pairs(own, sides, features_own, self_weight)
    weights, part = ends_pairs(own, sides, ends, part, weights)
    influence = influence_of(size_x, size_y, size_z)
    along_z, along_x, into_y, back_x, back_z = wave_tables(size_x, size_y, size_z)

    read = charge_weight[None, :]
    weights, preact, mesh, row_place = message_layer(
        own, ends, outer, corners, part, read, weights
    )
    mesh = swapped(mesh, plane).reshape(4, 4, PC, 128)
    slope_near = late_halo(slope_of(preact, read))
    lines = swapped(forward_xz(mesh, along_z, along_x), everyone)
    lines = swapped(filter_y(lines, into_y, influence), everyone)
    field, energy = inverse_xz(lines, back_x, back_z, coupling / (2.0 * volume * natoms))
    field = swapped(field.reshape(16, 64, 128), plane)
    potential, atom_potential, own_weights, slopes = interpolate(
        field, row_place.reshape(24, 8, slots), weights, slope_near, coupling / volume
    )
    across, within = partners(potential)
    side = jnp.full((1, slots), 1 - 2 * (lax.axis_index("gy") % 2), f32)
    weights, total, cotangent = beside(weights, own_weights, slopes, potential)
    grad = backward(
        weights, slopes, total, cotangent, across, within, side, msg_weight, self_weight
    )
    return (
        grad.reshape(features.shape),
        atom_potential.reshape(cells_x, cells_y, cells_z, slots),
        energy[0, 0],
    )


def solution(mesh):
    in_specs = (
        P("gx", "gy", "gz", None, None),
        P(),
        P(),
        P(),
        P("gx", "gy", "gz", None, None),
        P("gx", "gy", "gz", None, None),
    )
    out_specs = (P("gx", "gy", "gz", None, None), P("gx", "gy", "gz", None), P())
    return jax.shard_map(body, mesh=mesh, in_specs=in_specs, out_specs=out_specs, check_vma=False)
```

```python
import functools
import math

import jax
import jax.numpy as jnp
import numpy as np
from jax import lax
from jax.experimental import pallas as pl
from jax.experimental.pallas import tpu as pltpu
from jax.sharding import PartitionSpec as P

PC = 16
pair_scale = 0.1
coupling = 0.125
spread_width = 0.0625
f32 = jnp.float32
bf16 = jnp.bfloat16
plane = ("gx", "gz")
everyone = ("gx", "gy", "gz")


def dot(a, b):
    return jnp.dot(a, b, preferred_element_type=f32)


def dot_t(a, b, precision=None):
    return lax.dot_general(
        a, b, (((1,), (1,)), ((), ())), preferred_element_type=f32, precision=precision
    )


def whole(shape):
    zeros = (0,) * len(shape)
    return pl.BlockSpec(shape, lambda *_: zeros)


VM = pl.BlockSpec(memory_space=pltpu.VMEM)
ANY = pl.BlockSpec(memory_space=pl.ANY)
SMALL = pltpu.CompilerParams(vmem_limit_bytes=20 << 20)
FIRST = pltpu.CompilerParams(vmem_limit_bytes=60 << 20)
LARGE = pltpu.CompilerParams(vmem_limit_bytes=50 << 20)
MIDDLE = pltpu.CompilerParams(vmem_limit_bytes=40 << 20)
FIELD = pltpu.CompilerParams(vmem_limit_bytes=44 << 20)


def cas(rows, columns, size):
    turns = np.outer(rows, columns) % size
    angle = 2.0 * np.pi / size * turns
    return np.cos(angle) + np.sin(angle)


def moved(value, axis, step):
    count = lax.axis_size(axis)
    pairs = [(i, (i + step) % count) for i in range(count)]
    return lax.ppermute(value.reshape(-1, 128), axis, pairs).reshape(value.shape)


def partners(value):
    count = lax.axis_size("gy")
    across = [(i, (i + 1 if i % 2 else i - 1) % count) for i in range(count)]
    within = [(i, i ^ 1) for i in range(count)]
    return [lax.ppermute(value, "gy", pairs) for pairs in (across, within)]


def late_halo(own):
    last_x, last_z = own.shape[0] - 1, own.shape[1] - 1
    left, right = moved(own[:, last_z:], "gz", 1), moved(own[:, :1], "gz", -1)
    row = jnp.concatenate([left, own, right], axis=1)
    rows = jnp.stack([moved(row, "gy", 1), row, moved(row, "gy", -1)])
    return [rows, moved(rows[:, last_x:], "gx", 1), moved(rows[:, :1], "gx", -1)]


def early_halo(own):
    last_x, last_z = own.shape[0] - 1, own.shape[1] - 1
    below, above = moved(own, "gy", 1), moved(own, "gy", -1)
    beside = [moved(own[last_x:], "gx", 1), moved(own[:1], "gx", -1)]
    sides = jnp.stack([below, above])
    rows = [below, own, above]
    left = moved(jnp.stack([row[:, last_z:] for row in rows]), "gz", 1)
    right = moved(jnp.stack([row[:, :1] for row in rows]), "gz", -1)
    aside = [moved(sides[:, last_x:], "gx", 1), moved(sides[:, :1], "gx", -1)]
    corners = [
        moved(jnp.concatenate([left[:, at : at + 1], right[:, at : at + 1]], axis=2), "gx", step)
        for at, step in ((last_x, 1), (0, -1))
    ]
    return [below, above], [left, right], beside + aside, corners


def project_kernel(features_ref, weight_ref, corner_ref, fraction_ref, out_ref):
    value = dot(features_ref[...].reshape(1024, 128), weight_ref[...]).astype(bf16)
    out_ref[:, :128, :] = value.reshape(8, 128, 128)
    none = jnp.zeros((5, 128), f32)
    for x in range(2):
        place = corner_ref[x, 0].astype(f32) + 1.0 + fraction_ref[x, 0]
        high = place.astype(bf16).astype(f32)
        rest = place - high
        middle = rest.astype(bf16).astype(f32)
        low = rest - middle
        for z in range(4):
            rows = [part[d, z : z + 1] for part in (high, low) for d in range(3)]
            rows += [none[:2]] + [middle[d, z : z + 1] for d in range(3)] + [none]
            out_ref[x * 4 + z, 128:, :] = jnp.concatenate(rows, axis=0).astype(bf16)


def project(features, weight, corner, fraction):
    return pl.pallas_call(
        project_kernel,
        grid=(1,),
        in_specs=[whole((8, 128, 128)), whole((128, 128))]
        + [whole((2, 1, 3, 4, 128))] * 2,
        out_specs=whole((8, 144, 128)),
        out_shape=jax.ShapeDtypeStruct((8, 144, 128), bf16),
        compiler_params=FIRST,
        name="project",
    )(features, weight, corner, fraction)


def place_of(rows):
    rows = rows.astype(f32)
    return rows[0:8] + rows[8:16] + pltpu.roll(rows[0:8], 5, 0)


BLOCKS = ((0, 0), (0, 1), (1, 0), (1, 1), (1, 2), (1, 3), (2, 2), (2, 3))
SPANS = ((0, 2, 0, 2), (2, 6, 0, 4), (6, 8, 2, 2))
ORDER_Y = (0, 2, 1)


def position_of(rows):
    return (place_of(rows) * (1.0 / PC)).astype(bf16).astype(f32)


def weigh(centres, a, shift, near, store, pairs):
    for c in range(4):
        columns = jnp.transpose(centres[a, c])
        centre_x = jnp.broadcast_to(columns[:, 0:1], (128, 128))
        centre_y = jnp.broadcast_to(columns[:, 1:2], (128, 128))
        centre_z = jnp.broadcast_to(columns[:, 2:3], (128, 128))
        for block, (pair, owner) in enumerate(BLOCKS):
            if owner != c or pair not in pairs:
                continue
            for at, dy in enumerate(ORDER_Y):
                for half in range(2):
                    dz = 2 * pair + half - c - 1
                    if abs(dz) > 1:
                        tile = jnp.zeros((128, 128), bf16)
                    else:
                        row = near(dy, 2 * pair + half)
                        gap_x = (row[0:1] + shift) - centre_x
                        gap_y = (row[1:2] + (dy - 1.0)) - centre_y
                        gap_z = (row[2:3] + float(dz)) - centre_z
                        squared = gap_x * gap_x + gap_y * gap_y + gap_z * gap_z
                        inside = jnp.maximum(1.0 - squared, 0.0)
                        tile = (pair_scale * inside * inside).astype(bf16)
                    store(block, (at * 2 + half) * 128, tile)


def add_near(weight_ref, t, a, cell, total_ref, pairs):
    for pair in pairs:
        start, stop, first, width = SPANS[pair]
        near = jnp.concatenate(
            [cell(dy, 2 * pair + half)[0:128, :] for dy in ORDER_Y for half in range(2)], axis=0
        )
        part = dot(weight_ref[t, start:stop].reshape(width * 128, 768), near)
        total_ref[a, first : first + width] += part.reshape(width, 128, 128)


def columns_kernel(first, count, weight_ref, weight_out, sems, slot, spans):
    return [
        pltpu.make_async_copy(
            weight_ref.at[pl.ds(first, count), pl.ds(start, size)],
            weight_out.at[pl.ds(first, count), pl.ds(start, size)],
            sems.at[slot + i],
        )
        for i, (start, size) in enumerate(spans)
    ]


INSIDE = (1,)
ENDS = (0, 2)
INSIDE_BLOCKS = ((2, 4),)
END_BLOCKS = ((0, 2), (6, 2))


def centres_of(own_ref, centre_ref):
    def one(cell, carry):
        x, z = cell // 4, cell % 4
        centre_ref[x, z] = position_of(own_ref[x, z, 128:144, :])
        return carry

    lax.fori_loop(0, 8, one, 0)


def inside_kernel(
    own_ref, below_ref, above_ref, features_ref, self_ref,
    weight_out, total_ref, weight_ref, position_ref, sems
):
    refs = (below_ref, own_ref, above_ref)

    def positions(x, carry):
        for dy in range(3):
            for z in range(4):
                position_ref[dy, x, z] = position_of(refs[dy][x, z, 128:144, :])
        return carry

    lax.fori_loop(0, 2, positions, 0)
    total_ref[...] = dot(features_ref[...].reshape(1024, 128), self_ref[...]).reshape(
        2, 4, 128, 128
    )

    def column(t, carry):
        x, a = t // 2, t % 2

        def store(block, lane, tile):
            weight_ref[t, block, :, lane : lane + 128] = tile

        def near(dy, z):
            return position_ref[dy, x, z - 1]

        weigh(position_ref.at[1], a, (x - a).astype(f32), near, store, INSIDE)
        add_near(weight_ref, t, a, lambda dy, z: refs[dy].at[x, z - 1], total_ref, INSIDE)
        return carry

    lax.fori_loop(0, 4, column, 0)
    copies = columns_kernel(0, 4, weight_ref, weight_out, sems, 0, INSIDE_BLOCKS)
    for copy in copies:
        copy.start()
    for copy in copies:
        copy.wait()


def inside_pairs(own, sides, features, self_weight):
    return pl.pallas_call(
        inside_kernel,
        in_specs=[VM] * 5,
        out_specs=[ANY, VM],
        out_shape=[
            jax.ShapeDtypeStruct((6, 8, 128, 768), bf16),
            jax.ShapeDtypeStruct((2, 4, 128, 128), f32),
        ],
        scratch_shapes=[
            pltpu.VMEM((4, 8, 128, 768), bf16),
            pltpu.VMEM((3, 2, 4, 8, 128), f32),
            pltpu.SemaphoreType.DMA((1,)),
        ],
        cost_estimate=pl.CostEstimate(
            flops=5000000000, bytes_accessed=9000000, transcendentals=0
        ),
        compiler_params=LARGE,
        name="inside_pairs",
    )(own, *sides, features, self_weight)


def ends_kernel(
    own_ref, below_ref, above_ref, left_ref, right_ref,
    part_ref, _, weight_out, total_ref, weight_ref, centre_ref, position_ref, sems
):
    refs = (below_ref, own_ref, above_ref)

    def cell(dy, x, z):
        if z == 0:
            return left_ref.at[dy, x, 0]
        if z == 5:
            return right_ref.at[dy, x, 0]
        return refs[dy].at[x, z - 1]

    centres_of(own_ref, centre_ref)

    def positions(x, carry):
        for dy in range(3):
            for z in (0, 1, 4, 5):
                position_ref[dy, x, z] = position_of(cell(dy, x, z)[128:144, :])
        return carry

    lax.fori_loop(0, 2, positions, 0)
    total_ref[...] = part_ref[...]

    def column(t, carry):
        x, a = t // 2, t % 2

        def store(block, lane, tile):
            weight_ref[t, block, :, lane : lane + 128] = tile

        def near(dy, z):
            return position_ref[dy, x, z]

        weigh(centre_ref, a, (x - a).astype(f32), near, store, ENDS)
        add_near(weight_ref, t, a, lambda dy, z: cell(dy, x, z), total_ref, ENDS)
        return carry

    lax.fori_loop(0, 4, column, 0, unroll=2)
    copies = columns_kernel(0, 4, weight_ref, weight_out, sems, 0, END_BLOCKS)
    for copy in copies:
        copy.start()

    for copy in copies:
        copy.wait()


def ends_pairs(own, sides, ends, part, weights):
    return pl.pallas_call(
        ends_kernel,
        in_specs=[VM] * 6 + [ANY],
        out_specs=[ANY, VM],
        input_output_aliases={6: 0},
        out_shape=[
            jax.ShapeDtypeStruct((6, 8, 128, 768), bf16),
            jax.ShapeDtypeStruct((2, 4, 128, 128), f32),
        ],
        scratch_shapes=[
            pltpu.VMEM((4, 8, 128, 768), bf16),
            pltpu.VMEM((2, 4, 8, 128), f32),
            pltpu.VMEM((3, 2, 6, 8, 128), f32),
            pltpu.SemaphoreType.DMA((2,)),
        ],
        cost_estimate=pl.CostEstimate(
            flops=6000000000, bytes_accessed=9000000, transcendentals=0
        ),
        compiler_params=LARGE,
        name="ends_pairs",
    )(own, *sides, *ends, part, weights)


def spline_row(place):
    point = lax.broadcasted_iota(jnp.int32, (PC, 128), 0).astype(f32)
    away = jnp.abs(point - place)
    near = (4.0 - 6.0 * away * away + 3.0 * away * away * away) * (1.0 / 6.0)
    rest = 2.0 - away
    far = rest * rest * rest * (1.0 / 6.0)
    return jnp.where(away < 1.0, near, jnp.where(away < 2.0, far, 0.0))


def message_kernel(
    own_ref, left_ref, right_ref, before_own, after_own, before_side, after_side, before_end,
    after_end, part_ref, read_ref, _,
    weight_out, total_ref, mesh_ref, row_place_ref,
    weight_ref, position_ref, centre_ref, high_ref, low_ref, charge_ref, left_rows, right_rows, sems
):
    refs = ((before_own, before_side, before_end), (after_own, after_side, after_end))

    def cell(side, dy, z):
        own, beside, end = refs[side]
        if z in (0, 5):
            return end.at[dy, 0, z // 5]
        return own.at[0, z - 1] if dy == 1 else beside.at[dy // 2, 0, z - 1]

    centres_of(own_ref, centre_ref)
    for side in range(2):
        for dy in range(3):
            for z in range(6):
                position_ref[side, dy, z] = position_of(cell(side, dy, z)[128:144, :])
        for z in range(6):
            row_place_ref[3 * side, z] = place_of(cell(side, 1, z)[128:144, :])

    def row_places(x, carry):
        row_place_ref[1 + x, 0] = place_of(left_ref[1, x, 0, 128:144, :])
        for z in range(4):
            row_place_ref[1 + x, 1 + z] = place_of(own_ref[x, z, 128:144, :])
        row_place_ref[1 + x, 5] = place_of(right_ref[1, x, 0, 128:144, :])
        return carry

    lax.fori_loop(0, 2, row_places, 0)

    def column(side, carry):
        def store(block, lane, tile):
            weight_ref[side, block, :, lane : lane + 128] = tile

        def near(dy, z):
            return position_ref[side, dy, z]

        weigh(centre_ref, side, (2 * side - 1).astype(f32), near, store, ENDS + INSIDE)
        return carry

    lax.fori_loop(0, 2, column, 0)
    copies = [pltpu.make_async_copy(weight_ref, weight_out.at[pl.ds(4, 2)], sems.at[0])]
    for copy in copies:
        copy.start()
    total_ref[...] = part_ref[...]
    for side in range(2):
        add_near(
            weight_ref, side, side, lambda dy, z: cell(side, dy, z), total_ref, ENDS + INSIDE
        )

    def finish(index, carry):
        preact = total_ref[index // 4, index % 4]
        silu = preact * (0.5 + 0.5 * jnp.tanh(0.5 * preact))
        high = silu.astype(bf16)
        high_ref[index] = high
        low_ref[index] = (silu - high.astype(f32)).astype(bf16)
        return carry

    lax.fori_loop(0, 8, finish, 0, unroll=4)
    wide = jnp.broadcast_to(read_ref[...], (16, 128))
    charge_ref[...] = dot_t(wide, high_ref[...].reshape(1024, 128)) + dot_t(
        wide, low_ref[...].reshape(1024, 128)
    )
    block = lax.broadcasted_iota(jnp.int32, (128, 128), 0) // PC

    def spread(cell, carry):
        lanes = pl.ds(pl.multiple_of(cell * 128, 128), 128)
        place = row_place_ref[1 + cell // 4, 1 + cell % 4]
        row_x = spline_row(place[0:1])
        row_y = spline_row(place[1:2]) * charge_ref[0:1, lanes]
        row_z = spline_row(place[2:3])
        left_rows[:, lanes] = (
            (row_y[:, None, :] * row_x[None, :, :]).reshape(PC * PC, 128).astype(bf16)
        )
        right_rows[:, lanes] = jnp.where(block == cell, jnp.tile(row_z, (8, 1)), 0.0).astype(bf16)
        return carry

    lax.fori_loop(0, 8, spread, 0, unroll=4)
    mesh_ref[...] = dot_t(left_rows[...], right_rows[...]).reshape(PC, PC, 128).astype(bf16)
    for copy in copies:
        copy.wait()


def message_layer(own, ends, outer, corners, part, read, weights):
    return pl.pallas_call(
        message_kernel,
        in_specs=[VM] * 11 + [ANY],
        out_specs=[ANY, VM, VM, VM],
        input_output_aliases={11: 0},
        out_shape=[
            jax.ShapeDtypeStruct((6, 8, 128, 768), bf16),
            jax.ShapeDtypeStruct((2, 4, 128, 128), f32),
            jax.ShapeDtypeStruct((PC, PC, 128), bf16),
            jax.ShapeDtypeStruct((4, 6, 8, 128), f32),
        ],
        scratch_shapes=[
            pltpu.VMEM((2, 8, 128, 768), bf16),
            pltpu.VMEM((2, 3, 6, 8, 128), f32),
            pltpu.VMEM((2, 4, 8, 128), f32),
            pltpu.VMEM((8, 128, 128), bf16),
            pltpu.VMEM((8, 128, 128), bf16),
            pltpu.VMEM((16, 1024), f32),
            pltpu.VMEM((PC * PC, 1024), bf16),
            pltpu.VMEM((128, 1024), bf16),
            pltpu.SemaphoreType.DMA((1,)),
        ],
        cost_estimate=pl.CostEstimate(
            flops=5000000000, bytes_accessed=6000000, transcendentals=8 * 16384
        ),
        compiler_params=LARGE,
        name="message",
    )(own, *ends, *outer, *corners, part, read, weights)


def slope_kernel(total_ref, read_ref, out_ref):
    read = read_ref[...].astype(f32)

    def one(index, carry):
        a, c = index // 4, index % 4
        preact = total_ref[a, c]
        sigma = 0.5 + 0.5 * jnp.tanh(0.5 * preact)
        out_ref[a, c] = (read * (sigma * (1.0 + preact * (1.0 - sigma)))).astype(bf16)
        return carry

    lax.fori_loop(0, 8, one, 0, unroll=2)


def slope_of(total, read):
    return pl.pallas_call(
        slope_kernel,
        in_specs=[VM] * 2,
        out_specs=VM,
        out_shape=jax.ShapeDtypeStruct(total.shape, bf16),
        cost_estimate=pl.CostEstimate(
            flops=8 * 16384 * 8, bytes_accessed=900000, transcendentals=8 * 16384
        ),
        compiler_params=SMALL,
        name="slope",
    )(total, read)


def forward_kernel(mesh_ref, along_z_ref, along_x_ref, out_ref):
    lane = lax.broadcasted_iota(jnp.int32, (64, 128), 1)
    total = jnp.zeros((128, 256), f32)
    for g in range(4):
        mesh = mesh_ref[:, g].reshape(64, 128)
        none = jnp.zeros_like(mesh)
        halves = jnp.concatenate(
            [jnp.where(lane < 64, mesh, none), jnp.where(lane < 64, none, mesh)], axis=0
        )
        table = along_z_ref[g * 64 : (g + 1) * 64, :]
        total = total + dot(halves, jnp.concatenate([table, table], axis=0))
    lines = total.astype(bf16)
    waves = dot(along_x_ref[...], lines)
    out_ref[0:128, :] = waves[:, :128]
    out_ref[128:256, :] = waves[:, 128:]


def forward_xz(mesh, along_z, along_x):
    return pl.pallas_call(
        forward_kernel,
        in_specs=[VM] * 3,
        out_specs=VM,
        compiler_params=SMALL,
        out_shape=jax.ShapeDtypeStruct((256, 128), f32),
        cost_estimate=pl.CostEstimate(
            flops=2 * 64 * 512 * 512, bytes_accessed=800000, transcendentals=0
        ),
        name="forward_xz",
    )(mesh, along_z, along_x)


def filter_kernel(lines_ref, into_ref, influence_ref, out_ref):
    waves = dot(into_ref[...], lines_ref[...].astype(bf16))
    scaled = influence_ref[...] * waves
    power = jnp.sum(jnp.sum(scaled * waves, axis=0, keepdims=True), axis=1, keepdims=True)
    out_ref[pl.ds(0, 256, stride=2), :] = lax.dot_general(
        into_ref[...],
        scaled.astype(bf16),
        (((0,), (0,)), ((), ())),
        preferred_element_type=f32,
    )
    out_ref[pl.ds(1, 256, stride=2), :] = jnp.broadcast_to(power, (256, 128))


def filter_y(lines, into, influence):
    return pl.pallas_call(
        filter_kernel,
        in_specs=[VM] * 3,
        out_specs=VM,
        compiler_params=SMALL,
        out_shape=jax.ShapeDtypeStruct((512, 128), f32),
        cost_estimate=pl.CostEstimate(
            flops=4 * 256 * 256 * 128, bytes_accessed=700000, transcendentals=0
        ),
        name="filter_y",
    )(lines, into, influence)


def inverse_kernel(energy_scale, lines_ref, along_x_ref, along_z_ref, out_ref, energy_ref):
    waves = jnp.concatenate(
        [lines_ref[pl.ds(0, 128, stride=2), :], lines_ref[pl.ds(256, 128, stride=2), :]], axis=1
    ).astype(bf16)
    half = dot(along_x_ref[...], waves).astype(bf16)
    field = dot(half, along_z_ref[...]).astype(bf16)
    for gx in range(4):
        for gz in range(4):
            out_ref[gx, gz] = field[gx * 64 : (gx + 1) * 64, gz * 128 : (gz + 1) * 128]
    power = jnp.sum(lines_ref[pl.ds(1, 256, stride=2), :], axis=0, keepdims=True)
    energy_ref[...] = jnp.broadcast_to(power * energy_scale, (8, 128))


def inverse_xz(lines, along_x, along_z, energy_scale):
    return pl.pallas_call(
        functools.partial(inverse_kernel, energy_scale),
        in_specs=[VM] * 3,
        out_specs=[VM, VM],
        compiler_params=SMALL,
        out_shape=[
            jax.ShapeDtypeStruct((4, 4, 64, 128), bf16),
            jax.ShapeDtypeStruct((8, 128), f32),
        ],
        cost_estimate=pl.CostEstimate(
            flops=2 * 256 * 256 * 640, bytes_accessed=900000, transcendentals=0
        ),
        name="inverse_xz",
    )(lines, along_x, along_z)


def interpolate_kernel(
    field_scale, field_ref, place_ref, stored_ref, rows_ref, before_ref, after_ref,
    out_ref, own_ref, weight_ref, slope_ref, sems
):
    pairs = [
        (rows_ref, slope_ref.at[:, pl.ds(1, 2)]),
        (before_ref, slope_ref.at[:, pl.ds(0, 1)]),
        (after_ref, slope_ref.at[:, pl.ds(3, 1)]),
        (stored_ref.at[:, :, :, pl.ds(512, 256)], weight_ref),
    ]
    copies = [
        pltpu.make_async_copy(source, target, sems.at[i])
        for i, (source, target) in enumerate(pairs)
    ]
    for copy in copies:
        copy.start()
    block = lax.broadcasted_iota(jnp.int32, (128, 128), 0) // PC

    def gather(step, carry):
        ax, half = step // 2, 3 * (step % 2)
        field = field_ref[:, pl.ds(pl.multiple_of(ax * PC, PC), PC), :].reshape(PC * PC, 128)
        for third in range(3):
            cz = half + third
            place = place_ref[ax * 6 + cz]
            row_x = spline_row(place[0:1])
            row_y = spline_row(place[1:2])
            row_z = spline_row(place[2:3])
            right = jnp.where(block == cz + 1, jnp.tile(row_z, (8, 1)), 0.0).astype(bf16)
            partial = dot(field, right)
            left = (row_y[:, None, :] * row_x[None, :, :]).reshape(PC * PC, 128)
            out_ref[pl.ds(ax * 6 + cz, 1), :] = (
                jnp.sum(partial * left, axis=0, keepdims=True) * field_scale
            )
        return carry

    lax.fori_loop(0, 8, gather, 0, unroll=2)
    own_ref[0:4, :] = out_ref[7:11, :]
    own_ref[4:8, :] = out_ref[13:17, :]
    for copy in copies:
        copy.wait()


def interpolate(field, place, weights, slopes, field_scale):
    return pl.pallas_call(
        functools.partial(interpolate_kernel, field_scale),
        in_specs=[VM] * 2 + [ANY] * 4,
        out_specs=[VM] * 4,
        compiler_params=FIELD,
        out_shape=[
            jax.ShapeDtypeStruct((24, 128), f32),
            jax.ShapeDtypeStruct((8, 128), f32),
            jax.ShapeDtypeStruct((6, 8, 128, 256), bf16),
            jax.ShapeDtypeStruct((3, 4, 6, 128, 128), bf16),
        ],
        scratch_shapes=[pltpu.SemaphoreType.DMA((4,))],
        cost_estimate=pl.CostEstimate(
            flops=24 * 2 * 256 * 128 * 128, bytes_accessed=400000, transcendentals=0
        ),
        name="interpolate",
    )(field, place, weights, *slopes)


def combination_of(t):
    return jnp.where(t < 4, 1 + t // 2, 3 * (t - 4)), t % 2


def scaled(columns, cell, slope):
    return (columns[:, cell : cell + 1] * slope.astype(f32)).astype(bf16)


def beside_kernel(
    stored_ref, weight_ref, slope_ref, potential_ref, rest_ref, total_ref, own_out, near_ref, sems
):
    copies = [
        pltpu.make_async_copy(
            stored_ref.at[pl.ds(i, 3), :, :, pl.ds(0, 512)], rest_ref.at[pl.ds(i, 3)], sems.at[i // 3]
        )
        for i in (0, 3)
    ]
    for copy in copies:
        copy.start()
    columns = jnp.transpose(potential_ref[...])
    for x in range(4):
        for z in range(6):
            near_ref[x, z] = scaled(columns, x * 6 + z, slope_ref[1, x, z])
    own_out[...] = near_ref[1:3, 1:5]
    total_ref[...] = jnp.zeros_like(total_ref)

    def combination(t, carry):
        x, a = combination_of(t)
        for pair, (start, stop, first, width) in enumerate(SPANS):
            part = dot(
                weight_ref[t, start:stop].reshape(width * 128, 256),
                near_ref[x, 2 * pair : 2 * pair + 2].reshape(256, 128),
            )
            total_ref[a, first : first + width] += part.reshape(width, 128, 128)
        return carry

    lax.fori_loop(0, 6, combination, 0, unroll=3)
    for copy in copies:
        copy.wait()


def beside(stored, weights, slopes, potential):
    return pl.pallas_call(
        beside_kernel,
        in_specs=[ANY] + [VM] * 3,
        out_specs=[VM] * 3,
        out_shape=[
            jax.ShapeDtypeStruct((6, 8, 128, 512), bf16),
            jax.ShapeDtypeStruct((2, 4, 128, 128), f32),
            jax.ShapeDtypeStruct((2, 4, 128, 128), bf16),
        ],
        scratch_shapes=[
            pltpu.VMEM((4, 6, 128, 128), bf16),
            pltpu.SemaphoreType.DMA((2,)),
        ],
        cost_estimate=pl.CostEstimate(
            flops=3000000000, bytes_accessed=12000000, transcendentals=0
        ),
        compiler_params=MIDDLE,
        name="beside",
    )(stored, weights, slopes, potential)


def backward_kernel(
    weight_ref, slope_ref, part_ref, own_ref, across_ref, within_ref, side_ref, msg_ref, self_ref,
    out_ref, near_ref, total_ref, potential_ref
):
    even = jnp.broadcast_to(side_ref[...], (24, 128)) > 0.0
    potential_ref[0] = jnp.where(even, across_ref[...], within_ref[...])
    potential_ref[1] = jnp.where(even, within_ref[...], across_ref[...])

    def scale(side, carry):
        columns = jnp.transpose(potential_ref[side])
        for x in range(4):
            for z in range(6):
                near_ref[side, x, z] = scaled(columns, x * 6 + z, slope_ref[2 * side, x, z])
        return carry

    lax.fori_loop(0, 2, scale, 0)
    total_ref[...] = part_ref[...]

    def combination(t, carry):
        x, a = combination_of(t)
        for pair, (start, stop, first, width) in enumerate(SPANS):
            near = jnp.concatenate(
                [
                    near_ref[side, x, 2 * pair : 2 * pair + 2].reshape(256, 128)
                    for side in range(2)
                ],
                axis=0,
            )
            part = dot(weight_ref[t, start:stop].reshape(width * 128, 512), near)
            total_ref[a, first : first + width] += part.reshape(width, 128, 128)
        return carry

    lax.fori_loop(0, 6, combination, 0, unroll=3)

    def finish(a, carry):
        back = total_ref[a].reshape(512, 128).astype(bf16)
        own = own_ref[a].reshape(512, 128)
        out_ref[a] = (dot_t(back, msg_ref[...]) + dot_t(own, self_ref[...])).reshape(4, 128, 128)
        return carry

    lax.fori_loop(0, 2, finish, 0, unroll=2)


def backward(weights, slope, part, own, across, within, side, msg_weight, self_weight):
    return pl.pallas_call(
        backward_kernel,
        in_specs=[VM] * 9,
        out_specs=VM,
        out_shape=jax.ShapeDtypeStruct((2, 4, 128, 128), f32),
        scratch_shapes=[
            pltpu.VMEM((2, 4, 6, 128, 128), bf16),
            pltpu.VMEM((2, 4, 128, 128), f32),
            pltpu.VMEM((2, 24, 128), f32),
        ],
        cost_estimate=pl.CostEstimate(
            flops=4000000000, bytes_accessed=12000000, transcendentals=0
        ),
        compiler_params=SMALL,
        name="backward",
    )(weights, slope, part, own, across, within, side, msg_weight, self_weight)


def wave_tables(size_x, size_y, size_z):
    i16 = np.arange(16)
    points_x = np.array([g * 32 + a * 16 + i for a in range(2) for g in range(4) for i in i16])
    along_x = cas(np.arange(size_x), points_x, size_x)
    points_y = np.array(
        [gy * 16 + gx * 4 + gz for gx in range(4) for gy in range(16) for gz in range(4)]
    )
    into_y = cas(np.arange(size_y), points_y, size_y)
    back_x = np.array(
        [((2 * g - 1 + a) % 8) * 16 + i for g in range(4) for a in range(4) for i in i16]
    )
    back_z = np.array(
        [((4 * g - 2 + c) % 16) * 16 + k for g in range(4) for c in range(8) for k in i16]
    )
    tables = (
        cas(np.arange(size_z), np.arange(size_z), size_z),
        along_x,
        into_y,
        cas(back_x, np.arange(size_x), size_x),
        cas(np.arange(size_z), back_z, size_z),
    )
    return [jnp.asarray(np.ascontiguousarray(t), dtype=bf16) for t in tables]


def influence_of(size_x, size_y, size_z):
    device = lax.axis_index(everyone)

    def wave(index, size):
        signed = jnp.where(2 * index >= size, index - size, index)
        return signed.astype(f32) * (PC / size)

    wave_x = wave(device % size_x, size_x)
    wave_y = wave(jnp.arange(size_y, dtype=jnp.int32), size_y)[:, None]
    wave_z = wave(
        device // size_x * 128 + jnp.arange(size_z // 2, dtype=jnp.int32), size_z
    )[None, :]
    squared = wave_x * wave_x + wave_y * wave_y + wave_z * wave_z
    safe = jnp.where(squared > 0, squared, 1.0)
    return jnp.where(squared > 0, jnp.exp(-((math.pi * spread_width) ** 2) * squared) / safe, 0.0)


def swapped(value, axis):
    return lax.all_to_all(value, axis, split_axis=0, concat_axis=0, tiled=True)


def body(features, msg_weight, self_weight, charge_weight, spline_corner, spline_fraction):
    cells_x, cells_y, cells_z, slots, width = features.shape
    size_x = cells_x * PC * lax.axis_size("gx")
    size_y = cells_y * PC * lax.axis_size("gy")
    size_z = cells_z * PC * lax.axis_size("gz")
    volume = size_x // PC * (size_y // PC) * (size_z // PC)
    natoms = volume * slots
    cells = cells_x * cells_z

    features_own = features.reshape(cells, slots, width)
    own = project(
        features_own, msg_weight, spline_corner.swapaxes(2, 3), spline_fraction.swapaxes(2, 3)
    )
    own = own.reshape(cells_x, cells_z, slots + 16, width)
    sides, ends, outer, corners = early_halo(own)
    weights, part = inside_pairs(own, sides, features_own, self_weight)
    weights, part = ends_pairs(own, sides, ends, part, weights)
    influence = influence_of(size_x, size_y, size_z)
    along_z, along_x, into_y, back_x, back_z = wave_tables(size_x, size_y, size_z)

    read = charge_weight[None, :]
    weights, preact, mesh, row_place = message_layer(
        own, ends, outer, corners, part, read, weights
    )
    mesh = swapped(mesh, plane).reshape(4, 4, PC, 128)
    slope_near = late_halo(slope_of(preact, read))
    lines = swapped(forward_xz(mesh, along_z, along_x), everyone)
    lines = swapped(filter_y(lines, into_y, influence), everyone)
    field, energy = inverse_xz(lines, back_x, back_z, coupling / (2.0 * volume * natoms))
    field = swapped(field.reshape(16, 64, 128), plane)
    potential, atom_potential, own_weights, slopes = interpolate(
        field, row_place.reshape(24, 8, slots), weights, slope_near, coupling / volume
    )
    across, within = partners(potential)
    side = jnp.full((1, slots), 1 - 2 * (lax.axis_index("gy") % 2), f32)
    weights, total, cotangent = beside(weights, own_weights, slopes, potential)
    grad = backward(
        weights, slopes, total, cotangent, across, within, side, msg_weight, self_weight
    )
    return (
        grad.reshape(features.shape),
        atom_potential.reshape(cells_x, cells_y, cells_z, slots),
        energy[0, 0],
    )


def solution(mesh):
    in_specs = (
        P("gx", "gy", "gz", None, None),
        P(),
        P(),
        P(),
        P("gx", "gy", "gz", None, None),
        P("gx", "gy", "gz", None, None),
    )
    out_specs = (P("gx", "gy", "gz", None, None), P("gx", "gy", "gz", None), P())
    return jax.shard_map(body, mesh=mesh, in_specs=in_specs, out_specs=out_specs, check_vma=False)
```

```python
import functools
import math

import jax
import jax.numpy as jnp
import numpy as np
from jax import lax
from jax.experimental import pallas as pl
from jax.experimental.pallas import tpu as pltpu
from jax.sharding import PartitionSpec as P

PC = 16
pair_scale = 0.1
coupling = 0.125
spread_width = 0.0625
f32 = jnp.float32
bf16 = jnp.bfloat16
plane = ("gx", "gz")
everyone = ("gx", "gy", "gz")


def dot(a, b):
    return jnp.dot(a, b, preferred_element_type=f32)


def dot_t(a, b, precision=None):
    return lax.dot_general(
        a, b, (((1,), (1,)), ((), ())), preferred_element_type=f32, precision=precision
    )


def whole(shape):
    zeros = (0,) * len(shape)
    return pl.BlockSpec(shape, lambda *_: zeros)


VM = pl.BlockSpec(memory_space=pltpu.VMEM)
ANY = pl.BlockSpec(memory_space=pl.ANY)
SMALL = pltpu.CompilerParams(vmem_limit_bytes=20 << 20)
FIRST = pltpu.CompilerParams(vmem_limit_bytes=60 << 20)
LARGE = pltpu.CompilerParams(vmem_limit_bytes=50 << 20)
MIDDLE = pltpu.CompilerParams(vmem_limit_bytes=37 << 20)
FIELD = pltpu.CompilerParams(vmem_limit_bytes=44 << 20)


def cas(rows, columns, size):
    turns = np.outer(rows, columns) % size
    angle = 2.0 * np.pi / size * turns
    return np.cos(angle) + np.sin(angle)


def moved(value, axis, step):
    count = lax.axis_size(axis)
    pairs = [(i, (i + step) % count) for i in range(count)]
    return lax.ppermute(value.reshape(-1, 128), axis, pairs).reshape(value.shape)


def partners(value):
    count = lax.axis_size("gy")
    across = [(i, (i + 1 if i % 2 else i - 1) % count) for i in range(count)]
    within = [(i, i ^ 1) for i in range(count)]
    return [lax.ppermute(value, "gy", pairs) for pairs in (across, within)]


def late_halo(own):
    last_x, last_z = own.shape[0] - 1, own.shape[1] - 1
    left, right = moved(own[:, last_z:], "gz", 1), moved(own[:, :1], "gz", -1)
    row = jnp.concatenate([left, own, right], axis=1)
    rows = jnp.stack([moved(row, "gy", 1), row, moved(row, "gy", -1)])
    return [rows, moved(rows[:, last_x:], "gx", 1), moved(rows[:, :1], "gx", -1)]


def early_halo(own):
    last_x, last_z = own.shape[0] - 1, own.shape[1] - 1
    below, above = moved(own, "gy", 1), moved(own, "gy", -1)
    beside = [moved(own[last_x:], "gx", 1), moved(own[:1], "gx", -1)]
    sides = jnp.stack([below, above])
    rows = [below, own, above]
    left = moved(jnp.stack([row[:, last_z:] for row in rows]), "gz", 1)
    right = moved(jnp.stack([row[:, :1] for row in rows]), "gz", -1)
    aside = [moved(sides[:, last_x:], "gx", 1), moved(sides[:, :1], "gx", -1)]
    corners = [
        moved(jnp.concatenate([left[:, at : at + 1], right[:, at : at + 1]], axis=2), "gx", step)
        for at, step in ((last_x, 1), (0, -1))
    ]
    return [below, above], [left, right], beside + aside, corners


def project_kernel(features_ref, weight_ref, corner_ref, fraction_ref, out_ref):
    value = dot(features_ref[...].reshape(1024, 128), weight_ref[...]).astype(bf16)
    out_ref[:, :128, :] = value.reshape(8, 128, 128)
    none = jnp.zeros((5, 128), f32)
    for x in range(2):
        place = corner_ref[x, 0].astype(f32) + 1.0 + fraction_ref[x, 0]
        high = place.astype(bf16).astype(f32)
        rest = place - high
        middle = rest.astype(bf16).astype(f32)
        low = rest - middle
        for z in range(4):
            rows = [part[d, z : z + 1] for part in (high, low) for d in range(3)]
            rows += [none[:2]] + [middle[d, z : z + 1] for d in range(3)] + [none]
            out_ref[x * 4 + z, 128:, :] = jnp.concatenate(rows, axis=0).astype(bf16)


def project(features, weight, corner, fraction):
    return pl.pallas_call(
        project_kernel,
        grid=(1,),
        in_specs=[whole((8, 128, 128)), whole((128, 128))]
        + [whole((2, 1, 3, 4, 128))] * 2,
        out_specs=whole((8, 144, 128)),
        out_shape=jax.ShapeDtypeStruct((8, 144, 128), bf16),
        compiler_params=FIRST,
        name="project",
    )(features, weight, corner, fraction)


def place_of(rows):
    rows = rows.astype(f32)
    return rows[0:8] + rows[8:16] + pltpu.roll(rows[0:8], 5, 0)


BLOCKS = ((0, 0), (0, 1), (1, 0), (1, 1), (1, 2), (1, 3), (2, 2), (2, 3))
SPANS = ((0, 2, 0, 2), (2, 6, 0, 4), (6, 8, 2, 2))
ORDER_Y = (0, 2, 1)


def position_of(rows):
    return (place_of(rows) * (1.0 / PC)).astype(bf16).astype(f32)


def weigh(centres, a, shift, near, store, pairs):
    for c in range(4):
        columns = jnp.transpose(centres[a, c])
        centre_x = jnp.broadcast_to(columns[:, 0:1], (128, 128))
        centre_y = jnp.broadcast_to(columns[:, 1:2], (128, 128))
        centre_z = jnp.broadcast_to(columns[:, 2:3], (128, 128))
        for block, (pair, owner) in enumerate(BLOCKS):
            if owner != c or pair not in pairs:
                continue
            for at, dy in enumerate(ORDER_Y):
                for half in range(2):
                    dz = 2 * pair + half - c - 1
                    if abs(dz) > 1:
                        tile = jnp.zeros((128, 128), bf16)
                    else:
                        row = near(dy, 2 * pair + half)
                        gap_x = (row[0:1] + shift) - centre_x
                        gap_y = (row[1:2] + (dy - 1.0)) - centre_y
                        gap_z = (row[2:3] + float(dz)) - centre_z
                        squared = gap_x * gap_x + gap_y * gap_y + gap_z * gap_z
                        inside = jnp.maximum(1.0 - squared, 0.0)
                        tile = (pair_scale * inside * inside).astype(bf16)
                    store(block, (at * 2 + half) * 128, tile)


def add_near(weight_ref, t, a, cell, total_ref, pairs):
    for pair in pairs:
        start, stop, first, width = SPANS[pair]
        near = jnp.concatenate(
            [cell(dy, 2 * pair + half)[0:128, :] for dy in ORDER_Y for half in range(2)], axis=0
        )
        part = dot(weight_ref[t, start:stop].reshape(width * 128, 768), near)
        total_ref[a, first : first + width] += part.reshape(width, 128, 128)


def columns_kernel(first, count, weight_ref, weight_out, sems, slot, spans):
    return [
        pltpu.make_async_copy(
            weight_ref.at[pl.ds(first, count), pl.ds(start, size)],
            weight_out.at[pl.ds(first, count), pl.ds(start, size)],
            sems.at[slot + i],
        )
        for i, (start, size) in enumerate(spans)
    ]


INSIDE = (1,)
ENDS = (0, 2)
INSIDE_BLOCKS = ((2, 4),)
END_BLOCKS = ((0, 2), (6, 2))


def centres_of(own_ref, centre_ref):
    def one(cell, carry):
        x, z = cell // 4, cell % 4
        centre_ref[x, z] = position_of(own_ref[x, z, 128:144, :])
        return carry

    lax.fori_loop(0, 8, one, 0)


def inside_kernel(
    own_ref, below_ref, above_ref, features_ref, self_ref,
    weight_out, total_ref, weight_ref, position_ref, sems
):
    refs = (below_ref, own_ref, above_ref)

    def positions(x, carry):
        for dy in range(3):
            for z in range(4):
                position_ref[dy, x, z] = position_of(refs[dy][x, z, 128:144, :])
        return carry

    lax.fori_loop(0, 2, positions, 0)
    total_ref[...] = dot(features_ref[...].reshape(1024, 128), self_ref[...]).reshape(
        2, 4, 128, 128
    )

    def column(t, carry):
        x, a = t // 2, t % 2

        def store(block, lane, tile):
            weight_ref[t, block, :, lane : lane + 128] = tile

        def near(dy, z):
            return position_ref[dy, x, z - 1]

        weigh(position_ref.at[1], a, (x - a).astype(f32), near, store, INSIDE)
        add_near(weight_ref, t, a, lambda dy, z: refs[dy].at[x, z - 1], total_ref, INSIDE)
        return carry

    lax.fori_loop(0, 4, column, 0)
    copies = columns_kernel(0, 4, weight_ref, weight_out, sems, 0, INSIDE_BLOCKS)
    for copy in copies:
        copy.start()
    for copy in copies:
        copy.wait()


def inside_pairs(own, sides, features, self_weight):
    return pl.pallas_call(
        inside_kernel,
        in_specs=[VM] * 5,
        out_specs=[ANY, VM],
        out_shape=[
            jax.ShapeDtypeStruct((6, 8, 128, 768), bf16),
            jax.ShapeDtypeStruct((2, 4, 128, 128), f32),
        ],
        scratch_shapes=[
            pltpu.VMEM((4, 8, 128, 768), bf16),
            pltpu.VMEM((3, 2, 4, 8, 128), f32),
            pltpu.SemaphoreType.DMA((1,)),
        ],
        cost_estimate=pl.CostEstimate(
            flops=5000000000, bytes_accessed=9000000, transcendentals=0
        ),
        compiler_params=LARGE,
        name="inside_pairs",
    )(own, *sides, features, self_weight)


def ends_kernel(
    own_ref, below_ref, above_ref, left_ref, right_ref,
    part_ref, _, weight_out, total_ref, weight_ref, centre_ref, position_ref, sems
):
    refs = (below_ref, own_ref, above_ref)

    def cell(dy, x, z):
        if z == 0:
            return left_ref.at[dy, x, 0]
        if z == 5:
            return right_ref.at[dy, x, 0]
        return refs[dy].at[x, z - 1]

    centres_of(own_ref, centre_ref)

    def positions(x, carry):
        for dy in range(3):
            for z in (0, 1, 4, 5):
                position_ref[dy, x, z] = position_of(cell(dy, x, z)[128:144, :])
        return carry

    lax.fori_loop(0, 2, positions, 0)
    total_ref[...] = part_ref[...]

    def column(t, carry):
        x, a = t // 2, t % 2

        def store(block, lane, tile):
            weight_ref[t, block, :, lane : lane + 128] = tile

        def near(dy, z):
            return position_ref[dy, x, z]

        weigh(centre_ref, a, (x - a).astype(f32), near, store, ENDS)
        add_near(weight_ref, t, a, lambda dy, z: cell(dy, x, z), total_ref, ENDS)
        return carry

    lax.fori_loop(0, 4, column, 0, unroll=2)
    copies = columns_kernel(0, 4, weight_ref, weight_out, sems, 0, END_BLOCKS)
    for copy in copies:
        copy.start()

    for copy in copies:
        copy.wait()


def ends_pairs(own, sides, ends, part, weights):
    return pl.pallas_call(
        ends_kernel,
        in_specs=[VM] * 6 + [ANY],
        out_specs=[ANY, VM],
        input_output_aliases={6: 0},
        out_shape=[
            jax.ShapeDtypeStruct((6, 8, 128, 768), bf16),
            jax.ShapeDtypeStruct((2, 4, 128, 128), f32),
        ],
        scratch_shapes=[
            pltpu.VMEM((4, 8, 128, 768), bf16),
            pltpu.VMEM((2, 4, 8, 128), f32),
            pltpu.VMEM((3, 2, 6, 8, 128), f32),
            pltpu.SemaphoreType.DMA((2,)),
        ],
        cost_estimate=pl.CostEstimate(
            flops=6000000000, bytes_accessed=9000000, transcendentals=0
        ),
        compiler_params=LARGE,
        name="ends_pairs",
    )(own, *sides, *ends, part, weights)


def spline_row(place):
    point = lax.broadcasted_iota(jnp.int32, (PC, 128), 0).astype(f32)
    away = jnp.abs(point - place)
    near = (4.0 - 6.0 * away * away + 3.0 * away * away * away) * (1.0 / 6.0)
    rest = 2.0 - away
    far = rest * rest * rest * (1.0 / 6.0)
    return jnp.where(away < 1.0, near, jnp.where(away < 2.0, far, 0.0))


def message_kernel(
    own_ref, left_ref, right_ref, before_own, after_own, before_side, after_side, before_end,
    after_end, part_ref, read_ref, _,
    weight_out, total_ref, mesh_ref, row_place_ref,
    weight_ref, position_ref, centre_ref, high_ref, low_ref, charge_ref, left_rows, right_rows, sems
):
    refs = ((before_own, before_side, before_end), (after_own, after_side, after_end))

    def cell(side, dy, z):
        own, beside, end = refs[side]
        if z in (0, 5):
            return end.at[dy, 0, z // 5]
        return own.at[0, z - 1] if dy == 1 else beside.at[dy // 2, 0, z - 1]

    centres_of(own_ref, centre_ref)
    for side in range(2):
        for dy in range(3):
            for z in range(6):
                position_ref[side, dy, z] = position_of(cell(side, dy, z)[128:144, :])
        for z in range(6):
            row_place_ref[3 * side, z] = place_of(cell(side, 1, z)[128:144, :])

    def row_places(x, carry):
        row_place_ref[1 + x, 0] = place_of(left_ref[1, x, 0, 128:144, :])
        for z in range(4):
            row_place_ref[1 + x, 1 + z] = place_of(own_ref[x, z, 128:144, :])
        row_place_ref[1 + x, 5] = place_of(right_ref[1, x, 0, 128:144, :])
        return carry

    lax.fori_loop(0, 2, row_places, 0)

    def column(side, carry):
        def store(block, lane, tile):
            weight_ref[side, block, :, lane : lane + 128] = tile

        def near(dy, z):
            return position_ref[side, dy, z]

        weigh(centre_ref, side, (2 * side - 1).astype(f32), near, store, ENDS + INSIDE)
        return carry

    lax.fori_loop(0, 2, column, 0)
    copies = [pltpu.make_async_copy(weight_ref, weight_out.at[pl.ds(4, 2)], sems.at[0])]
    for copy in copies:
        copy.start()
    total_ref[...] = part_ref[...]
    for side in range(2):
        add_near(
            weight_ref, side, side, lambda dy, z: cell(side, dy, z), total_ref, ENDS + INSIDE
        )

    def finish(index, carry):
        preact = total_ref[index // 4, index % 4]
        silu = preact * (0.5 + 0.5 * jnp.tanh(0.5 * preact))
        high = silu.astype(bf16)
        high_ref[index] = high
        low_ref[index] = (silu - high.astype(f32)).astype(bf16)
        return carry

    lax.fori_loop(0, 8, finish, 0, unroll=4)
    wide = jnp.broadcast_to(read_ref[...], (16, 128))
    charge_ref[...] = dot_t(wide, high_ref[...].reshape(1024, 128)) + dot_t(
        wide, low_ref[...].reshape(1024, 128)
    )
    block = lax.broadcasted_iota(jnp.int32, (128, 128), 0) // PC

    def spread(cell, carry):
        lanes = pl.ds(pl.multiple_of(cell * 128, 128), 128)
        place = row_place_ref[1 + cell // 4, 1 + cell % 4]
        row_x = spline_row(place[0:1])
        row_y = spline_row(place[1:2]) * charge_ref[0:1, lanes]
        row_z = spline_row(place[2:3])
        left_rows[:, lanes] = (
            (row_y[:, None, :] * row_x[None, :, :]).reshape(PC * PC, 128).astype(bf16)
        )
        right_rows[:, lanes] = jnp.where(block == cell, jnp.tile(row_z, (8, 1)), 0.0).astype(bf16)
        return carry

    lax.fori_loop(0, 8, spread, 0, unroll=4)
    mesh_ref[...] = dot_t(left_rows[...], right_rows[...]).reshape(PC, PC, 128).astype(bf16)
    for copy in copies:
        copy.wait()


def message_layer(own, ends, outer, corners, part, read, weights):
    return pl.pallas_call(
        message_kernel,
        in_specs=[VM] * 11 + [ANY],
        out_specs=[ANY, VM, VM, VM],
        input_output_aliases={11: 0},
        out_shape=[
            jax.ShapeDtypeStruct((6, 8, 128, 768), bf16),
            jax.ShapeDtypeStruct((2, 4, 128, 128), f32),
            jax.ShapeDtypeStruct((PC, PC, 128), bf16),
            jax.ShapeDtypeStruct((4, 6, 8, 128), f32),
        ],
        scratch_shapes=[
            pltpu.VMEM((2, 8, 128, 768), bf16),
            pltpu.VMEM((2, 3, 6, 8, 128), f32),
            pltpu.VMEM((2, 4, 8, 128), f32),
            pltpu.VMEM((8, 128, 128), bf16),
            pltpu.VMEM((8, 128, 128), bf16),
            pltpu.VMEM((16, 1024), f32),
            pltpu.VMEM((PC * PC, 1024), bf16),
            pltpu.VMEM((128, 1024), bf16),
            pltpu.SemaphoreType.DMA((1,)),
        ],
        cost_estimate=pl.CostEstimate(
            flops=5000000000, bytes_accessed=6000000, transcendentals=8 * 16384
        ),
        compiler_params=LARGE,
        name="message",
    )(own, *ends, *outer, *corners, part, read, weights)


def slope_kernel(total_ref, read_ref, out_ref):
    read = read_ref[...].astype(f32)

    def one(index, carry):
        a, c = index // 4, index % 4
        preact = total_ref[a, c]
        sigma = 0.5 + 0.5 * jnp.tanh(0.5 * preact)
        out_ref[a, c] = (read * (sigma * (1.0 + preact * (1.0 - sigma)))).astype(bf16)
        return carry

    lax.fori_loop(0, 8, one, 0, unroll=2)


def slope_of(total, read):
    return pl.pallas_call(
        slope_kernel,
        in_specs=[VM] * 2,
        out_specs=VM,
        out_shape=jax.ShapeDtypeStruct(total.shape, bf16),
        cost_estimate=pl.CostEstimate(
            flops=8 * 16384 * 8, bytes_accessed=900000, transcendentals=8 * 16384
        ),
        compiler_params=SMALL,
        name="slope",
    )(total, read)


def forward_kernel(mesh_ref, along_z_ref, along_x_ref, out_ref):
    lane = lax.broadcasted_iota(jnp.int32, (64, 128), 1)
    total = jnp.zeros((128, 256), f32)
    for g in range(4):
        mesh = mesh_ref[:, g].reshape(64, 128)
        none = jnp.zeros_like(mesh)
        halves = jnp.concatenate(
            [jnp.where(lane < 64, mesh, none), jnp.where(lane < 64, none, mesh)], axis=0
        )
        table = along_z_ref[g * 64 : (g + 1) * 64, :]
        total = total + dot(halves, jnp.concatenate([table, table], axis=0))
    lines = total.astype(bf16)
    waves = dot(along_x_ref[...], lines)
    out_ref[0:128, :] = waves[:, :128]
    out_ref[128:256, :] = waves[:, 128:]


def forward_xz(mesh, along_z, along_x):
    return pl.pallas_call(
        forward_kernel,
        in_specs=[VM] * 3,
        out_specs=VM,
        compiler_params=SMALL,
        out_shape=jax.ShapeDtypeStruct((256, 128), f32),
        cost_estimate=pl.CostEstimate(
            flops=2 * 64 * 512 * 512, bytes_accessed=800000, transcendentals=0
        ),
        name="forward_xz",
    )(mesh, along_z, along_x)


def filter_kernel(lines_ref, into_ref, influence_ref, out_ref):
    waves = dot(into_ref[...], lines_ref[...].astype(bf16))
    scaled = influence_ref[...] * waves
    power = jnp.sum(jnp.sum(scaled * waves, axis=0, keepdims=True), axis=1, keepdims=True)
    out_ref[pl.ds(0, 256, stride=2), :] = lax.dot_general(
        into_ref[...],
        scaled.astype(bf16),
        (((0,), (0,)), ((), ())),
        preferred_element_type=f32,
    )
    out_ref[pl.ds(1, 256, stride=2), :] = jnp.broadcast_to(power, (256, 128))


def filter_y(lines, into, influence):
    return pl.pallas_call(
        filter_kernel,
        in_specs=[VM] * 3,
        out_specs=VM,
        compiler_params=SMALL,
        out_shape=jax.ShapeDtypeStruct((512, 128), f32),
        cost_estimate=pl.CostEstimate(
            flops=4 * 256 * 256 * 128, bytes_accessed=700000, transcendentals=0
        ),
        name="filter_y",
    )(lines, into, influence)


def inverse_kernel(energy_scale, lines_ref, along_x_ref, along_z_ref, out_ref, energy_ref):
    waves = jnp.concatenate(
        [lines_ref[pl.ds(0, 128, stride=2), :], lines_ref[pl.ds(256, 128, stride=2), :]], axis=1
    ).astype(bf16)
    half = dot(along_x_ref[...], waves).astype(bf16)
    field = dot(half, along_z_ref[...]).astype(bf16)
    for gx in range(4):
        for gz in range(4):
            out_ref[gx, gz] = field[gx * 64 : (gx + 1) * 64, gz * 128 : (gz + 1) * 128]
    power = jnp.sum(lines_ref[pl.ds(1, 256, stride=2), :], axis=0, keepdims=True)
    energy_ref[...] = jnp.broadcast_to(power * energy_scale, (8, 128))


def inverse_xz(lines, along_x, along_z, energy_scale):
    return pl.pallas_call(
        functools.partial(inverse_kernel, energy_scale),
        in_specs=[VM] * 3,
        out_specs=[VM, VM],
        compiler_params=SMALL,
        out_shape=[
            jax.ShapeDtypeStruct((4, 4, 64, 128), bf16),
            jax.ShapeDtypeStruct((8, 128), f32),
        ],
        cost_estimate=pl.CostEstimate(
            flops=2 * 256 * 256 * 640, bytes_accessed=900000, transcendentals=0
        ),
        name="inverse_xz",
    )(lines, along_x, along_z)


def interpolate_kernel(
    field_scale, field_ref, place_ref, stored_ref, rows_ref, before_ref, after_ref,
    out_ref, own_ref, weight_ref, slope_ref, sems
):
    pairs = [
        (rows_ref.at[1], slope_ref.at[pl.ds(1, 2)]),
        (before_ref.at[1], slope_ref.at[pl.ds(0, 1)]),
        (after_ref.at[1], slope_ref.at[pl.ds(3, 1)]),
        (stored_ref.at[:, :, :, pl.ds(512, 256)], weight_ref),
    ]
    copies = [
        pltpu.make_async_copy(source, target, sems.at[i])
        for i, (source, target) in enumerate(pairs)
    ]
    for copy in copies:
        copy.start()
    block = lax.broadcasted_iota(jnp.int32, (128, 128), 0) // PC

    def gather(step, carry):
        ax, half = step // 2, 3 * (step % 2)
        field = field_ref[:, pl.ds(pl.multiple_of(ax * PC, PC), PC), :].reshape(PC * PC, 128)
        for third in range(3):
            cz = half + third
            place = place_ref[ax * 6 + cz]
            row_x = spline_row(place[0:1])
            row_y = spline_row(place[1:2])
            row_z = spline_row(place[2:3])
            right = jnp.where(block == cz + 1, jnp.tile(row_z, (8, 1)), 0.0).astype(bf16)
            partial = dot(field, right)
            left = (row_y[:, None, :] * row_x[None, :, :]).reshape(PC * PC, 128)
            out_ref[pl.ds(ax * 6 + cz, 1), :] = (
                jnp.sum(partial * left, axis=0, keepdims=True) * field_scale
            )
        return carry

    lax.fori_loop(0, 8, gather, 0, unroll=2)
    own_ref[0:4, :] = out_ref[7:11, :]
    own_ref[4:8, :] = out_ref[13:17, :]
    for copy in copies:
        copy.wait()


def interpolate(field, place, weights, slopes, field_scale):
    return pl.pallas_call(
        functools.partial(interpolate_kernel, field_scale),
        in_specs=[VM] * 2 + [ANY] * 4,
        out_specs=[VM] * 4,
        compiler_params=FIELD,
        out_shape=[
            jax.ShapeDtypeStruct((24, 128), f32),
            jax.ShapeDtypeStruct((8, 128), f32),
            jax.ShapeDtypeStruct((6, 8, 128, 256), bf16),
            jax.ShapeDtypeStruct((4, 6, 128, 128), bf16),
        ],
        scratch_shapes=[pltpu.SemaphoreType.DMA((4,))],
        cost_estimate=pl.CostEstimate(
            flops=24 * 2 * 256 * 128 * 128, bytes_accessed=400000, transcendentals=0
        ),
        name="interpolate",
    )(field, place, weights, *slopes)


def combination_of(t):
    return jnp.where(t < 4, 1 + t // 2, 3 * (t - 4)), t % 2


def scaled(columns, cell, slope):
    return (columns[:, cell : cell + 1] * slope.astype(f32)).astype(bf16)


def beside_kernel(
    stored_ref, rows_ref, before_ref, after_ref, weight_ref, slope_ref, potential_ref,
    rest_ref, sides_ref, total_ref, own_out, near_ref, sems
):
    copies = [
        pltpu.make_async_copy(
            stored_ref.at[pl.ds(i, 3), :, :, pl.ds(0, 512)], rest_ref.at[pl.ds(i, 3)], sems.at[i // 3]
        )
        for i in (0, 3)
    ]
    pieces = ((rows_ref, 1, 2), (before_ref, 0, 1), (after_ref, 3, 1))
    copies += [
        pltpu.make_async_copy(
            ref.at[2 * side], sides_ref.at[side, pl.ds(first, size)], sems.at[2 + 3 * side + i]
        )
        for side in range(2)
        for i, (ref, first, size) in enumerate(pieces)
    ]
    for copy in copies:
        copy.start()
    columns = jnp.transpose(potential_ref[...])
    for x in range(4):
        for z in range(6):
            near_ref[x, z] = scaled(columns, x * 6 + z, slope_ref[x, z])
    own_out[...] = near_ref[1:3, 1:5]
    total_ref[...] = jnp.zeros_like(total_ref)

    def combination(t, carry):
        x, a = combination_of(t)
        for pair, (start, stop, first, width) in enumerate(SPANS):
            part = dot(
                weight_ref[t, start:stop].reshape(width * 128, 256),
                near_ref[x, 2 * pair : 2 * pair + 2].reshape(256, 128),
            )
            total_ref[a, first : first + width] += part.reshape(width, 128, 128)
        return carry

    lax.fori_loop(0, 6, combination, 0, unroll=3)
    for copy in copies:
        copy.wait()


def beside(stored, parts, weights, slopes, potential):
    return pl.pallas_call(
        beside_kernel,
        in_specs=[ANY] * 4 + [VM] * 3,
        out_specs=[VM] * 4,
        out_shape=[
            jax.ShapeDtypeStruct((6, 8, 128, 512), bf16),
            jax.ShapeDtypeStruct((2, 4, 6, 128, 128), bf16),
            jax.ShapeDtypeStruct((2, 4, 128, 128), f32),
            jax.ShapeDtypeStruct((2, 4, 128, 128), bf16),
        ],
        scratch_shapes=[
            pltpu.VMEM((4, 6, 128, 128), bf16),
            pltpu.SemaphoreType.DMA((8,)),
        ],
        cost_estimate=pl.CostEstimate(
            flops=3000000000, bytes_accessed=12000000, transcendentals=0
        ),
        compiler_params=MIDDLE,
        name="beside",
    )(stored, *parts, weights, slopes, potential)


def backward_kernel(
    weight_ref, slope_ref, part_ref, own_ref, across_ref, within_ref, side_ref, msg_ref, self_ref,
    out_ref, near_ref, total_ref, potential_ref
):
    even = jnp.broadcast_to(side_ref[...], (24, 128)) > 0.0
    potential_ref[0] = jnp.where(even, across_ref[...], within_ref[...])
    potential_ref[1] = jnp.where(even, within_ref[...], across_ref[...])

    def scale(side, carry):
        columns = jnp.transpose(potential_ref[side])
        for x in range(4):
            for z in range(6):
                near_ref[side, x, z] = scaled(columns, x * 6 + z, slope_ref[side, x, z])
        return carry

    lax.fori_loop(0, 2, scale, 0)
    total_ref[...] = part_ref[...]

    def combination(t, carry):
        x, a = combination_of(t)
        for pair, (start, stop, first, width) in enumerate(SPANS):
            near = jnp.concatenate(
                [
                    near_ref[side, x, 2 * pair : 2 * pair + 2].reshape(256, 128)
                    for side in range(2)
                ],
                axis=0,
            )
            part = dot(weight_ref[t, start:stop].reshape(width * 128, 512), near)
            total_ref[a, first : first + width] += part.reshape(width, 128, 128)
        return carry

    lax.fori_loop(0, 6, combination, 0, unroll=3)

    def finish(a, carry):
        back = total_ref[a].reshape(512, 128).astype(bf16)
        own = own_ref[a].reshape(512, 128)
        out_ref[a] = (dot_t(back, msg_ref[...]) + dot_t(own, self_ref[...])).reshape(4, 128, 128)
        return carry

    lax.fori_loop(0, 2, finish, 0, unroll=2)


def backward(weights, slope, part, own, across, within, side, msg_weight, self_weight):
    return pl.pallas_call(
        backward_kernel,
        in_specs=[VM] * 9,
        out_specs=VM,
        out_shape=jax.ShapeDtypeStruct((2, 4, 128, 128), f32),
        scratch_shapes=[
            pltpu.VMEM((2, 4, 6, 128, 128), bf16),
            pltpu.VMEM((2, 4, 128, 128), f32),
            pltpu.VMEM((2, 24, 128), f32),
        ],
        cost_estimate=pl.CostEstimate(
            flops=4000000000, bytes_accessed=12000000, transcendentals=0
        ),
        compiler_params=SMALL,
        name="backward",
    )(weights, slope, part, own, across, within, side, msg_weight, self_weight)


def wave_tables(size_x, size_y, size_z):
    i16 = np.arange(16)
    points_x = np.array([g * 32 + a * 16 + i for a in range(2) for g in range(4) for i in i16])
    along_x = cas(np.arange(size_x), points_x, size_x)
    points_y = np.array(
        [gy * 16 + gx * 4 + gz for gx in range(4) for gy in range(16) for gz in range(4)]
    )
    into_y = cas(np.arange(size_y), points_y, size_y)
    back_x = np.array(
        [((2 * g - 1 + a) % 8) * 16 + i for g in range(4) for a in range(4) for i in i16]
    )
    back_z = np.array(
        [((4 * g - 2 + c) % 16) * 16 + k for g in range(4) for c in range(8) for k in i16]
    )
    tables = (
        cas(np.arange(size_z), np.arange(size_z), size_z),
        along_x,
        into_y,
        cas(back_x, np.arange(size_x), size_x),
        cas(np.arange(size_z), back_z, size_z),
    )
    return [jnp.asarray(np.ascontiguousarray(t), dtype=bf16) for t in tables]


def influence_of(size_x, size_y, size_z):
    device = lax.axis_index(everyone)

    def wave(index, size):
        signed = jnp.where(2 * index >= size, index - size, index)
        return signed.astype(f32) * (PC / size)

    wave_x = wave(device % size_x, size_x)
    wave_y = wave(jnp.arange(size_y, dtype=jnp.int32), size_y)[:, None]
    wave_z = wave(
        device // size_x * 128 + jnp.arange(size_z // 2, dtype=jnp.int32), size_z
    )[None, :]
    squared = wave_x * wave_x + wave_y * wave_y + wave_z * wave_z
    safe = jnp.where(squared > 0, squared, 1.0)
    return jnp.where(squared > 0, jnp.exp(-((math.pi * spread_width) ** 2) * squared) / safe, 0.0)


def swapped(value, axis):
    return lax.all_to_all(value, axis, split_axis=0, concat_axis=0, tiled=True)


def body(features, msg_weight, self_weight, charge_weight, spline_corner, spline_fraction):
    cells_x, cells_y, cells_z, slots, width = features.shape
    size_x = cells_x * PC * lax.axis_size("gx")
    size_y = cells_y * PC * lax.axis_size("gy")
    size_z = cells_z * PC * lax.axis_size("gz")
    volume = size_x // PC * (size_y // PC) * (size_z // PC)
    natoms = volume * slots
    cells = cells_x * cells_z

    features_own = features.reshape(cells, slots, width)
    own = project(
        features_own, msg_weight, spline_corner.swapaxes(2, 3), spline_fraction.swapaxes(2, 3)
    )
    own = own.reshape(cells_x, cells_z, slots + 16, width)
    sides, ends, outer, corners = early_halo(own)
    weights, part = inside_pairs(own, sides, features_own, self_weight)
    weights, part = ends_pairs(own, sides, ends, part, weights)
    influence = influence_of(size_x, size_y, size_z)
    along_z, along_x, into_y, back_x, back_z = wave_tables(size_x, size_y, size_z)

    read = charge_weight[None, :]
    weights, preact, mesh, row_place = message_layer(
        own, ends, outer, corners, part, read, weights
    )
    mesh = swapped(mesh, plane).reshape(4, 4, PC, 128)
    slope_near = late_halo(slope_of(preact, read))
    lines = swapped(forward_xz(mesh, along_z, along_x), everyone)
    lines = swapped(filter_y(lines, into_y, influence), everyone)
    field, energy = inverse_xz(lines, back_x, back_z, coupling / (2.0 * volume * natoms))
    field = swapped(field.reshape(16, 64, 128), plane)
    potential, atom_potential, own_weights, slopes = interpolate(
        field, row_place.reshape(24, 8, slots), weights, slope_near, coupling / volume
    )
    across, within = partners(potential)
    side = jnp.full((1, slots), 1 - 2 * (lax.axis_index("gy") % 2), f32)
    weights, slopes, total, cotangent = beside(
        weights, slope_near, own_weights, slopes, potential
    )
    grad = backward(
        weights, slopes, total, cotangent, across, within, side, msg_weight, self_weight
    )
    return (
        grad.reshape(features.shape),
        atom_potential.reshape(cells_x, cells_y, cells_z, slots),
        energy[0, 0],
    )


def solution(mesh):
    in_specs = (
        P("gx", "gy", "gz", None, None),
        P(),
        P(),
        P(),
        P("gx", "gy", "gz", None, None),
        P("gx", "gy", "gz", None, None),
    )
    out_specs = (P("gx", "gy", "gz", None, None), P("gx", "gy", "gz", None), P())
    return jax.shard_map(body, mesh=mesh, in_specs=in_specs, out_specs=out_specs, check_vma=False)
```
